512 devices in a mesh: group: 8 (over y, core), box: 64 (over z, x).
Axes of the slice: x: 4, y: 4, z: 16, core: 2. Of those that a mesh axis runs over, the one named last changes fastest.
Arguments:
- dipoles: float32 [3, 131072], P(None, ('group', 'box')), may hold values from -6 to 6
- perm_field: float32 [3, 131072], P(None, ('group', 'box')), may hold values from -6 to 6
- positions: float32 [3, 131072], P(None, ('group', 'box')), may hold values from -1 to 1
- polarizability: float32 [131072], P(('group', 'box')), may hold values from 0.5 to 2.5
- occupancy: int32 [1024], P(('group', 'box')), may hold values from 1 to 128
- far_boxes: int32 [1024, 189], P(('group', 'box')), may hold values from 0 to 1023, as said below
- far_class: int32 [1024, 189], P(('group', 'box')), may hold values from 0 to 7
- far_count: int32 [1024], P(('group', 'box')), may hold values from 94 to 189
- far_scale: float32 [1024, 189], P(('group', 'box')), may hold values from 0.2 to 1
- translations: float32 [8, 165, 165], replicated, may hold values from -0.0015015624 to 0.0015015624
Outputs:
- new_dipoles: float32 [3, 131072], P(None, ('group', 'box'))
- residual: float32 [3, 131072], P(None, ('group', 'box'))
The draws below stay inside these ranges and needn't reach their ends.
Inputs may be any that keep to these rules, and one draw needn't show every extreme that they name: Entry far_boxes[b, e] names a box of layer z' in group g' with |z' - z| <= 4 for box b's own layer z and group g, and |z' - z| >= 2 where g' = g; the first entry of every list is 4 layers away.
All inputs are finite; a program needn't handle non-finite values.
Results may differ from the reference program's by a relative error of at most 0.0003.
Values sent between devices are 32-bit elements; how exact they have to be, the bound alone decides.
No kernel may reach another device: no remote copies, remote signals or barrier semaphores. Data moves between devices by JAX's collectives and lax.ppermute only.
A program may use at most 64 MiB of HBM per device.

```python
import math
import jax
import jax.numpy as jnp
import numpy as np
from jax import lax

TILE = 128
ORDER = 8
NTERM = 165
FX = 2
FY = 1
BOX_DEV = 2
ILIST = 189
REACH = 4
CLASSES = 8
GROUPS = 8
OWNERS = 64
BOXES = 1024
ATOMS = 131072


def draw_far_boxes(key, part):
    numbers = jnp.arange(BOXES, dtype=jnp.int32)
    layer = numbers // BOX_DEV % OWNERS
    home_group = numbers // (BOX_DEV * OWNERS)
    key_group, key_step, key_far, key_slot = jax.random.split(key, 4)
    target_group = jax.random.randint(key_group, (BOXES, ILIST), 0, GROUPS)
    stride = jax.random.randint(key_step, (BOXES, ILIST), 0, 2 * REACH + 1) - REACH
    direction = jnp.where(stride >= 0, 1, -1)
    far_step = direction * jax.random.randint(key_far, (BOXES, ILIST), 2, REACH + 1)
    too_close = (target_group == home_group[:, None]) & (jnp.abs(stride) < 2)
    stride = jnp.where(too_close, far_step, stride)
    stride = stride.at[:, 0].set(REACH)
    landing = layer[:, None] + stride
    stride = jnp.where((landing < 0) | (landing >= OWNERS), -stride, stride)
    within = jax.random.randint(key_slot, (BOXES, ILIST), 0, BOX_DEV)
    result = (target_group * OWNERS + layer[:, None] + stride) * BOX_DEV + within
    return result.astype(jnp.int32)


def with_ends(values, key, least, top_value):
    extent = values.shape
    place = [jax.random.randint(jax.random.fold_in(key, axis), (), 0, extent[axis]) for axis in range(len(extent))]
    values = values.at[tuple(place)].set(least)
    longest = extent.index(max(extent))
    place[longest] = (place[longest] + 1) % extent[longest]
    return values.at[tuple(place)].set(top_value)


def block_scale(rng, extent, shards, low, top_value):
    def one(position, shards_of):
        heights = jax.random.uniform(jax.random.fold_in(jax.random.fold_in(rng, 6), position), (shards_of,), jnp.float32, low / len(shards), top_value / len(shards))
        return jnp.repeat(jnp.exp(heights), extent[position] // shards_of).reshape((-1,) + (1,) * (len(extent) - position - 1))

    factor_of = one(*shards[0])
    for cut in shards[1:]:
        factor_of = factor_of * one(*cut)
    return factor_of


def centred(key, shape, width, reach, pieces=(), kind=jnp.bfloat16):
    entries = width * jax.random.normal(key, shape, jnp.float32)
    if pieces:
        entries = entries * block_scale(key, shape, pieces, -0.22, 0.18)
    return jnp.clip(entries, -reach, reach).astype(kind)


def setup_inputs(seed: int = 0) -> dict:
    key_list = jax.random.split(jax.random.key(seed), 11)
    return {
        "dipoles": centred(key_list[0], (3, ATOMS), 1.0, 6.0, ((1, 512),), jnp.float32),
        "perm_field": centred(key_list[1], (3, ATOMS), 1.0, 6.0, ((1, 512),), jnp.float32),
        "positions": jnp.clip(jax.random.uniform(key_list[2], (3, ATOMS), jnp.float32, -1.0, 1.0) * block_scale(key_list[2], (3, ATOMS), ((1, 512),), -0.4, 0.0), -1.0, 1.0),
        "polarizability": jnp.clip(jnp.exp(math.log(2.5) - 1.609438 * jax.random.uniform(key_list[3], (ATOMS,), jnp.float32) ** block_scale(key_list[3], (ATOMS,), ((0, 512),), -0.2, 0.2)), 0.5, 2.5),
        "occupancy": with_ends(jax.random.randint(key_list[4], (BOXES,), 1, TILE + 1), jax.random.fold_in(key_list[4], 1), 1, TILE).astype(jnp.int32),
        "far_boxes": draw_far_boxes(jax.random.fold_in(key_list[10], 71), 0),
        "far_class": with_ends(jax.random.randint(key_list[6], (BOXES, ILIST), 0, CLASSES), jax.random.fold_in(key_list[6], 1), 0, CLASSES - 1).astype(jnp.int32),
        "far_count": with_ends(jax.random.randint(key_list[7], (BOXES,), ILIST // 2, ILIST + 1), jax.random.fold_in(key_list[7], 1), ILIST // 2, ILIST).astype(jnp.int32),
        "far_scale": jnp.clip(jnp.exp(math.log(1.0) - 1.609438 * jax.random.uniform(key_list[8], (BOXES, ILIST), jnp.float32) ** block_scale(key_list[8], (BOXES, ILIST), ((0, 512),), -0.2, 0.2)), 0.2, 1.0),
        "translations": centred(key_list[9], (CLASSES, NTERM, NTERM), (0.5 * (NTERM * ILIST * TILE) ** -0.5), 0.0015015624, (), jnp.float32),
    }


HALF = 5.4
THOLE = 0.39
SOFT = 1.0
HIGH = lax.Precision.HIGHEST

def term_table(order):
    listing = []
    for degree in range(order + 1):
        for first_idx in range(degree + 1):
            for second_idx in range(degree + 1 - first_idx):
                listing.append((first_idx, second_idx, degree - first_idx - second_idx))
    return np.array(listing, dtype=np.int32)

def chebyshev(coord, order):
    series = [jnp.ones_like(coord), coord]
    for number in range(2, order + 1):
        series.append(2.0 * coord * series[-1] - series[-2])
    return jnp.stack(series[:order + 1])

def monomials(positions):
    table = term_table(ORDER)
    cheb_x = chebyshev(positions[0], ORDER)
    cheb_y = chebyshev(positions[1], ORDER)
    cheb_z = chebyshev(positions[2], ORDER)
    return cheb_x[table[:, 0]] * cheb_y[table[:, 1]] * cheb_z[table[:, 2]]

def pair_field(target_rel, target_root, source_rel, source_root, source_dip, offset, keep_mask):
    deltas = [HALF * (target_rel[component][:, :, None] - source_rel[component][:, None, :] - 2.0 * offset[component]) for component in range(3)]
    squared = deltas[0] * deltas[0] + deltas[1] * deltas[1] + deltas[2] * deltas[2] + SOFT
    inverse = lax.rsqrt(squared)
    cube_inv = inverse * inverse * inverse
    strength = THOLE * squared * jnp.sqrt(squared) * target_root[:, :, None] * source_root[:, None, :]
    damping = jnp.exp(-strength)
    lambda_three = -jnp.expm1(-strength)
    lambda_five = lambda_three - strength * damping
    projection = deltas[0] * source_dip[0][:, None, :] + deltas[1] * source_dip[1][:, None, :] + deltas[2] * source_dip[2][:, None, :]
    radial = keep_mask * 3.0 * lambda_five * cube_inv * inverse * inverse * projection
    direct = keep_mask * lambda_three * cube_inv
    return jnp.stack([lax.optimization_barrier(jnp.sum(deltas[component] * radial - direct * source_dip[component][:, None, :], axis=2)) for component in range(3)])

def near_field(source, positions, root_pol):
    shape = (GROUPS, OWNERS, FX, FY, TILE)
    padding = ((0, 0), (1, 1), (1, 1), (1, 1), (0, 0))
    src_dip = jnp.moveaxis(jnp.pad(source.reshape((3,) + shape), ((0, 0),) + padding), 1, 0)
    src_rel = jnp.moveaxis(jnp.pad(positions.reshape((3,) + shape), ((0, 0),) + padding), 1, 0)
    src_root = jnp.pad(root_pol.reshape(shape), padding)
    tgt_rel = jnp.moveaxis(positions.reshape((3,) + shape), 1, 0)
    tgt_root = root_pol.reshape(shape)
    boxes = OWNERS * FX * FY

    def per_group(inputs):
        dip_g, rel_g, root_g, trel_g, troot_g = inputs
        target_rel = trel_g.reshape(3, boxes, TILE)
        target_root = troot_g.reshape(boxes, TILE)
        total = jnp.zeros((3, boxes, TILE), jnp.float32)
        for shift_z in (-1, 0, 1):
            for shift_x in (-1, 0, 1):
                for shift_y in (-1, 0, 1):
                    window_dip = dip_g[:, 1 + shift_z:1 + shift_z + OWNERS, 1 + shift_x:1 + shift_x + FX, 1 + shift_y:1 + shift_y + FY].reshape(3, boxes, TILE)
                    window_rel = rel_g[:, 1 + shift_z:1 + shift_z + OWNERS, 1 + shift_x:1 + shift_x + FX, 1 + shift_y:1 + shift_y + FY].reshape(3, boxes, TILE)
                    window_root = root_g[1 + shift_z:1 + shift_z + OWNERS, 1 + shift_x:1 + shift_x + FX, 1 + shift_y:1 + shift_y + FY].reshape(boxes, TILE)
                    if shift_z == 0 and shift_x == 0 and (shift_y == 0):
                        keep_mask = 1.0 - jnp.eye(TILE, dtype=jnp.float32)
                    else:
                        keep_mask = jnp.float32(1.0)
                    total = total + pair_field(target_rel, target_root, window_rel, window_root, window_dip, (float(shift_x), float(shift_y), float(shift_z)), keep_mask)
        return total
    fields = lax.map(per_group, (src_dip, src_rel, src_root, tgt_rel, tgt_root))
    return jnp.moveaxis(fields, 1, 0).reshape(3, -1)

def far_field(source, monomial, far_boxes, far_class, far_count, far_scale, translations):
    mono_b = monomial.reshape(NTERM, BOXES, TILE)
    dip_b = source.reshape(3, BOXES, TILE)
    multipole = jnp.einsum('tbs,cbs->bct', mono_b, dip_b, precision=HIGH).reshape(BOXES, 3 * NTERM)
    listing = lax.broadcasted_iota(jnp.int32, (BOXES, ILIST), 1)
    weights = far_scale * (listing < far_count[:, None]).astype(jnp.float32)
    classes = (far_class[:, :, None] == lax.broadcasted_iota(jnp.int32, (1, 1, CLASSES), 2)).astype(jnp.float32) * weights[:, :, None]
    blocks = BOXES // BOX_DEV

    def per_block(inputs):
        box_ids, class_w = inputs
        picked = multipole[box_ids.astype(jnp.int32)]
        return jnp.einsum('bjo,bjq->boq', class_w, picked, precision=HIGH)
    summed = lax.map(per_block, (far_boxes.reshape(blocks, BOX_DEV, ILIST), classes.reshape(blocks, BOX_DEV, ILIST, CLASSES)))
    summed = summed.reshape(BOXES, CLASSES, 3, NTERM)
    local = jnp.einsum('bocu,otu->bct', summed, translations, precision=HIGH)
    return jnp.einsum('tbs,bct->cbs', mono_b, local, precision=HIGH).reshape(3, ATOMS)

def reference(dipoles, perm_field, positions, polarizability, occupancy, far_boxes, far_class, far_count, far_scale, translations):
    slot = lax.broadcasted_iota(jnp.int32, (BOXES, TILE), 1)
    live_mask = (slot < occupancy[:, None]).astype(jnp.float32).reshape(-1)
    source = dipoles * live_mask
    root_pol = lax.rsqrt(polarizability)
    monomial = monomials(positions)
    far_part = far_field(source, monomial, far_boxes, far_class, far_count, far_scale, translations)
    near_zero = near_field(source, positions, root_pol)
    residual = live_mask * (perm_field + far_part + near_zero - source / polarizability)
    sweep_one = polarizability * residual
    sweep_two = live_mask * polarizability * (residual + near_field(sweep_one, positions, root_pol))
    sweep_three = live_mask * polarizability * (residual + near_field(sweep_two, positions, root_pol))
    return (source + sweep_three, residual)
```

```python
import jax
import jax.numpy as jnp
import numpy as np
from jax import lax
from jax.experimental import pallas as pl
from jax.experimental.pallas import tpu as pltpu
from jax.sharding import Mesh
from jax.sharding import PartitionSpec as P

TILE = 128
ORDER = 8
NTERM = 165
REST = NTERM - TILE
ILIST = 189
CLASSES = 8
GROUPS = 8
OWNERS = 64
NX = 4
NY = 4
PLANE = NX * NY
CHUNK = 48
F32 = jnp.float32
BF16 = jnp.bfloat16

HALF = 5.4
ROOT_THOLE = 0.39**0.5
HIGH = lax.Precision.HIGHEST
NT = (((1,), (1,)), ((), ()))
NN = (((1,), (0,)), ((), ()))


def term_table():
    listing = []
    for degree in range(ORDER + 1):
        for first in range(degree + 1):
            for second in range(degree + 1 - first):
                listing.append((first, second, degree - first - second))
    return listing


TERMS = term_table()


def dot(a, b, dims, precision=HIGH):
    return lax.dot_general(a, b, dims, precision=precision, preferred_element_type=F32)


def chebyshev(coord):
    series = [None, coord]
    doubled = 2.0 * coord
    series.append(doubled * coord - 1.0)
    for _ in range(3, ORDER + 1):
        series.append(doubled * series[-1] - series[-2])
    return series


def write_monomials(ref, px, py, pz):
    cx, cy, cz = chebyshev(px), chebyshev(py), chebyshev(pz)
    cross = {}
    for t, (i, j, k) in enumerate(TERMS):
        if (i, j) not in cross:
            if i and j:
                cross[i, j] = cx[i] * cy[j]
            else:
                cross[i, j] = cx[i] if i else cy[j]
        head = cross[i, j]
        if head is None:
            value = jnp.ones_like(px) if k == 0 else cz[k]
        else:
            value = head if k == 0 else head * cz[k]
        ref[t * 8 : t * 8 + 8, :] = value


def first_kernel(
    me_ref, occ_ref, count_ref, dip_ref, perm_ref, pos_ref, pol_ref, boxes_ref, class_ref, scale_ref, out_ref, mono, chunk
):
    chunk[...] = jnp.zeros_like(chunk)
    lane = lax.broadcasted_iota(jnp.int32, (1, TILE), 1)
    for w in range(2):
        live = (lane < occ_ref[w]).astype(F32)
        lanes = slice(w * TILE, (w + 1) * TILE)
        base = 8 + w * 8
        chunk[base : base + 3, :] = pos_ref[:, lanes]
        chunk[base + 3 : base + 4, :] = pol_ref[:, lanes]
        chunk[base + 4 : base + 7, :] = dip_ref[:, lanes] * live
        chunk[base + 7 : base + 8, :] = live
        chunk[24 + w * 3 : 27 + w * 3, :] = perm_ref[:, lanes]
    plane = lax.rem(me_ref[0], OWNERS) // NX
    box = boxes_ref[...]
    within = box & 1
    layer = (box >> 1) & (OWNERS - 1)
    group = box >> 7
    step = (layer >> 2) - plane
    stack = jnp.where(step == 0, 0, jnp.where(step < 0, 1, 2))
    place = stack * 256 + (((group & 1) * PLANE + (group >> 1) * NX + (layer & 3)) << 3) + within
    place = place.astype(F32)
    kind = class_ref[...].astype(F32)
    entry = lax.broadcasted_iota(jnp.int32, (1, ILIST), 1)
    for w in range(2):
        weight = scale_ref[w : w + 1, :] * (entry < count_ref[w]).astype(F32)
        for n, row in enumerate((place[w : w + 1, :], kind[w : w + 1, :], weight)):
            at = 32 + w * 6 + n * 2
            chunk[at : at + 1, :] = row[:, :TILE]
            chunk[at + 1 : at + 2, 0 : ILIST - TILE] = row[:, TILE:]
    def both(row):
        two = chunk[pl.ds(8 + row, 2, stride=8), :]
        return jnp.concatenate([two, two, two, two], axis=0)

    write_monomials(mono, both(0), both(1), both(2))
    for w in range(2):
        terms = mono[pl.ds(w, NTERM, stride=8), :]
        moment = dot(chunk[12 + w * 8 : 15 + w * 8, :], terms, NT)
        for c in range(3):
            chunk[c * 2 + w : c * 2 + w + 1, :] = moment[c : c + 1, :TILE]
            chunk[6 + w : 7 + w, c * REST : (c + 1) * REST] = moment[c : c + 1, TILE:]
    whole = chunk[...]
    for m in range(PLANE):
        out_ref[m, :, :] = whole


def spread(wide_ref, cols, number, fields):
    for box in range(number):
        for f in fields:
            at = box * 8 + f
            wide_ref[f, box * TILE : (box + 1) * TILE, :] = jnp.broadcast_to(cols[:, at : at + 1], (TILE, TILE))


def write_fields(rows_ref, number, px, py, pz, root, first_layer):
    box = lax.broadcasted_iota(jnp.int32, (number, TILE), 0)
    rows_ref[pl.ds(0, number, stride=8), :] = HALF * (px + 2.0 * (box & 1).astype(F32))
    rows_ref[pl.ds(1, number, stride=8), :] = HALF * py
    rows_ref[pl.ds(2, number, stride=8), :] = HALF * (pz + 2.0 * ((box >> 1) + first_layer).astype(F32))
    rows_ref[pl.ds(3, number, stride=8), :] = root


def root_of(pol):
    return jnp.where(pol > 0.0, ROOT_THOLE * lax.rsqrt(jnp.where(pol > 0.0, pol, 1.0)), 0.0)


def pair(target, source):
    dx, dy, dz = target[0] - source[0], target[1] - source[1], target[2] - source[2]
    squared = dx * dx + dy * dy + (dz * dz + 1.0)
    inverse = lax.rsqrt(squared)
    inv_two = inverse * inverse
    inv_three = inverse * inv_two
    minus = (squared * (squared * inverse)) * (target[3] * source[3])
    damping = jnp.exp(minus)
    lambda_three = 1.0 - damping
    lambda_five = lambda_three + minus * damping
    direct = lambda_three * inv_three
    radial = (3.0 * lambda_five) * (inv_three * inv_two)
    return (dx, dy, dz), radial, direct


def apply_pair(delta, radial, direct, moment, total):
    along = radial * (delta[0] * moment[0] + delta[1] * moment[1] + delta[2] * moment[2])
    return tuple(total[c] + (delta[c] * along - direct * moment[c]) for c in range(3))


def target_rows(rows_ref, box):
    rows = [jnp.broadcast_to(rows_ref[pl.ds(box * 8 + f, 1), :], (8, TILE)) for f in range(4)]
    rows[3] = -rows[3]
    return rows


def near_sum(wide_ref, targets, first_tile, tiles, keep=None, unroll=4):
    zero = tuple(jnp.zeros((8, TILE), F32) for _ in range(6))

    def body(n, total):
        total = [total[:3], total[3:]]
        for u in range(unroll):
            at = pl.ds(pl.multiple_of((first_tile + n * unroll + u) * 8, 8), 8)
            source = [wide_ref[f, at, :] for f in range(4)]
            moment = [wide_ref[f, at, :] for f in range(4, 7)]
            for w in range(2):
                delta, radial, direct = pair(targets[w], source)
                if keep is not None:
                    slot = (n * unroll + u) * 2 + w
                    keep[0, pl.ds(pl.multiple_of(slot * 8, 8), 8), :] = radial
                    keep[1, pl.ds(pl.multiple_of(slot * 8, 8), 8), :] = direct
                total[w] = apply_pair(delta, radial, direct, moment, total[w])
        return tuple(total[0]) + tuple(total[1])

    total = lax.fori_loop(0, tiles // unroll, body, zero)
    return total[:3], total[3:]


def self_term(root):
    return 1.0 - jnp.exp(-(root * root))


def row_sum(x):
    return jnp.sum(x, axis=0, keepdims=True)


def second_kernel(me_ref, block_ref, sel_ref, near_ref, rows, wide):
    mine = (me_ref[0] // (2 * OWNERS)) * NX
    near = [[block_ref[mine + x, 8 + w * 8 : 16 + w * 8, :] for w in range(2)] for x in range(NX)]
    near = jnp.concatenate([near[x][w] for x in range(NX) for w in range(2)], axis=0)
    rows[...] = jnp.zeros_like(rows)
    rows[0:64, :] = near

    def field(f):
        return rows[pl.ds(f, 8, stride=8), :]

    px, py, pz, root = field(0), field(1), field(2), root_of(field(3))
    write_fields(rows, 8, px, py, pz, root, 0)
    spread(wide, jnp.transpose(rows[...]), 8, range(7))
    for layer in range(NX):
        low, high = max(layer - 1, 0), min(layer + 1, NX - 1)
        targets = [target_rows(rows, layer * 2 + w) for w in range(2)]
        totals = near_sum(wide, targets, low * 32, (high - low + 1) * 32)
        for w in range(2):
            for c in range(3):
                near_ref[c * 8 + layer * 2 + w : c * 8 + layer * 2 + w + 1, :] = row_sum(totals[w][c])
    spot = lax.broadcasted_iota(jnp.int32, (768, TILE), 0)
    kinds = lax.broadcasted_iota(jnp.int32, (CLASSES, TILE), 0)
    for x in range(NX):
        for w in range(2):
            total = jnp.zeros((CLASSES, 768), F32)
            for half in range(2):
                at = 32 + w * 6 + half
                place = block_ref[mine + x, at : at + 1, :].astype(jnp.int32)
                kind = block_ref[mine + x, at + 2 : at + 3, :].astype(jnp.int32)
                weight = jnp.where(kinds == kind, block_ref[mine + x, at + 4 : at + 5, :], 0.0)
                chosen = jnp.where(spot == place, 1.0, 0.0).astype(BF16)
                high = weight.astype(BF16)
                left = weight - high.astype(F32)
                middle = left.astype(BF16)
                low = (left - middle.astype(F32)).astype(BF16)
                parts = jnp.concatenate([high.astype(F32), middle.astype(F32), low.astype(F32)], axis=0).astype(BF16)
                got = dot(parts, chosen, NT, None)
                total = total + (got[0:8] + got[8:16] + got[16:24])
            k = x * 2 + w
            sel_ref[k * 8 : k * 8 + 8, :] = total


def third_kernel(
    me_ref, block_ref, own_ref, low_ref, high_ref, sel_ref, near_ref, trans_ref, res_ref, send_ref,
    summed, local, mono, rows, wide, edge,
):
    mine = (me_ref[0] // (2 * OWNERS)) * NX
    x_me = lax.rem(me_ref[0], NX)
    sel = sel_ref[...]
    lhs = jnp.concatenate([sel] + [pltpu.roll(sel, 2 * n, 1) for n in range(1, 4)], axis=0)
    stacked = jnp.concatenate([own_ref[...], low_ref[0:256, :], high_ref[0:256, :]], axis=0)
    summed[...] = dot(lhs, stacked, NN)
    total = jnp.zeros((24, NTERM), F32)
    for o in range(CLASSES):
        rest = summed[pl.ds(192 + o, 8, stride=8), :]
        parts = []
        for c in range(3):
            head = summed[pl.ds(c * 64 + o, 8, stride=8), :]
            parts.append(jnp.concatenate([head, rest[:, c * REST : (c + 1) * REST]], axis=1))
        total = total + dot(jnp.concatenate(parts, axis=0), trans_ref[o], NT)
    local[0:24, :] = total[:, :TILE]
    local[24:48, 0:REST] = total[:, TILE:]
    near = jnp.concatenate([block_ref[mine + x, 8 + w * 8 : 16 + w * 8, :] for x in range(NX) for w in range(2)], axis=0)
    edge_low = low_ref[272:288, :]
    edge_high = high_ref[256:272, :]
    rows[...] = jnp.zeros_like(rows)
    rows[0:16, :] = edge_low
    rows[16:80, :] = near
    rows[80:96, :] = edge_high

    def field(f):
        return rows[pl.ds(f, 12, stride=8), :]

    px, py, pz, pol = field(0), field(1), field(2), field(3)
    live = rows[pl.ds(16 + 7, 8, stride=8), :]
    source = [rows[pl.ds(16 + 4 + c, 8, stride=8), :] for c in range(3)]
    root = root_of(pol)
    write_monomials(mono, px[2:10], py[2:10], pz[2:10])
    write_fields(rows, 12, px, py, pz, root, -1)
    cols = jnp.transpose(rows[...])
    for slot, box in enumerate((0, 1, 10, 11)):
        for f in range(7):
            at = box * 8 + f
            wide[f, slot * TILE : (slot + 1) * TILE, :] = jnp.broadcast_to(cols[:, at : at + 1], (TILE, TILE))
    edge[...] = near_ref[...]
    for side, layer in ((0, 0), (1, NX - 1)):
        targets = [target_rows(rows, 2 + layer * 2 + w) for w in range(2)]
        totals = near_sum(wide, targets, side * 32, 32)
        for w in range(2):
            for c in range(3):
                at = c * 8 + layer * 2 + w
                edge[at : at + 1, :] = edge[at : at + 1, :] + row_sum(totals[w][c])
    far = [[] for _ in range(3)]
    for k in range(8):
        mine_k = jnp.concatenate([local[pl.ds(k, 3, stride=8), :], local[pl.ds(24 + k, 3, stride=8), :][:, 0:REST]], axis=1)
        got = dot(mine_k, mono[pl.ds(k, NTERM, stride=8), :], NN)
        for c in range(3):
            far[c].append(got[c : c + 1, :])
    alone = self_term(root[2:10])
    for c in range(3):
        perm = jnp.concatenate(
            [block_ref[mine + x, 24 + w * 3 + c : 25 + w * 3 + c, :] for x in range(NX) for w in range(2)], axis=0
        )
        near_zero = edge[c * 8 : c * 8 + 8, :] + alone * source[c]
        res_ref[c * 8 : c * 8 + 8, :] = live * (
            perm + jnp.concatenate(far[c], axis=0) + near_zero - source[c] / pol[2:10]
        )
    first = jnp.where(x_me < 2, 4, 0)
    for c in range(3):
        for k in range(4):
            send_ref[c * 4 + k : c * 4 + k + 1, :] = res_ref[pl.ds(c * 8 + first + k, 1), :]


def fourth_kernel(
    me_ref, block_ref, low_ref, high_ref, res_ref, got_ref, new_ref, out_ref, every, rows, moved, wide, keep, field_two
):
    mine = (me_ref[0] // (2 * OWNERS)) * NX
    x_me = lax.rem(me_ref[0], NX)
    every[0:32, :] = low_ref[256:288, :]
    for x in range(NX):
        every[32 + x * 16 : 48 + x * 16, :] = block_ref[mine + x, 8:24, :]
    every[96:128, :] = high_ref[256:288, :]
    for c in range(3):
        got = got_ref[c * 4 : c * 4 + 4, :]
        moved[c, 0:4, :] = got
        moved[c, 4:12, :] = res_ref[c * 8 : c * 8 + 8, :]
        moved[c, 12:16, :] = got
    first = x_me * 2
    rows[...] = jnp.zeros_like(rows)
    for k in range(10):
        rows[k * 8 : k * 8 + 8, :] = every[pl.ds(pl.multiple_of((first + k) * 8, 8), 8), :]

    def field(f):
        return rows[pl.ds(f, 10, stride=8), :]

    px, py, pz, pol, live = field(0), field(1), field(2), field(3), field(7)
    source = [rows[pl.ds(32 + 4 + c, 2, stride=8), :] for c in range(3)]
    residual = [
        jnp.concatenate([moved[c, pl.ds(first + k, 1), :] for k in range(10)], axis=0) for c in range(3)
    ]
    root = root_of(pol)
    alone = self_term(root)
    write_fields(rows, 10, px, py, pz, root, -2)
    one = [pol * residual[c] for c in range(3)]
    for c in range(3):
        rows[pl.ds(4 + c, 10, stride=8), :] = one[c]
    spread(wide, jnp.transpose(rows[...]), 10, range(7))
    for layer in (1, 2, 3):
        targets = [target_rows(rows, layer * 2 + w) for w in range(2)]
        totals = near_sum(wide, targets, (layer - 1) * 32, 96, keep if layer == 2 else None)
        for w in range(2):
            for c in range(3):
                at = (layer - 1) * 2 + w
                field_two[c, at : at + 1, :] = row_sum(totals[w][c])
    two = []
    for c in range(3):
        total = field_two[c, 0:6, :] + alone[2:8] * one[c][2:8]
        two.append(live[2:8] * pol[2:8] * (residual[c][2:8] + total))
        rows[pl.ds(16 + 4 + c, 6, stride=8), :] = two[c]
    cols = jnp.transpose(rows[...])
    for box in range(2, 8):
        for f in range(4, 7):
            at = box * 8 + f
            wide[f, box * TILE : (box + 1) * TILE, :] = jnp.broadcast_to(cols[:, at : at + 1], (TILE, TILE))
    targets = [target_rows(rows, 4 + w) for w in range(2)]

    def body(n, total):
        total = [total[:3], total[3:]]
        for u in range(4):
            tile = n * 4 + u
            at = pl.ds(pl.multiple_of((32 + tile) * 8, 8), 8)
            source_at = [wide[f, at, :] for f in range(3)]
            moment = [wide[f, at, :] for f in range(4, 7)]
            for w in range(2):
                slot = pl.ds(pl.multiple_of((tile * 2 + w) * 8, 8), 8)
                delta = [targets[w][c] - source_at[c] for c in range(3)]
                total[w] = apply_pair(delta, keep[0, slot, :], keep[1, slot, :], moment, total[w])
        return tuple(total[0]) + tuple(total[1])

    final = lax.fori_loop(0, 24, body, tuple(jnp.zeros((8, TILE), F32) for _ in range(6)))
    for c in range(3):
        for w in range(2):
            box = 4 + w
            own = residual[c][box : box + 1]
            total = row_sum(final[w * 3 + c]) + alone[box : box + 1] * two[c][2 + w : 3 + w]
            three = live[box : box + 1] * pol[box : box + 1] * (own + total)
            new_ref[c : c + 1, w * TILE : (w + 1) * TILE] = source[c][w : w + 1] + three
            out_ref[c : c + 1, w * TILE : (w + 1) * TILE] = own


VMEM = pl.BlockSpec(memory_space=pltpu.VMEM)
SMEM = pl.BlockSpec(memory_space=pltpu.SMEM)


def call(body, ins, outs, scratch, cost, name):
    return pl.pallas_call(
        body,
        in_specs=ins,
        out_specs=[VMEM] * len(outs),
        out_shape=[jax.ShapeDtypeStruct(shape, F32) for shape in outs],
        scratch_shapes=[pltpu.VMEM(shape, F32) for shape in scratch],
        cost_estimate=pl.CostEstimate(flops=cost, bytes_accessed=1 << 20, transcendentals=0),
        name=name,
    )


def device(group, box):
    return group * OWNERS + box


def rounds():
    plane = [
        [device(2 * y + core, z * NX + x) for y in range(NY) for x in range(NX)]
        for core in range(2)
        for z in range(OWNERS // NX)
    ]
    chip = [[device(2 * y, b), device(2 * y + 1, b)] for y in range(NY) for b in range(OWNERS)]
    up = [(device(g, b), device(g, b + NX)) for g in range(GROUPS) for b in range(OWNERS - NX)]
    down = [(target, source) for source, target in up]
    near_side = [(s, t) for s, t in up if s % NX < 2] + [(s, t) for s, t in down if s % NX >= 2]
    return plane, chip, up, down, near_side


PLANE_SETS, CHIP_SETS, UP, DOWN, NEAR_SIDE = rounds()


def on_device(
    dipoles, perm_field, positions, polarizability, occupancy, far_boxes, far_class, far_count, far_scale, translations
):
    me = lax.axis_index("d").astype(jnp.int32)[None]
    [chunk] = call(
        first_kernel, [SMEM] * 3 + [VMEM] * 7, [(PLANE, CHUNK, TILE)], [(NTERM * 8, TILE), (CHUNK, TILE)], 1 << 20, "first"
    )(
        me, occupancy, far_count, dipoles, perm_field, positions, polarizability.reshape(1, 2 * TILE),
        far_boxes, far_class, far_scale,
    )
    block = lax.all_to_all(chunk, "d", 0, 0, axis_index_groups=PLANE_SETS, tiled=True)
    own = lax.all_gather(block[:, 0:8, :], "d", axis_index_groups=CHIP_SETS, axis=0).reshape(256, TILE)
    mine = (me[0] // (2 * OWNERS)) * NX
    near = lax.dynamic_slice(block, (mine, 8, 0), (NX, 16, TILE))
    low = lax.ppermute(jnp.concatenate([own, near[2:4].reshape(32, TILE)], axis=0), "d", UP)
    high = lax.ppermute(jnp.concatenate([own, near[0:2].reshape(32, TILE)], axis=0), "d", DOWN)
    sel, near_zero = call(
        second_kernel, [SMEM, VMEM], [(64, 768), (24, TILE)], [(TILE, TILE), (7, 8 * TILE, TILE)], 1 << 26, "second"
    )(me, block)
    residual, send = call(
        third_kernel,
        [SMEM] + [VMEM] * 7,
        [(24, TILE), (12, TILE)],
        [(256, TILE), (48, TILE), (NTERM * 8, TILE), (TILE, TILE), (7, 4 * TILE, TILE), (24, TILE)],
        1 << 26,
        "third",
    )(me, block, own, low, high, sel, near_zero, translations)
    got = lax.ppermute(send, "d", NEAR_SIDE)
    new, out = call(
        fourth_kernel,
        [SMEM] + [VMEM] * 5,
        [(3, 2 * TILE), (3, 2 * TILE)],
        [(TILE, TILE), (TILE, TILE), (3, 16, TILE), (7, 10 * TILE, TILE), (2, 192 * 8, TILE), (3, 8, TILE)],
        1 << 26,
        "fourth",
    )(me, block, low, high, residual, got)
    return new, out


def solution(mesh):
    flat = Mesh(mesh.devices.reshape(-1), ("d",))
    return jax.shard_map(
        on_device,
        mesh=flat,
        in_specs=(
            P(None, "d"), P(None, "d"), P(None, "d"), P("d"), P("d"), P("d", None), P("d", None), P("d"), P("d", None), P(),
        ),
        out_specs=(P(None, "d"), P(None, "d")),
        check_vma=False,
    )
```

```python
import jax
import jax.numpy as jnp
from jax import lax
from jax.experimental import pallas as pl
from jax.experimental.pallas import tpu as pltpu
from jax.sharding import Mesh
from jax.sharding import PartitionSpec as P

TILE = 128
ORDER = 8
NTERM = 165
REST = NTERM - TILE
ILIST = 189
CLASSES = 8
GROUPS = 8
OWNERS = 64
NX = 4
NY = 4
PLANE = NX * NY
CHUNK = 48
F32 = jnp.float32
BF16 = jnp.bfloat16

HALF = 5.4
ROOT_THOLE = 0.39**0.5
NT = (((1,), (1,)), ((), ()))
NN = (((1,), (0,)), ((), ()))


def term_table():
    listing = []
    for degree in range(ORDER + 1):
        for first in range(degree + 1):
            for second in range(degree + 1 - first):
                listing.append((first, second, degree - first - second))
    return listing


TERMS = term_table()


def dot(a, b, dims):
    return lax.dot_general(a, b, dims, preferred_element_type=F32)


def halves(x):
    high = x.astype(BF16)
    return high, (x - high.astype(F32)).astype(BF16)


def dot_three(a, b, dims):
    a_high, a_low = halves(a)
    b_high, b_low = halves(b)
    return dot(a_high, b_high, dims) + (dot(a_high, b_low, dims) + dot(a_low, b_high, dims))


def chebyshev(coord):
    series = [None, coord]
    doubled = 2.0 * coord
    series.append(doubled * coord - 1.0)
    for _ in range(3, ORDER + 1):
        series.append(doubled * series[-1] - series[-2])
    return series


def write_monomials(ref, px, py, pz):
    cx, cy, cz = chebyshev(px), chebyshev(py), chebyshev(pz)
    cross = {}
    for t, (i, j, k) in enumerate(TERMS):
        if (i, j) not in cross:
            if i and j:
                cross[i, j] = cx[i] * cy[j]
            else:
                cross[i, j] = cx[i] if i else cy[j]
        head = cross[i, j]
        if head is None:
            value = jnp.ones_like(px) if k == 0 else cz[k]
        else:
            value = head if k == 0 else head * cz[k]
        ref[t * 8 : t * 8 + 8, :] = value


def first_kernel(
    me_ref, occ_ref, count_ref, dip_ref, perm_ref, pos_ref, pol_ref, boxes_ref, class_ref, scale_ref, out_ref, mono, chunk
):
    chunk[...] = jnp.zeros_like(chunk)
    lane = lax.broadcasted_iota(jnp.int32, (1, TILE), 1)
    for w in range(2):
        live = (lane < occ_ref[w]).astype(F32)
        lanes = slice(w * TILE, (w + 1) * TILE)
        base = 8 + w * 8
        chunk[base : base + 3, :] = pos_ref[:, lanes]
        chunk[base + 3 : base + 4, :] = pol_ref[:, lanes]
        chunk[base + 4 : base + 7, :] = dip_ref[:, lanes] * live
        chunk[base + 7 : base + 8, :] = live
        chunk[24 + w * 3 : 27 + w * 3, :] = perm_ref[:, lanes]
    plane = lax.rem(me_ref[0], OWNERS) // NX
    box = boxes_ref[...]
    within = box & 1
    layer = (box >> 1) & (OWNERS - 1)
    group = box >> 7
    step = (layer >> 2) - plane
    stack = jnp.where(step == 0, 0, jnp.where(step < 0, 1, 2))
    place = within * 96 + stack * 32 + (group & 1) * PLANE + (group >> 1) * NX + (layer & 3)
    place = place.astype(F32)
    kind = class_ref[...].astype(F32)
    entry = lax.broadcasted_iota(jnp.int32, (1, ILIST), 1)
    for w in range(2):
        weight = scale_ref[w : w + 1, :] * (entry < count_ref[w]).astype(F32)
        for n, row in enumerate((place[w : w + 1, :], kind[w : w + 1, :], weight)):
            at = 32 + w * 6 + n * 2
            chunk[at : at + 1, :] = row[:, :TILE]
            chunk[at + 1 : at + 2, 0 : ILIST - TILE] = row[:, TILE:]
    def both(row):
        two = chunk[pl.ds(8 + row, 2, stride=8), :]
        return jnp.concatenate([two, two, two, two], axis=0)

    write_monomials(mono, both(0), both(1), both(2))
    for w in range(2):
        terms = mono[pl.ds(w, NTERM, stride=8), :]
        moment = dot_three(chunk[12 + w * 8 : 15 + w * 8, :], terms, NT)
        for c in range(3):
            chunk[c * 2 + w : c * 2 + w + 1, :] = moment[c : c + 1, :TILE]
            chunk[6 + w : 7 + w, c * REST : (c + 1) * REST] = moment[c : c + 1, TILE:]
    whole = chunk[...]
    for m in range(PLANE):
        out_ref[m, :, :] = whole


def spread(wide_ref, cols, boxes, fields):
    for slot, box in enumerate(boxes):
        for f in fields:
            at = box * 8 + f
            wide_ref[f, slot * TILE : (slot + 1) * TILE, :] = jnp.broadcast_to(cols[:, at : at + 1], (TILE, TILE))


def write_fields(rows_ref, number, px, py, pz, root, first_layer):
    box = lax.broadcasted_iota(jnp.int32, (number, TILE), 0)
    rows_ref[pl.ds(0, number, stride=8), :] = HALF * (px + 2.0 * (box & 1).astype(F32))
    rows_ref[pl.ds(1, number, stride=8), :] = HALF * py
    rows_ref[pl.ds(2, number, stride=8), :] = HALF * (pz + 2.0 * ((box >> 1) + first_layer).astype(F32))
    rows_ref[pl.ds(3, number, stride=8), :] = root


def root_of(pol):
    return jnp.where(pol > 0.0, ROOT_THOLE * lax.rsqrt(jnp.where(pol > 0.0, pol, 1.0)), 0.0)


def scalars(delta, roots):
    dx, dy, dz = delta
    squared = dx * dx + dy * dy + (dz * dz + 1.0)
    inverse = lax.rsqrt(squared)
    inv_two = inverse * inverse
    inv_three = inverse * inv_two
    minus = -((squared * (squared * inverse)) * roots)
    damping = jnp.exp(minus)
    lambda_three = 1.0 - damping
    lambda_five = lambda_three + minus * damping
    return (3.0 * lambda_five) * (inv_three * inv_two), lambda_three * inv_three


def field_of(delta, radial, direct, moment):
    along = radial * (delta[0] * moment[0] + delta[1] * moment[1] + delta[2] * moment[2])
    return [delta[c] * along - direct * moment[c] for c in range(3)]


def added(parts):
    while len(parts) > 1:
        parts = [parts[i] + parts[i + 1] if i + 1 < len(parts) else parts[i] for i in range(0, len(parts), 2)]
    return parts[0]


def row(ref, at):
    return ref[pl.ds(at, 8, stride=0), :]


def tile_at(n, base=0):
    return pl.ds(pl.multiple_of(base + n * 8, 8), 8)


def trips_of(live):
    count = jnp.sum(live, axis=1, keepdims=True)
    return ((count + 7.0) * 0.125).astype(jnp.int32)


def near_box(total_ref, slot, wide_ref, target, trips, rows_ref, sources):
    def body(n, carry):
        at = tile_at(n, target * TILE)
        mine = [wide_ref[f, at, :] for f in range(4)]
        parts = []
        for box in sources:
            delta = [mine[c] - row(rows_ref, box * 8 + c) for c in range(3)]
            radial, direct = scalars(delta, mine[3] * row(rows_ref, box * 8 + 3))
            parts.append(field_of(delta, radial, direct, [row(rows_ref, box * 8 + 4 + c) for c in range(3)]))
        for c in range(3):
            total_ref[c, tile_at(n, slot * TILE), :] = added([part[c] for part in parts])
        return carry

    lax.fori_loop(0, trips, body, 0)


def lane_sums(total_ref, c, slot):
    return jnp.sum(jnp.transpose(total_ref[c, slot * TILE : (slot + 1) * TILE, :]), axis=0, keepdims=True)


def self_term(root):
    return 1.0 - jnp.exp(-(root * root))


def prepare_kernel(trans_ref, high_ref, low_ref):
    high_ref[...] = jnp.zeros_like(high_ref)
    low_ref[...] = jnp.zeros_like(low_ref)
    for o in range(CLASSES):
        high, low = halves(jnp.transpose(trans_ref[:, o, :]))
        high_ref[o * 256 : o * 256 + NTERM, :] = high
        low_ref[o * 256 : o * 256 + NTERM, :] = low


def second_kernel(me_ref, block_ref, sel_ref, near_ref, wide, rows, total):
    mine = (me_ref[0] // (2 * OWNERS)) * NX
    rows[...] = jnp.zeros_like(rows)
    for x in range(NX):
        rows[x * 16 : x * 16 + 16, :] = block_ref[mine + x, 8:24, :]

    def field(f):
        return rows[pl.ds(f, 8, stride=8), :]

    px, py, pz, root = field(0), field(1), field(2), root_of(field(3))
    trips = trips_of(field(7))
    write_fields(rows, 8, px, py, pz, root, 0)
    spread(wide, jnp.transpose(rows[...]), range(8), range(4))
    for box in range(8):
        low, high = max(box // 2 - 1, 0), min(box // 2 + 1, NX - 1)
        near_box(total, box, wide, box, trips[box, 0], rows, range(low * 2, high * 2 + 2))
    spot = lax.broadcasted_iota(jnp.int32, (192, TILE), 0)
    kinds = lax.broadcasted_iota(jnp.int32, (CLASSES, TILE), 0)
    for k in range(8):
        got = jnp.zeros((16, 192), F32)
        for half in range(2):
            at = 32 + (k % 2) * 6 + half
            place = block_ref[mine + k // 2, at : at + 1, :].astype(jnp.int32)
            kind = block_ref[mine + k // 2, at + 2 : at + 3, :].astype(jnp.int32)
            weight = jnp.where(kinds == kind, block_ref[mine + k // 2, at + 4 : at + 5, :], 0.0)
            chosen = jnp.where(spot == place, 1.0, 0.0).astype(BF16)
            high = weight.astype(BF16).astype(F32)
            parts = jnp.concatenate([high, weight - high], axis=0).astype(BF16)
            got = got + dot(parts, chosen, NT)
        sel_ref[k * 8 : k * 8 + 8, :] = got[0:8] + got[8:16]
    for c in range(3):
        for box in range(8):
            near_ref[c * 8 + box : c * 8 + box + 1, :] = lane_sums(total, c, box)


def third_kernel(
    me_ref, block_ref, own_ref, low_ref, high_ref, sel_ref, near_ref, wide_ref, t_high_ref, t_low_ref, res_ref, send_ref,
    summed, local, mono, rows, total,
):
    mine = (me_ref[0] // (2 * OWNERS)) * NX
    x_me = lax.rem(me_ref[0], NX)
    sel_high, sel_low = halves(sel_ref[...])
    both = jnp.concatenate([sel_high, sel_low], axis=0)
    for kind in range(4):
        flat = jnp.concatenate(
            [ref[pl.ds(kind * 2 + w, 32, stride=8), :] for w in range(2) for ref in (own_ref, low_ref, high_ref)], axis=0
        )
        high, low = halves(flat)
        got = dot(both, high, NN)
        summed[kind * 64 : kind * 64 + 64, :] = got[0:64] + (got[64:128] + dot(sel_high, low, NN))
    parts = []
    for c in range(3):
        pieces = []
        for o in range(CLASSES):
            pieces.append(summed[pl.ds(c * 64 + o, 8, stride=8), :])
            rest = summed[pl.ds(192 + o, 8, stride=8), :][:, c * REST : (c + 1) * REST]
            pieces.append(jnp.concatenate([rest, jnp.zeros((8, TILE - REST), F32)], axis=1))
        parts.append(jnp.concatenate(pieces, axis=1))
    high, low = halves(jnp.concatenate(parts, axis=0))
    t_high, t_low = t_high_ref[...], t_low_ref[...]
    moved = dot(high, t_high, NN) + (dot(low, t_high, NN) + dot(high, t_low, NN))
    local[:, 0:NTERM] = moved
    rows[...] = jnp.zeros_like(rows)
    rows[0:16, :] = low_ref[272:288, :]
    for x in range(NX):
        rows[16 + x * 16 : 32 + x * 16, :] = block_ref[mine + x, 8:24, :]
    rows[80:96, :] = high_ref[256:272, :]

    def field(f):
        return rows[pl.ds(f, 12, stride=8), :]

    px, py, pz, pol = field(0), field(1), field(2), field(3)
    live = rows[pl.ds(16 + 7, 8, stride=8), :]
    source = [rows[pl.ds(16 + 4 + c, 8, stride=8), :] for c in range(3)]
    root = root_of(pol)
    trips = trips_of(live)
    write_monomials(mono, px[2:10], py[2:10], pz[2:10])
    write_fields(rows, 12, px, py, pz, root, -1)
    for slot, box, sources in ((0, 0, (0, 1)), (1, 1, (0, 1)), (2, 6, (10, 11)), (3, 7, (10, 11))):
        near_box(total, slot, wide_ref, box, trips[box, 0], rows, sources)
    far = [jnp.zeros((8, TILE), F32) for _ in range(3)]
    for t in range(NTERM):
        term = mono[t * 8 : t * 8 + 8, :]
        for c in range(3):
            far[c] = far[c] + jnp.broadcast_to(local[c * 8 : c * 8 + 8, t : t + 1], (8, TILE)) * term
    alone = self_term(root[2:10])
    nothing = jnp.zeros((4, TILE), F32)
    for c in range(3):
        perm = jnp.concatenate(
            [block_ref[mine + x, 24 + w * 3 + c : 25 + w * 3 + c, :] for x in range(NX) for w in range(2)], axis=0
        )
        ends = [lane_sums(total, c, slot) for slot in range(4)]
        edge = jnp.concatenate(ends[0:2] + [nothing] + ends[2:4], axis=0)
        near_zero = near_ref[c * 8 : c * 8 + 8, :] + edge + alone * source[c]
        res_ref[c * 8 : c * 8 + 8, :] = jnp.where(
            live > 0.0, perm + far[c] + near_zero - source[c] / pol[2:10], 0.0
        )
    first = jnp.where(x_me < 2, 4, 0)
    for c in range(3):
        for k in range(4):
            send_ref[c * 4 + k : c * 4 + k + 1, :] = res_ref[pl.ds(c * 8 + first + k, 1), :]


def window_kernel(me_ref, block_ref, low_ref, high_ref, rows, keep, wide, every):
    mine = (me_ref[0] // (2 * OWNERS)) * NX
    first = lax.rem(me_ref[0], NX) * 2
    every[0:32, :] = low_ref[256:288, :]
    for x in range(NX):
        every[32 + x * 16 : 48 + x * 16, :] = block_ref[mine + x, 8:24, :]
    every[96:128, :] = high_ref[256:288, :]
    rows[...] = jnp.zeros_like(rows)
    for k in range(10):
        rows[k * 8 : k * 8 + 8, :] = every[pl.ds(pl.multiple_of((first + k) * 8, 8), 8), :]

    def field(f):
        return rows[pl.ds(f, 10, stride=8), :]

    px, py, pz, pol, live = field(0), field(1), field(2), field(3), field(7)
    root = root_of(pol)
    rows[80:90, :] = pol
    rows[96:106, :] = self_term(root)
    trips = trips_of(live)
    write_fields(rows, 10, px, py, pz, root, -2)
    spread(wide, jnp.transpose(rows[...]), range(2, 8), range(4))
    for box in range(2, 8):

        def body(n, carry):
            at = tile_at(n, (box - 2) * TILE)
            spot = [wide[f, at, :] for f in range(4)]
            for k in range(6):
                source = (box // 2 - 1) * 2 + k
                delta = [spot[c] - row(rows, source * 8 + c) for c in range(3)]
                radial, direct = scalars(delta, spot[3] * row(rows, source * 8 + 3))
                keep[k, at, :] = radial
                keep[6 + k, at, :] = direct
            return carry

        lax.fori_loop(0, trips[box, 0], body, 0)


def fourth_kernel(me_ref, rows_ref, keep_ref, wide_ref, res_ref, got_ref, new_ref, out_ref, moved, rows, total):
    first = lax.rem(me_ref[0], NX) * 2
    for c in range(3):
        got = got_ref[c * 4 : c * 4 + 4, :]
        moved[c, 0:4, :] = got
        moved[c, 4:12, :] = res_ref[c * 8 : c * 8 + 8, :]
        moved[c, 12:16, :] = got
    rows[...] = rows_ref[...]
    pol, alone = rows[80:90, :], rows[96:106, :]
    live = rows[pl.ds(7, 10, stride=8), :]
    trips = trips_of(live)
    source = [rows[pl.ds(32 + 4 + c, 2, stride=8), :] for c in range(3)]
    residual = [jnp.concatenate([moved[c, pl.ds(first + k, 1), :] for k in range(10)], axis=0) for c in range(3)]

    def sweep(boxes, moments):
        for c in range(3):
            rows[pl.ds(4 + c, 10, stride=8), :] = moments[c]
        for box in boxes:

            def body(n, carry):
                at = tile_at(n, (box - 2) * TILE)
                spot = [wide_ref[c, at, :] for c in range(3)]
                parts = []
                for k in range(6):
                    near = (box // 2 - 1) * 2 + k
                    delta = [spot[c] - row(rows, near * 8 + c) for c in range(3)]
                    moment = [row(rows, near * 8 + 4 + c) for c in range(3)]
                    parts.append(field_of(delta, keep_ref[k, at, :], keep_ref[6 + k, at, :], moment))
                for c in range(3):
                    total[c, at, :] = added([part[c] for part in parts])
                return carry

            lax.fori_loop(0, trips[box, 0], body, 0)
        return [jnp.concatenate([lane_sums(total, c, box - 2) for box in boxes], axis=0) for c in range(3)]

    one = [pol * residual[c] for c in range(3)]
    fields = sweep(range(2, 8), one)
    two = []
    edge = jnp.zeros((2, TILE), F32)
    for c in range(3):
        value = pol[2:8] * (residual[c][2:8] + fields[c] + alone[2:8] * one[c][2:8])
        two.append(jnp.concatenate([edge, jnp.where(live[2:8] > 0.0, value, 0.0), edge], axis=0))
    fields = sweep(range(4, 6), two)
    for c in range(3):
        value = pol[4:6] * (residual[c][4:6] + fields[c] + alone[4:6] * two[c][4:6])
        three = source[c] + jnp.where(live[4:6] > 0.0, value, 0.0)
        for w in range(2):
            new_ref[c : c + 1, w * TILE : (w + 1) * TILE] = three[w : w + 1]
            out_ref[c : c + 1, w * TILE : (w + 1) * TILE] = residual[c][4 + w : 5 + w]


VMEM = pl.BlockSpec(memory_space=pltpu.VMEM)
SMEM = pl.BlockSpec(memory_space=pltpu.SMEM)


def shape_of(shape):
    return shape if isinstance(shape, jax.ShapeDtypeStruct) else jax.ShapeDtypeStruct(shape, F32)


def call(body, ins, outs, scratch, cost, limit, name):
    return pl.pallas_call(
        body,
        in_specs=ins,
        out_specs=[VMEM] * len(outs),
        out_shape=[shape_of(shape) for shape in outs],
        scratch_shapes=[pltpu.VMEM(shape, F32) for shape in scratch],
        cost_estimate=pl.CostEstimate(flops=cost, bytes_accessed=1 << 20, transcendentals=0),
        compiler_params=pltpu.CompilerParams(vmem_limit_bytes=limit << 20),
        name=name,
    )


def device(group, box):
    return group * OWNERS + box


def rounds():
    plane = [
        [device(2 * y + core, z * NX + x) for y in range(NY) for x in range(NX)]
        for core in range(2)
        for z in range(OWNERS // NX)
    ]
    chip = [[device(2 * y, b), device(2 * y + 1, b)] for y in range(NY) for b in range(OWNERS)]
    up = [(device(g, b), device(g, b + NX)) for g in range(GROUPS) for b in range(OWNERS - NX)]
    down = [(target, source) for source, target in up]
    near_side = [(s, t) for s, t in up if s % NX < 2] + [(s, t) for s, t in down if s % NX >= 2]
    return plane, chip, up, down, near_side


PLANE_SETS, CHIP_SETS, UP, DOWN, NEAR_SIDE = rounds()


def on_device(
    dipoles, perm_field, positions, polarizability, occupancy, far_boxes, far_class, far_count, far_scale, translations
):
    me = lax.axis_index("d").astype(jnp.int32)[None]
    [chunk] = call(
        first_kernel, [SMEM] * 3 + [VMEM] * 7, [(PLANE, CHUNK, TILE)], [(NTERM * 8, TILE), (CHUNK, TILE)], 1 << 20, 8, "first"
    )(
        me, occupancy, far_count, dipoles, perm_field, positions, polarizability.reshape(1, 2 * TILE),
        far_boxes, far_class, far_scale,
    )
    block = lax.all_to_all(chunk, "d", 0, 0, axis_index_groups=PLANE_SETS, tiled=True)
    half = jax.ShapeDtypeStruct((CLASSES * 256, NTERM), BF16)
    t_high, t_low = call(prepare_kernel, [VMEM], [half, half], [], 1 << 28, 12, "prepare")(
        jnp.transpose(translations, (1, 0, 2))
    )
    own = lax.all_gather(block[:, 0:8, :], "d", axis_index_groups=CHIP_SETS, axis=0).reshape(256, TILE)
    mine = (me[0] // (2 * OWNERS)) * NX
    near = lax.dynamic_slice(block, (mine, 8, 0), (NX, 16, TILE))
    low = lax.ppermute(jnp.concatenate([own, near[2:4].reshape(32, TILE)], axis=0), "d", UP)
    high = lax.ppermute(jnp.concatenate([own, near[0:2].reshape(32, TILE)], axis=0), "d", DOWN)
    sel, near_zero, wide = call(
        second_kernel,
        [SMEM, VMEM],
        [(64, 192), (24, TILE), (4, 8 * TILE, TILE)],
        [(TILE, TILE), (3, 8 * TILE, TILE)],
        1 << 28,
        12,
        "second",
    )(me, block)
    residual, send = call(
        third_kernel,
        [SMEM] + [VMEM] * 9,
        [(24, TILE), (12, TILE)],
        [(256, TILE), (24, 256), (NTERM * 8, TILE), (TILE, TILE), (3, 4 * TILE, TILE)],
        1 << 28,
        16,
        "third",
    )(me, block, own, low, high, sel, near_zero, wide, t_high, t_low)
    got = lax.ppermute(send, "d", NEAR_SIDE)
    rows, keep, spread_out = call(
        window_kernel,
        [SMEM] + [VMEM] * 3,
        [(TILE, TILE), (12, 6 * TILE, TILE), (4, 6 * TILE, TILE)],
        [(TILE, TILE)],
        1 << 28,
        16,
        "window",
    )(me, block, low, high)
    new, out = call(
        fourth_kernel,
        [SMEM] + [VMEM] * 5,
        [(3, 2 * TILE), (3, 2 * TILE)],
        [(3, 16, TILE), (TILE, TILE), (3, 6 * TILE, TILE)],
        1 << 28,
        16,
        "fourth",
    )(me, rows, keep, spread_out, residual, got)
    return new, out


def solution(mesh):
    flat = Mesh(mesh.devices.reshape(-1), ("d",))
    return jax.shard_map(
        on_device,
        mesh=flat,
        in_specs=(
            P(None, "d"), P(None, "d"), P(None, "d"), P("d"), P("d"), P("d", None), P("d", None), P("d"), P("d", None), P(),
        ),
        out_specs=(P(None, "d"), P(None, "d")),
        check_vma=False,
    )
```

```python
import jax
import jax.numpy as jnp
from jax import lax
from jax.experimental import pallas as pl
from jax.experimental.pallas import tpu as pltpu
from jax.sharding import Mesh
from jax.sharding import PartitionSpec as P

TILE = 128
ORDER = 8
NTERM = 165
REST = NTERM - TILE
ILIST = 189
CLASSES = 8
GROUPS = 8
OWNERS = 64
NX = 4
NY = 4
PLANE = NX * NY
CHUNK = 40
F32 = jnp.float32
BF16 = jnp.bfloat16

HALF = 5.4
ROOT_THOLE = 0.39**0.5
NT = (((1,), (1,)), ((), ()))
NN = (((1,), (0,)), ((), ()))


def term_table():
    listing = []
    for degree in range(ORDER + 1):
        for first in range(degree + 1):
            for second in range(degree + 1 - first):
                listing.append((first, second, degree - first - second))
    return listing


TERMS = term_table()


def dot(a, b, dims):
    return lax.dot_general(a, b, dims, preferred_element_type=F32)


def halves(x):
    high = x.astype(BF16)
    return high, (x - high.astype(F32)).astype(BF16)


def dot_three(a, b, dims):
    a_high, a_low = halves(a)
    b_high, b_low = halves(b)
    return dot(a_high, b_high, dims) + (dot(a_high, b_low, dims) + dot(a_low, b_high, dims))


def chebyshev(coord):
    series = [None, coord]
    doubled = 2.0 * coord
    series.append(doubled * coord - 1.0)
    for _ in range(3, ORDER + 1):
        series.append(doubled * series[-1] - series[-2])
    return series


def write_monomials(ref, px, py, pz):
    cx, cy, cz = chebyshev(px), chebyshev(py), chebyshev(pz)
    cross = {}
    for t, (i, j, k) in enumerate(TERMS):
        if (i, j) not in cross:
            if i and j:
                cross[i, j] = cx[i] * cy[j]
            else:
                cross[i, j] = cx[i] if i else cy[j]
        head = cross[i, j]
        if head is None:
            value = jnp.ones_like(px) if k == 0 else cz[k]
        else:
            value = head if k == 0 else head * cz[k]
        ref[t * 8 : t * 8 + 8, :] = value


def first_kernel(
    me_ref, occ_ref, count_ref, dip_hbm, perm_hbm, pos_hbm, pol_hbm, boxes_hbm, class_hbm, scale_hbm, out_ref,
    mono, chunk, dip_ref, perm_ref, pos_ref, pol_ref, scale_ref, boxes_ref, class_ref, sems,
):
    pairs = (
        (pos_hbm, pos_ref), (dip_hbm, dip_ref), (pol_hbm, pol_ref), (perm_hbm, perm_ref),
        (boxes_hbm, boxes_ref), (class_hbm, class_ref), (scale_hbm, scale_ref),
    )
    copies = [pltpu.make_async_copy(source, target, sems.at[n]) for n, (source, target) in enumerate(pairs)]
    for copy in copies:
        copy.start()
    chunk[...] = jnp.zeros_like(chunk)
    lane = lax.broadcasted_iota(jnp.int32, (1, TILE), 1)
    for copy in copies:
        copy.wait()
    for w in range(2):
        live = (lane < occ_ref[w]).astype(F32)
        lanes = slice(w * TILE, (w + 1) * TILE)
        base = 8 + w * 8
        chunk[base : base + 3, :] = pos_ref[:, lanes]
        chunk[base + 3 : base + 4, :] = pol_ref[:, lanes]
        chunk[base + 4 : base + 7, :] = dip_ref[:, lanes] * live
        chunk[base + 7 : base + 8, :] = live
        chunk[24 + w * 3 : 27 + w * 3, :] = perm_ref[:, lanes]
    plane = lax.rem(me_ref[0], OWNERS) // NX
    box = boxes_ref[...]
    within = box & 1
    layer = (box >> 1) & (OWNERS - 1)
    group = box >> 7
    step = (layer >> 2) - plane
    stack = jnp.where(step == 0, 0, jnp.where(step < 0, 1, 2))
    place = within * 96 + stack * 32 + (group & 1) * PLANE + (group >> 1) * NX + (layer & 3)
    place = place.astype(F32)
    kind = class_ref[...].astype(F32)
    entry = lax.broadcasted_iota(jnp.int32, (1, ILIST), 1)
    for w in range(2):
        weight = scale_ref[w : w + 1, :] * (entry < count_ref[w]).astype(F32)
        for n, row in enumerate((place[w : w + 1, :], kind[w : w + 1, :], weight)):
            chunk[30 + w * 3 + n : 31 + w * 3 + n, :] = row[:, :TILE]
            chunk[36 + n : 37 + n, w * 64 : w * 64 + ILIST - TILE] = row[:, TILE:]
    def both(row):
        two = chunk[pl.ds(8 + row, 2, stride=8), :]
        return jnp.concatenate([two, two, two, two], axis=0)

    write_monomials(mono, both(0), both(1), both(2))
    for w in range(2):
        terms = mono[pl.ds(w, NTERM, stride=8), :]
        moment = dot_three(chunk[12 + w * 8 : 15 + w * 8, :], terms, NT)
        for c in range(3):
            chunk[c * 2 + w : c * 2 + w + 1, :] = moment[c : c + 1, :TILE]
            chunk[6 + w : 7 + w, c * REST : (c + 1) * REST] = moment[c : c + 1, TILE:]
    whole = chunk[...]
    for m in range(PLANE):
        out_ref[m, :, :] = whole


def write_fields(rows_ref, number, px, py, pz, root, first_layer):
    box = lax.broadcasted_iota(jnp.int32, (number, TILE), 0)
    rows_ref[pl.ds(0, number, stride=8), :] = HALF * (px + 2.0 * (box & 1).astype(F32))
    rows_ref[pl.ds(1, number, stride=8), :] = HALF * py
    rows_ref[pl.ds(2, number, stride=8), :] = HALF * (pz + 2.0 * ((box >> 1) + first_layer).astype(F32))
    rows_ref[pl.ds(3, number, stride=8), :] = root


def root_of(pol):
    return jnp.where(pol > 0.0, ROOT_THOLE * lax.rsqrt(jnp.where(pol > 0.0, pol, 1.0)), 0.0)


def scalars(delta, roots):
    dx, dy, dz = delta
    squared = dx * dx + dy * dy + (dz * dz + 1.0)
    inverse = lax.rsqrt(squared)
    inv_two = inverse * inverse
    inv_three = inverse * inv_two
    minus = -((squared * (squared * inverse)) * roots)
    damping = jnp.exp(minus)
    lambda_three = 1.0 - damping
    lambda_five = lambda_three + minus * damping
    return (3.0 * lambda_five) * (inv_three * inv_two), lambda_three * inv_three


def field_of(delta, radial, direct, moment):
    along = radial * (delta[0] * moment[0] + delta[1] * moment[1] + delta[2] * moment[2])
    return [delta[c] * along - direct * moment[c] for c in range(3)]


def added(parts):
    while len(parts) > 1:
        parts = [parts[i] + parts[i + 1] if i + 1 < len(parts) else parts[i] for i in range(0, len(parts), 2)]
    return parts[0]


def row(ref, at):
    return ref[pl.ds(at, 8, stride=0), :]


def tile_at(n, base=0):
    return pl.ds(pl.multiple_of(base + n * 8, 8), 8)


def trips_of(live):
    count = jnp.sum(live, axis=1, keepdims=True)
    return ((count + 7.0) * 0.125).astype(jnp.int32)


def spread(cols_ref, n, columns):
    tile = cols_ref[tile_at(n), :]
    return [jnp.broadcast_to(tile[:, at : at + 1], (8, TILE)) for at in columns]


def drain(sums_ref, n, lanes, totals):
    lane = lax.broadcasted_iota(jnp.int32, (8, TILE), 1)
    value = sums_ref[tile_at(n), :]
    for at, total in zip(lanes, totals):
        value = jnp.where(lane == at, jnp.sum(total, axis=1, keepdims=True), value)
    sums_ref[tile_at(n), :] = value


def tile_loop(trips, cols_ref, columns, sums_ref, lanes, work):
    width = len(columns)

    def body(n, carry):
        spot, before = list(carry[:width]), list(carry[width:])
        following = spread(cols_ref, n + 1, columns)
        totals = work(n, spot)
        drain(sums_ref, n, lanes, before)
        return tuple(following) + tuple(totals)

    start = tuple(spread(cols_ref, 0, columns)) + tuple(jnp.zeros((8, TILE), F32) for _ in lanes)
    end = lax.fori_loop(0, trips, body, start)
    drain(sums_ref, trips, lanes, list(end[width:]))


def sums_of(sums_ref):
    return jnp.transpose(sums_ref[8 : 8 + TILE, :])


def near_boxes(targets, trips, cols_ref, column_of, rows_ref, sources, sums_ref, slots):
    columns = [column_of(box) * 8 + f for box in targets for f in range(4)]
    lanes = [c * 8 + slot for slot in slots for c in range(3)]

    def work(n, spot):
        parts = [[] for _ in targets]
        for box in sources:
            where = [row(rows_ref, box * 8 + f) for f in range(7)]
            for i in range(len(targets)):
                mine = spot[i * 4 : i * 4 + 4]
                delta = [mine[c] - where[c] for c in range(3)]
                radial, direct = scalars(delta, mine[3] * where[3])
                parts[i].append(field_of(delta, radial, direct, where[4:7]))
        return [added([part[c] for part in parts[i]]) for i in range(len(targets)) for c in range(3)]

    tile_loop(trips, cols_ref, columns, sums_ref, lanes, work)


def self_term(root):
    return 1.0 - jnp.exp(-(root * root))


def prepare_kernel(trans_ref, high_ref, low_ref):
    high_ref[...] = jnp.zeros_like(high_ref)
    low_ref[...] = jnp.zeros_like(low_ref)
    for o in range(CLASSES):
        high, low = halves(jnp.transpose(trans_ref[:, o, :]))
        high_ref[o * 256 : o * 256 + NTERM, :] = high
        low_ref[o * 256 : o * 256 + NTERM, :] = low


def second_kernel(me_ref, block_ref, sel_ref, near_ref, rows, cols, sums):
    mine = (me_ref[0] // (2 * OWNERS)) * NX
    rows[...] = jnp.zeros_like(rows)
    for x in range(NX):
        rows[x * 16 : x * 16 + 16, :] = block_ref[mine + x, 8:24, :]

    def field(f):
        return rows[pl.ds(f, 8, stride=8), :]

    px, py, pz, root = field(0), field(1), field(2), root_of(field(3))
    trips = trips_of(field(7))
    write_fields(rows, 8, px, py, pz, root, 0)
    cols[0:TILE, :] = jnp.transpose(rows[...])
    for box in range(8):
        low, high = max(box // 2 - 1, 0), min(box // 2 + 1, NX - 1)
        near_boxes([box], trips[box, 0], cols, lambda k: k, rows, range(low * 2, high * 2 + 2), sums, [box])
    spot = lax.broadcasted_iota(jnp.int32, (192, TILE), 0)
    kinds = lax.broadcasted_iota(jnp.int32, (CLASSES, TILE), 0)
    side = lax.broadcasted_iota(jnp.int32, (CLASSES, TILE), 1) >> 6
    for x in range(NX):
        got = jnp.zeros((32, 192), F32)
        first, second = [], []
        for w in range(2):
            at = 30 + w * 3
            place = block_ref[mine + x, at : at + 1, :].astype(jnp.int32)
            kind = block_ref[mine + x, at + 1 : at + 2, :].astype(jnp.int32)
            weight = jnp.where(kinds == kind, block_ref[mine + x, at + 2 : at + 3, :], 0.0)
            chosen = jnp.where(spot == place, 1.0, 0.0).astype(BF16)
            high = weight.astype(BF16).astype(F32)
            first.append(dot(jnp.concatenate([high, weight - high], axis=0).astype(BF16), chosen, NT))
        place = block_ref[mine + x, 36:37, :].astype(jnp.int32)
        kind = block_ref[mine + x, 37:38, :].astype(jnp.int32)
        weight = jnp.where(kinds == kind, block_ref[mine + x, 38:39, :], 0.0)
        high = weight.astype(BF16).astype(F32)
        low = weight - high
        both = [jnp.where(side == w, part, 0.0) for w in range(2) for part in (high, low)]
        chosen = jnp.where(spot == place, 1.0, 0.0).astype(BF16)
        second = dot(jnp.concatenate(both, axis=0).astype(BF16), chosen, NT)
        for w in range(2):
            k = x * 2 + w
            tail = second[w * 16 : w * 16 + 16]
            sel_ref[k * 8 : k * 8 + 8, :] = (first[w][0:8] + tail[0:8]) + (first[w][8:16] + tail[8:16])
    near_ref[...] = sums_of(sums)[0:24]


def third_kernel(
    me_ref, block_ref, own_ref, low_ref, high_ref, sel_ref, near_ref, t_high_ref, t_low_ref, res_ref, send_ref,
    summed, local, mono, rows, cols, sums,
):
    mine = (me_ref[0] // (2 * OWNERS)) * NX
    x_me = lax.rem(me_ref[0], NX)
    sel_high, sel_low = halves(sel_ref[...])
    both = jnp.concatenate([sel_high, sel_low], axis=0)
    for kind in range(4):
        flat = jnp.concatenate(
            [ref[pl.ds(kind * 2 + w, 32, stride=8), :] for w in range(2) for ref in (own_ref, low_ref, high_ref)], axis=0
        )
        high, low = halves(flat)
        got = dot(both, high, NN)
        summed[kind * 64 : kind * 64 + 64, :] = got[0:64] + (got[64:128] + dot(sel_high, low, NN))
    parts = []
    for c in range(3):
        pieces = []
        for o in range(CLASSES):
            pieces.append(summed[pl.ds(c * 64 + o, 8, stride=8), :])
            rest = summed[pl.ds(192 + o, 8, stride=8), :][:, c * REST : (c + 1) * REST]
            pieces.append(jnp.concatenate([rest, jnp.zeros((8, TILE - REST), F32)], axis=1))
        parts.append(jnp.concatenate(pieces, axis=1))
    parts.append(jnp.zeros((8, CLASSES * 256), F32))
    high, low = halves(jnp.concatenate(parts, axis=0))
    got = dot(jnp.concatenate([high, low], axis=0), t_high_ref[...], NN)
    moved = got[0:24] + (got[32:56] + dot(high, t_low_ref[...], NN)[0:24])
    local[:, 0:TILE] = moved[:, 0:TILE]
    local[:, TILE : TILE + REST] = moved[:, TILE:]
    rows[...] = jnp.zeros_like(rows)
    rows[0:16, :] = low_ref[272:288, :]
    for x in range(NX):
        rows[16 + x * 16 : 32 + x * 16, :] = block_ref[mine + x, 8:24, :]
    rows[80:96, :] = high_ref[256:272, :]

    def field(f):
        return rows[pl.ds(f, 12, stride=8), :]

    px, py, pz, pol = field(0), field(1), field(2), field(3)
    live = rows[pl.ds(16 + 7, 8, stride=8), :]
    source = [rows[pl.ds(16 + 4 + c, 8, stride=8), :] for c in range(3)]
    root = root_of(pol)
    trips = trips_of(live)
    write_monomials(mono, px[2:10], py[2:10], pz[2:10])
    write_fields(rows, 12, px, py, pz, root, -1)
    cols[0:TILE, :] = jnp.transpose(rows[...])
    sums[...] = jnp.zeros_like(sums)
    for boxes, sources in (((0, 1), (0, 1)), ((6, 7), (10, 11))):
        most = jnp.maximum(trips[boxes[0], 0], trips[boxes[1], 0])
        near_boxes(boxes, most, cols, lambda k: k + 2, rows, sources, sums, boxes)

    def evaluate(n, far):
        far = list(far)
        shift = n * 11
        for c in range(3):
            wide = pltpu.roll(local[c * 8 : c * 8 + 8, :], (256 - shift) & 255, 1)[:, 0:TILE]
            for u in range(11):
                term = mono[pl.ds(pl.multiple_of((shift + u) * 8, 8), 8), :]
                far[c] = far[c] + jnp.broadcast_to(wide[:, u : u + 1], (8, TILE)) * term
        return tuple(far)

    far = lax.fori_loop(0, 15, evaluate, tuple(jnp.zeros((8, TILE), F32) for _ in range(3)))
    alone = self_term(root[2:10])
    edge = sums_of(sums)
    for c in range(3):
        perm = jnp.concatenate(
            [block_ref[mine + x, 24 + w * 3 + c : 25 + w * 3 + c, :] for x in range(NX) for w in range(2)], axis=0
        )
        near_zero = near_ref[c * 8 : c * 8 + 8, :] + edge[c * 8 : c * 8 + 8, :] + alone * source[c]
        res_ref[c * 8 : c * 8 + 8, :] = jnp.where(
            live > 0.0, perm + far[c] + near_zero - source[c] / pol[2:10], 0.0
        )
    first = jnp.where(x_me < 2, 4, 0)
    for c in range(3):
        for k in range(4):
            send_ref[c * 4 + k : c * 4 + k + 1, :] = res_ref[pl.ds(c * 8 + first + k, 1), :]


def window_kernel(me_ref, block_ref, low_ref, high_ref, rows, keep, cols, every):
    mine = (me_ref[0] // (2 * OWNERS)) * NX
    first = lax.rem(me_ref[0], NX) * 2
    every[0:32, :] = low_ref[256:288, :]
    for x in range(NX):
        every[32 + x * 16 : 48 + x * 16, :] = block_ref[mine + x, 8:24, :]
    every[96:128, :] = high_ref[256:288, :]
    rows[...] = jnp.zeros_like(rows)
    for k in range(10):
        rows[k * 8 : k * 8 + 8, :] = every[pl.ds(pl.multiple_of((first + k) * 8, 8), 8), :]

    def field(f):
        return rows[pl.ds(f, 10, stride=8), :]

    px, py, pz, pol, live = field(0), field(1), field(2), field(3), field(7)
    root = root_of(pol)
    rows[80:90, :] = pol
    rows[96:106, :] = self_term(root)
    trips = trips_of(live)
    write_fields(rows, 10, px, py, pz, root, -2)
    cols[0:TILE, :] = jnp.transpose(rows[...])
    cols[TILE : TILE + 8, :] = jnp.zeros((8, TILE), F32)
    for box in range(2, 8):
        columns = [box * 8 + f for f in range(4)]

        def body(n, spot):
            following = spread(cols, n + 1, columns)
            at = tile_at(n, (box - 2) * TILE)
            for k in range(6):
                source = (box // 2 - 1) * 2 + k
                delta = [spot[c] - row(rows, source * 8 + c) for c in range(3)]
                radial, direct = scalars(delta, spot[3] * row(rows, source * 8 + 3))
                keep[k, at, :] = radial
                keep[6 + k, at, :] = direct
            return tuple(following)

        lax.fori_loop(0, trips[box, 0], body, tuple(spread(cols, 0, columns)))


def fourth_kernel(me_ref, rows_ref, keep_ref, cols_ref, res_ref, got_ref, new_ref, out_ref, moved, rows, sums):
    first = lax.rem(me_ref[0], NX) * 2
    for c in range(3):
        got = got_ref[c * 4 : c * 4 + 4, :]
        moved[c, 0:4, :] = got
        moved[c, 4:12, :] = res_ref[c * 8 : c * 8 + 8, :]
        moved[c, 12:16, :] = got
    rows[...] = rows_ref[...]
    pol, alone = rows[80:90, :], rows[96:106, :]
    live = rows[pl.ds(7, 10, stride=8), :]
    trips = trips_of(live)
    source = [rows[pl.ds(32 + 4 + c, 2, stride=8), :] for c in range(3)]
    residual = [jnp.concatenate([moved[c, pl.ds(first + k, 1), :] for k in range(10)], axis=0) for c in range(3)]

    def sweep(boxes, moments):
        for c in range(3):
            rows[pl.ds(4 + c, 10, stride=8), :] = moments[c]
        for box in boxes:

            def work(n, spot):
                at = tile_at(n, (box - 2) * TILE)
                parts = []
                for k in range(6):
                    near = (box // 2 - 1) * 2 + k
                    delta = [spot[c] - row(rows, near * 8 + c) for c in range(3)]
                    moment = [row(rows, near * 8 + 4 + c) for c in range(3)]
                    parts.append(field_of(delta, keep_ref[k, at, :], keep_ref[6 + k, at, :], moment))
                return [added([part[c] for part in parts]) for c in range(3)]

            columns = [box * 8 + c for c in range(3)]
            tile_loop(trips[box, 0], cols_ref, columns, sums, [c * 8 + box for c in range(3)], work)
        return sums_of(sums)

    one = [pol * residual[c] for c in range(3)]
    fields = sweep(range(2, 8), one)
    two = []
    edge = jnp.zeros((2, TILE), F32)
    for c in range(3):
        value = pol[2:8] * (residual[c][2:8] + fields[c * 8 + 2 : c * 8 + 8] + alone[2:8] * one[c][2:8])
        two.append(jnp.concatenate([edge, jnp.where(live[2:8] > 0.0, value, 0.0), edge], axis=0))
    fields = sweep(range(4, 6), two)
    for c in range(3):
        value = pol[4:6] * (residual[c][4:6] + fields[c * 8 + 4 : c * 8 + 6] + alone[4:6] * two[c][4:6])
        three = source[c] + jnp.where(live[4:6] > 0.0, value, 0.0)
        for w in range(2):
            new_ref[c : c + 1, w * TILE : (w + 1) * TILE] = three[w : w + 1]
            out_ref[c : c + 1, w * TILE : (w + 1) * TILE] = residual[c][4 + w : 5 + w]


VMEM = pl.BlockSpec(memory_space=pltpu.VMEM)
SMEM = pl.BlockSpec(memory_space=pltpu.SMEM)
HBM = pl.BlockSpec(memory_space=pltpu.HBM)


def shape_of(shape):
    return shape if isinstance(shape, jax.ShapeDtypeStruct) else jax.ShapeDtypeStruct(shape, F32)


def call(body, ins, outs, scratch, cost, limit, name):
    return pl.pallas_call(
        body,
        in_specs=ins,
        out_specs=[VMEM] * len(outs),
        out_shape=[shape_of(shape) for shape in outs],
        scratch_shapes=[pltpu.VMEM(shape, F32) if isinstance(shape, tuple) else shape for shape in scratch],
        cost_estimate=pl.CostEstimate(flops=cost, bytes_accessed=1 << 20, transcendentals=0),
        compiler_params=pltpu.CompilerParams(vmem_limit_bytes=limit << 20),
        name=name,
    )


def device(group, box):
    return group * OWNERS + box


def rounds():
    plane = [
        [device(2 * y + core, z * NX + x) for y in range(NY) for x in range(NX)]
        for core in range(2)
        for z in range(OWNERS // NX)
    ]
    chip = [[device(2 * y, b), device(2 * y + 1, b)] for y in range(NY) for b in range(OWNERS)]
    up = [(device(g, b), device(g, b + NX)) for g in range(GROUPS) for b in range(OWNERS - NX)]
    down = [(target, source) for source, target in up]
    near_side = [(s, t) for s, t in up if s % NX < 2] + [(s, t) for s, t in down if s % NX >= 2]
    return plane, chip, up, down, near_side


PLANE_SETS, CHIP_SETS, UP, DOWN, NEAR_SIDE = rounds()


def on_device(
    dipoles, perm_field, positions, polarizability, occupancy, far_boxes, far_class, far_count, far_scale, translations
):
    me = lax.axis_index("d").astype(jnp.int32)[None]
    lists = pltpu.VMEM((2, ILIST), jnp.int32)
    [chunk] = call(
        first_kernel,
        [SMEM] * 3 + [HBM] * 7,
        [(PLANE, CHUNK, TILE)],
        [(NTERM * 8, TILE), (CHUNK, TILE)]
        + [(3, 2 * TILE)] * 3
        + [(1, 2 * TILE), (2, ILIST), lists, lists, pltpu.SemaphoreType.DMA((7,))],
        1 << 20,
        8,
        "first",
    )(
        me, occupancy, far_count, dipoles, perm_field, positions, polarizability.reshape(1, 2 * TILE),
        far_boxes, far_class, far_scale,
    )
    block = lax.all_to_all(chunk, "d", 0, 0, axis_index_groups=PLANE_SETS, tiled=True)
    half = jax.ShapeDtypeStruct((CLASSES * 256, NTERM), BF16)
    t_high, t_low = call(prepare_kernel, [VMEM], [half, half], [], 1 << 28, 12, "prepare")(
        jnp.transpose(translations, (1, 0, 2))
    )
    part, t_high, t_low = lax.optimization_barrier((block[:, 0:8, :], t_high, t_low))
    own = lax.all_gather(part, "d", axis_index_groups=CHIP_SETS, axis=0).reshape(256, TILE)
    mine = (me[0] // (2 * OWNERS)) * NX
    near = lax.dynamic_slice(block, (mine, 8, 0), (NX, 16, TILE))
    low = lax.ppermute(jnp.concatenate([own, near[2:4].reshape(32, TILE)], axis=0), "d", UP)
    high = lax.ppermute(jnp.concatenate([own, near[0:2].reshape(32, TILE)], axis=0), "d", DOWN)
    columns = (TILE + 8, TILE)
    sel, near_zero = call(
        second_kernel,
        [SMEM, VMEM],
        [(64, 192), (24, TILE)],
        [(TILE, TILE), columns, columns],
        1 << 28,
        12,
        "second",
    )(me, block)
    residual, send = call(
        third_kernel,
        [SMEM] + [VMEM] * 8,
        [(24, TILE), (12, TILE)],
        [(256, TILE), (24, 256), (NTERM * 8, TILE), (TILE, TILE), columns, columns],
        1 << 28,
        16,
        "third",
    )(me, block, own, low, high, sel, near_zero, t_high, t_low)
    got = lax.ppermute(send, "d", NEAR_SIDE)
    rows, keep, cols = call(
        window_kernel,
        [SMEM] + [VMEM] * 3,
        [(TILE, TILE), (12, 6 * TILE, TILE), columns],
        [(TILE, TILE)],
        1 << 28,
        16,
        "window",
    )(me, block, low, high)
    new, out = call(
        fourth_kernel,
        [SMEM] + [VMEM] * 5,
        [(3, 2 * TILE), (3, 2 * TILE)],
        [(3, 16, TILE), (TILE, TILE), columns],
        1 << 28,
        16,
        "fourth",
    )(me, rows, keep, cols, residual, got)
    return new, out


def solution(mesh):
    flat = Mesh(mesh.devices.reshape(-1), ("d",))
    return jax.shard_map(
        on_device,
        mesh=flat,
        in_specs=(
            P(None, "d"), P(None, "d"), P(None, "d"), P("d"), P("d"), P("d", None), P("d", None), P("d"), P("d", None), P(),
        ),
        out_specs=(P(None, "d"), P(None, "d")),
        check_vma=False,
    )
```

```python
import jax
import jax.numpy as jnp
from jax import lax
from jax.experimental import pallas as pl
from jax.experimental.pallas import tpu as pltpu
from jax.sharding import Mesh
from jax.sharding import PartitionSpec as P

TILE = 128
ORDER = 8
NTERM = 165
REST = NTERM - TILE
ILIST = 189
CLASSES = 8
GROUPS = 8
OWNERS = 64
NX = 4
NY = 4
PLANE = NX * NY
CHUNK = 40
F32 = jnp.float32
BF16 = jnp.bfloat16

HALF = 5.4
ROOT_THOLE = 0.39**0.5
NT = (((1,), (1,)), ((), ()))
NN = (((1,), (0,)), ((), ()))


def term_table():
    listing = []
    for degree in range(ORDER + 1):
        for first in range(degree + 1):
            for second in range(degree + 1 - first):
                listing.append((first, second, degree - first - second))
    return listing


TERMS = term_table()


def dot(a, b, dims):
    return lax.dot_general(a, b, dims, preferred_element_type=F32)


def halves(x):
    high = x.astype(BF16)
    return high, (x - high.astype(F32)).astype(BF16)


def dot_three(a, b, dims):
    a_high, a_low = halves(a)
    b_high, b_low = halves(b)
    return dot(a_high, b_high, dims) + (dot(a_high, b_low, dims) + dot(a_low, b_high, dims))


def chebyshev(coord):
    series = [None, coord]
    doubled = 2.0 * coord
    series.append(doubled * coord - 1.0)
    for _ in range(3, ORDER + 1):
        series.append(doubled * series[-1] - series[-2])
    return series


def write_monomials(ref, px, py, pz):
    cx, cy, cz = chebyshev(px), chebyshev(py), chebyshev(pz)
    cross = {}
    for t, (i, j, k) in enumerate(TERMS):
        if (i, j) not in cross:
            if i and j:
                cross[i, j] = cx[i] * cy[j]
            else:
                cross[i, j] = cx[i] if i else cy[j]
        head = cross[i, j]
        if head is None:
            value = jnp.ones_like(px) if k == 0 else cz[k]
        else:
            value = head if k == 0 else head * cz[k]
        ref[t * 8 : t * 8 + 8, :] = value


def first_kernel(
    me_ref, occ_ref, count_ref, dip_hbm, perm_hbm, pos_hbm, pol_hbm, boxes_hbm, class_hbm, scale_hbm, out_ref,
    mono, chunk, dip_ref, perm_ref, pos_ref, pol_ref, scale_ref, boxes_ref, class_ref, sems,
):
    pairs = (
        (pos_hbm, pos_ref), (dip_hbm, dip_ref), (pol_hbm, pol_ref), (perm_hbm, perm_ref),
        (boxes_hbm, boxes_ref), (class_hbm, class_ref), (scale_hbm, scale_ref),
    )
    copies = [pltpu.make_async_copy(source, target, sems.at[n]) for n, (source, target) in enumerate(pairs)]
    for copy in copies:
        copy.start()
    chunk[...] = jnp.zeros_like(chunk)
    lane = lax.broadcasted_iota(jnp.int32, (1, TILE), 1)
    for copy in copies:
        copy.wait()
    for w in range(2):
        live = (lane < occ_ref[w]).astype(F32)
        lanes = slice(w * TILE, (w + 1) * TILE)
        base = 8 + w * 8
        chunk[base : base + 3, :] = pos_ref[:, lanes]
        chunk[base + 3 : base + 4, :] = pol_ref[:, lanes]
        chunk[base + 4 : base + 7, :] = dip_ref[:, lanes] * live
        chunk[base + 7 : base + 8, :] = live
        chunk[24 + w * 3 : 27 + w * 3, :] = perm_ref[:, lanes]
    plane = lax.rem(me_ref[0], OWNERS) // NX
    box = boxes_ref[...]
    within = box & 1
    layer = (box >> 1) & (OWNERS - 1)
    group = box >> 7
    step = (layer >> 2) - plane
    stack = jnp.where(step == 0, 0, jnp.where(step < 0, 1, 2))
    place = within * 96 + stack * 32 + (group & 1) * PLANE + (group >> 1) * NX + (layer & 3)
    place = place.astype(F32)
    kind = class_ref[...].astype(F32)
    entry = lax.broadcasted_iota(jnp.int32, (1, ILIST), 1)
    for w in range(2):
        weight = scale_ref[w : w + 1, :] * (entry < count_ref[w]).astype(F32)
        for n, row in enumerate((place[w : w + 1, :], kind[w : w + 1, :], weight)):
            chunk[30 + w * 3 + n : 31 + w * 3 + n, :] = row[:, :TILE]
            chunk[36 + n : 37 + n, w * 64 : w * 64 + ILIST - TILE] = row[:, TILE:]
    def both(row):
        two = chunk[pl.ds(8 + row, 2, stride=8), :]
        return jnp.concatenate([two, two, two, two], axis=0)

    write_monomials(mono, both(0), both(1), both(2))
    for w in range(2):
        terms = mono[pl.ds(w, NTERM, stride=8), :]
        moment = dot_three(chunk[12 + w * 8 : 15 + w * 8, :], terms, NT)
        for c in range(3):
            chunk[c * 2 + w : c * 2 + w + 1, :] = moment[c : c + 1, :TILE]
            chunk[6 + w : 7 + w, c * REST : (c + 1) * REST] = moment[c : c + 1, TILE:]
    whole = chunk[...]
    for m in range(PLANE):
        out_ref[m, :, :] = whole


def write_fields(rows_ref, number, px, py, pz, root, first_layer):
    box = lax.broadcasted_iota(jnp.int32, (number, TILE), 0)
    rows_ref[pl.ds(0, number, stride=8), :] = HALF * (px + 2.0 * (box & 1).astype(F32))
    rows_ref[pl.ds(1, number, stride=8), :] = HALF * py
    rows_ref[pl.ds(2, number, stride=8), :] = HALF * (pz + 2.0 * ((box >> 1) + first_layer).astype(F32))
    rows_ref[pl.ds(3, number, stride=8), :] = root


def root_of(pol):
    return jnp.where(pol > 0.0, ROOT_THOLE * lax.rsqrt(jnp.where(pol > 0.0, pol, 1.0)), 0.0)


def scalars(delta, roots):
    dx, dy, dz = delta
    squared = dx * dx + dy * dy + (dz * dz + 1.0)
    inverse = lax.rsqrt(squared)
    inv_two = inverse * inverse
    inv_three = inverse * inv_two
    minus = (squared * (squared * inverse)) * roots
    damping = jnp.exp(minus)
    lambda_three = 1.0 - damping
    lambda_five = lambda_three + minus * damping
    return (3.0 * lambda_five) * (inv_three * inv_two), lambda_three * inv_three


def field_of(delta, radial, direct, moment):
    along = radial * (delta[0] * moment[0] + delta[1] * moment[1] + delta[2] * moment[2])
    return [delta[c] * along - direct * moment[c] for c in range(3)]


def added(parts):
    while len(parts) > 1:
        parts = [parts[i] + parts[i + 1] if i + 1 < len(parts) else parts[i] for i in range(0, len(parts), 2)]
    return parts[0]


def row(ref, at):
    return ref[pl.ds(at, 8, stride=0), :]


def tile_at(n, base=0):
    return pl.ds(pl.multiple_of(base + n * 8, 8), 8)


def trips_of(live):
    count = jnp.sum(live, axis=1, keepdims=True)
    return ((count + 7.0) * 0.125).astype(jnp.int32)


def spread(wide_ref, cols, boxes, fields):
    for slot, box in enumerate(boxes):
        for f in fields:
            at = box * 8 + f
            value = jnp.broadcast_to(cols[:, at : at + 1], (TILE, TILE))
            wide_ref[f, slot * TILE : (slot + 1) * TILE, :] = -value if f == 3 else value


def near_boxes(total_ref, slots, wide_ref, targets, trips, rows_ref, sources):
    def body(n, carry):
        mine = [[wide_ref[f, tile_at(n, target * TILE), :] for f in range(4)] for target in targets]
        parts = [[] for _ in targets]
        for box in sources:
            where = [row(rows_ref, box * 8 + f) for f in range(7)]
            for i, spot in enumerate(mine):
                delta = [spot[c] - where[c] for c in range(3)]
                radial, direct = scalars(delta, spot[3] * where[3])
                parts[i].append(field_of(delta, radial, direct, where[4:7]))
        for i, slot in enumerate(slots):
            for c in range(3):
                total_ref[c, tile_at(n, slot * TILE), :] = added([part[c] for part in parts[i]])
        return carry

    lax.fori_loop(0, trips, body, 0)


def lane_sums(total_ref, c, slot):
    return jnp.sum(jnp.transpose(total_ref[c, slot * TILE : (slot + 1) * TILE, :]), axis=0, keepdims=True)


def self_term(root):
    return 1.0 - jnp.exp(-(root * root))


def prepare_kernel(trans_ref, high_ref, low_ref):
    high_ref[...] = jnp.zeros_like(high_ref)
    low_ref[...] = jnp.zeros_like(low_ref)
    for o in range(CLASSES):
        high, low = halves(jnp.transpose(trans_ref[:, o, :]))
        high_ref[o * 256 : o * 256 + NTERM, :] = high
        low_ref[o * 256 : o * 256 + NTERM, :] = low


def second_kernel(me_ref, block_ref, sel_ref, near_ref, wide, m_high_ref, m_low_ref, rows, total, mono):
    mine = (me_ref[0] // (2 * OWNERS)) * NX
    rows[...] = jnp.zeros_like(rows)
    for x in range(NX):
        rows[x * 16 : x * 16 + 16, :] = block_ref[mine + x, 8:24, :]

    def field(f):
        return rows[pl.ds(f, 8, stride=8), :]

    px, py, pz, root = field(0), field(1), field(2), root_of(field(3))
    trips = trips_of(field(7))
    write_monomials(mono, px, py, pz)
    write_fields(rows, 8, px, py, pz, root, 0)
    spread(wide, jnp.transpose(rows[...]), range(8), range(4))
    for k in range(8):
        high, low = halves(mono[pl.ds(k, NTERM, stride=8), :])
        m_high_ref[k * 176 : k * 176 + NTERM, :] = high
        m_low_ref[k * 176 : k * 176 + NTERM, :] = low
    for box in range(8):
        low, high = max(box // 2 - 1, 0), min(box // 2 + 1, NX - 1)
        near_boxes(total, [box], wide, [box], trips[box, 0], rows, range(low * 2, high * 2 + 2))
    spot = lax.broadcasted_iota(jnp.int32, (192, TILE), 0)
    kinds = lax.broadcasted_iota(jnp.int32, (CLASSES, TILE), 0)
    side = lax.broadcasted_iota(jnp.int32, (CLASSES, TILE), 1) >> 6
    for x in range(NX):
        got = jnp.zeros((32, 192), F32)
        first, second = [], []
        for w in range(2):
            at = 30 + w * 3
            place = block_ref[mine + x, at : at + 1, :].astype(jnp.int32)
            kind = block_ref[mine + x, at + 1 : at + 2, :].astype(jnp.int32)
            weight = jnp.where(kinds == kind, block_ref[mine + x, at + 2 : at + 3, :], 0.0)
            chosen = jnp.where(spot == place, 1.0, 0.0).astype(BF16)
            high = weight.astype(BF16).astype(F32)
            first.append(dot(jnp.concatenate([high, weight - high], axis=0).astype(BF16), chosen, NT))
        place = block_ref[mine + x, 36:37, :].astype(jnp.int32)
        kind = block_ref[mine + x, 37:38, :].astype(jnp.int32)
        weight = jnp.where(kinds == kind, block_ref[mine + x, 38:39, :], 0.0)
        high = weight.astype(BF16).astype(F32)
        low = weight - high
        both = [jnp.where(side == w, part, 0.0) for w in range(2) for part in (high, low)]
        chosen = jnp.where(spot == place, 1.0, 0.0).astype(BF16)
        second = dot(jnp.concatenate(both, axis=0).astype(BF16), chosen, NT)
        for w in range(2):
            k = x * 2 + w
            tail = second[w * 16 : w * 16 + 16]
            sel_ref[k * 8 : k * 8 + 8, :] = (first[w][0:8] + tail[0:8]) + (first[w][8:16] + tail[8:16])
    for c in range(3):
        for box in range(8):
            near_ref[c * 8 + box : c * 8 + box + 1, :] = lane_sums(total, c, box)


def third_kernel(
    me_ref, block_ref, own_ref, sides_ref, sel_ref, near_ref, wide_ref, m_high_ref, m_low_ref, t_high_ref, t_low_ref,
    res_ref, send_ref, summed, head, rest, far, rows, total,
):
    mine = (me_ref[0] // (2 * OWNERS)) * NX
    core = lax.rem(me_ref[0] // OWNERS, 2)
    x_me = lax.rem(me_ref[0], NX)
    sel_high, sel_low = halves(sel_ref[...])
    both = jnp.concatenate([sel_high, sel_low], axis=0)
    for kind in range(4):
        pieces = []
        for w in range(2):
            pieces += [own_ref[pl.ds(at + kind * 2 + w, 16, stride=8), :] for at in (0, OWN_ROWS)]
            pieces += [sides_ref[pl.ds(at + kind * 2 + w, 32, stride=8), :] for at in (0, SIDE_ROWS)]
        high, low = halves(jnp.concatenate(pieces, axis=0))
        got = dot(both, high, NN)
        summed[kind * 64 : kind * 64 + 64, :] = got[0:64] + (got[64:128] + dot(sel_high, low, NN))
    parts = []
    for c in range(3):
        pieces = []
        for o in range(CLASSES):
            pieces.append(summed[pl.ds(c * 64 + o, 8, stride=8), :])
            tail = summed[pl.ds(192 + o, 8, stride=8), :][:, c * REST : (c + 1) * REST]
            pieces.append(jnp.concatenate([tail, jnp.zeros((8, TILE - REST), F32)], axis=1))
        parts.append(jnp.concatenate(pieces, axis=1))
    parts.append(jnp.zeros((8, CLASSES * 256), F32))
    high, low = halves(jnp.concatenate(parts, axis=0))
    got = dot(jnp.concatenate([high, low], axis=0), t_high_ref[...], NN)
    moved = got[0:24] + (got[32:56] + dot(high, t_low_ref[...], NN)[0:24])
    moved_high = moved.astype(BF16).astype(F32)
    for n, part in enumerate((moved_high, moved - moved_high)):
        head[n * 24 : n * 24 + 24, :] = part[:, 0:TILE]
        rest[n * 24 : n * 24 + 24, 0:REST] = part[:, TILE:]
    rows[...] = jnp.zeros_like(rows)
    rows[0:16, :] = sides_ref[pl.ds(pl.multiple_of(272 + 32 * core, 8), 16), :]
    for x in range(NX):
        rows[16 + x * 16 : 32 + x * 16, :] = block_ref[mine + x, 8:24, :]
    rows[80:96, :] = sides_ref[pl.ds(pl.multiple_of(SIDE_ROWS + 256 + 32 * core, 8), 16), :]

    def field(f):
        return rows[pl.ds(f, 12, stride=8), :]

    px, py, pz, pol = field(0), field(1), field(2), field(3)
    live = rows[pl.ds(16 + 7, 8, stride=8), :]
    source = [rows[pl.ds(16 + 4 + c, 8, stride=8), :] for c in range(3)]
    root = root_of(pol)
    trips = trips_of(live)
    write_fields(rows, 12, px, py, pz, root, -1)
    for slots, boxes, sources in (((0, 1), (0, 1), (0, 1)), ((2, 3), (6, 7), (10, 11))):
        most = jnp.maximum(trips[boxes[0], 0], trips[boxes[1], 0])
        near_boxes(total, slots, wide_ref, boxes, most, rows, sources)
    for k in range(8):
        left = jnp.concatenate([head[pl.ds(k, 6, stride=8), :], rest[pl.ds(k, 6, stride=8), :][:, 0:REST]], axis=1)
        left = left.astype(BF16)
        with_high = dot(left, m_high_ref[k * 176 : k * 176 + NTERM, :], NN)
        with_low = dot(left, m_low_ref[k * 176 : k * 176 + NTERM, :], NN)
        value = with_high[0:3] + (with_high[3:6] + with_low[0:3])
        for c in range(3):
            far[c * 8 + k : c * 8 + k + 1, :] = value[c : c + 1]
    alone = self_term(root[2:10])
    nothing = jnp.zeros((4, TILE), F32)
    for c in range(3):
        perm = jnp.concatenate(
            [block_ref[mine + x, 24 + w * 3 + c : 25 + w * 3 + c, :] for x in range(NX) for w in range(2)], axis=0
        )
        ends = [lane_sums(total, c, slot) for slot in range(4)]
        edge = jnp.concatenate(ends[0:2] + [nothing] + ends[2:4], axis=0)
        near_zero = near_ref[c * 8 : c * 8 + 8, :] + edge + alone * source[c]
        res_ref[c * 8 : c * 8 + 8, :] = jnp.where(
            live > 0.0, perm + far[c * 8 : c * 8 + 8, :] + near_zero - source[c] / pol[2:10], 0.0
        )
    first = jnp.where(x_me < 2, 4, 0)
    for c in range(3):
        for k in range(4):
            send_ref[c * 4 + k : c * 4 + k + 1, :] = res_ref[pl.ds(c * 8 + first + k, 1), :]


def window_kernel(me_ref, block_ref, sides_ref, rows, keep, wide, every):
    mine = (me_ref[0] // (2 * OWNERS)) * NX
    core = lax.rem(me_ref[0] // OWNERS, 2)
    first = lax.rem(me_ref[0], NX) * 2
    every[0:32, :] = sides_ref[pl.ds(pl.multiple_of(256 + 32 * core, 8), 32), :]
    for x in range(NX):
        every[32 + x * 16 : 48 + x * 16, :] = block_ref[mine + x, 8:24, :]
    every[96:128, :] = sides_ref[pl.ds(pl.multiple_of(SIDE_ROWS + 256 + 32 * core, 8), 32), :]
    rows[...] = jnp.zeros_like(rows)
    for k in range(10):
        rows[k * 8 : k * 8 + 8, :] = every[pl.ds(pl.multiple_of((first + k) * 8, 8), 8), :]

    def field(f):
        return rows[pl.ds(f, 10, stride=8), :]

    px, py, pz, pol, live = field(0), field(1), field(2), field(3), field(7)
    root = root_of(pol)
    rows[80:90, :] = pol
    rows[96:106, :] = self_term(root)
    trips = trips_of(live)
    write_fields(rows, 10, px, py, pz, root, -2)
    spread(wide, jnp.transpose(rows[...]), range(2, 8), range(4))
    for box in range(2, 8):

        def body(n, carry):
            at = tile_at(n, (box - 2) * TILE)
            spot = [wide[f, at, :] for f in range(4)]
            for k in range(6):
                source = (box // 2 - 1) * 2 + k
                delta = [spot[c] - row(rows, source * 8 + c) for c in range(3)]
                radial, direct = scalars(delta, spot[3] * row(rows, source * 8 + 3))
                keep[k, at, :] = radial
                keep[6 + k, at, :] = direct
            return carry

        lax.fori_loop(0, trips[box, 0], body, 0)


def fourth_kernel(me_ref, rows_ref, keep_ref, wide_ref, res_ref, got_ref, new_ref, out_ref, moved, rows, total):
    first = lax.rem(me_ref[0], NX) * 2
    for c in range(3):
        got = got_ref[c * 4 : c * 4 + 4, :]
        moved[c, 0:4, :] = got
        moved[c, 4:12, :] = res_ref[c * 8 : c * 8 + 8, :]
        moved[c, 12:16, :] = got
    rows[...] = rows_ref[...]
    pol, alone = rows[80:90, :], rows[96:106, :]
    live = rows[pl.ds(7, 10, stride=8), :]
    trips = trips_of(live)
    source = [rows[pl.ds(32 + 4 + c, 2, stride=8), :] for c in range(3)]
    residual = [jnp.concatenate([moved[c, pl.ds(first + k, 1), :] for k in range(10)], axis=0) for c in range(3)]

    def sweep(boxes, moments):
        for c in range(3):
            rows[pl.ds(4 + c, 10, stride=8), :] = moments[c]
        for box in boxes:

            def body(n, carry):
                at = tile_at(n, (box - 2) * TILE)
                spot = [wide_ref[c, at, :] for c in range(3)]
                parts = []
                for k in range(6):
                    near = (box // 2 - 1) * 2 + k
                    delta = [spot[c] - row(rows, near * 8 + c) for c in range(3)]
                    moment = [row(rows, near * 8 + 4 + c) for c in range(3)]
                    parts.append(field_of(delta, keep_ref[k, at, :], keep_ref[6 + k, at, :], moment))
                for c in range(3):
                    total[c, at, :] = added([part[c] for part in parts])
                return carry

            lax.fori_loop(0, trips[box, 0], body, 0)
        return [jnp.concatenate([lane_sums(total, c, box - 2) for box in boxes], axis=0) for c in range(3)]

    one = [pol * residual[c] for c in range(3)]
    fields = sweep(range(2, 8), one)
    two = []
    edge = jnp.zeros((2, TILE), F32)
    for c in range(3):
        value = pol[2:8] * (residual[c][2:8] + fields[c] + alone[2:8] * one[c][2:8])
        two.append(jnp.concatenate([edge, jnp.where(live[2:8] > 0.0, value, 0.0), edge], axis=0))
    fields = sweep(range(4, 6), two)
    for c in range(3):
        value = pol[4:6] * (residual[c][4:6] + fields[c] + alone[4:6] * two[c][4:6])
        three = source[c] + jnp.where(live[4:6] > 0.0, value, 0.0)
        for w in range(2):
            new_ref[c : c + 1, w * TILE : (w + 1) * TILE] = three[w : w + 1]
            out_ref[c : c + 1, w * TILE : (w + 1) * TILE] = residual[c][4 + w : 5 + w]


VMEM = pl.BlockSpec(memory_space=pltpu.VMEM)
SMEM = pl.BlockSpec(memory_space=pltpu.SMEM)
HBM = pl.BlockSpec(memory_space=pltpu.HBM)


def shape_of(shape):
    return shape if isinstance(shape, jax.ShapeDtypeStruct) else jax.ShapeDtypeStruct(shape, F32)


def call(body, ins, outs, scratch, cost, limit, name):
    return pl.pallas_call(
        body,
        in_specs=ins,
        out_specs=[VMEM] * len(outs),
        out_shape=[shape_of(shape) for shape in outs],
        scratch_shapes=[pltpu.VMEM(shape, F32) if isinstance(shape, tuple) else shape for shape in scratch],
        cost_estimate=pl.CostEstimate(flops=cost, bytes_accessed=1 << 20, transcendentals=0),
        compiler_params=pltpu.CompilerParams(vmem_limit_bytes=limit << 20),
        name=name,
    )


def device(group, box):
    return group * OWNERS + box


def rounds():
    plane = [
        [device(2 * y + core, z * NX + x) for y in range(NY) for x in range(NX)]
        for core in range(2)
        for z in range(OWNERS // NX)
    ]
    chip = [[device(2 * y, b), device(2 * y + 1, b)] for y in range(NY) for b in range(OWNERS)]
    up = [[(device(g, b), device(g, b + NX)) for b in range(OWNERS - NX)] for g in range(GROUPS)]
    down = [[(target, source) for source, target in pairs] for pairs in up]
    apart = [pair for g in range(GROUPS) for pair in (down[g] if g % 2 else up[g])]
    near_side = [(s, t) for pairs in up for s, t in pairs if s % NX < 2]
    near_side += [(s, t) for pairs in down for s, t in pairs if s % NX >= 2]
    return plane, chip, apart, near_side


PLANE_SETS, CHIP_SETS, APART, NEAR_SIDE = rounds()
OWN_ROWS = PLANE * 8 + 64
SIDE_ROWS = 256 + 64


def on_device(
    dipoles, perm_field, positions, polarizability, occupancy, far_boxes, far_class, far_count, far_scale, translations
):
    me = lax.axis_index("d").astype(jnp.int32)[None]
    lists = pltpu.VMEM((2, ILIST), jnp.int32)
    [chunk] = call(
        first_kernel,
        [SMEM] * 3 + [HBM] * 7,
        [(PLANE, CHUNK, TILE)],
        [(NTERM * 8, TILE), (CHUNK, TILE)]
        + [(3, 2 * TILE)] * 3
        + [(1, 2 * TILE), (2, ILIST), lists, lists, pltpu.SemaphoreType.DMA((7,))],
        1 << 20,
        60,
        "first",
    )(
        me, occupancy, far_count, dipoles, perm_field, positions, polarizability.reshape(1, 2 * TILE),
        far_boxes, far_class, far_scale,
    )
    block = lax.all_to_all(chunk, "d", 0, 0, axis_index_groups=PLANE_SETS, tiled=True)
    half = jax.ShapeDtypeStruct((CLASSES * 256, NTERM), BF16)
    t_high, t_low = call(prepare_kernel, [VMEM], [half, half], [], 1 << 28, 12, "prepare")(
        jnp.transpose(translations, (1, 0, 2))
    )
    mine = (me[0] // (2 * OWNERS)) * NX
    core = (me[0] // OWNERS) % 2
    near = lax.dynamic_slice(block, (mine, 8, 0), (NX, 16, TILE)).reshape(64, TILE)
    part = jnp.concatenate([block[:, 0:8, :].reshape(PLANE * 8, TILE), near], axis=0)
    part, t_high, t_low = lax.optimization_barrier((part, t_high, t_low))
    own = lax.all_gather(part, "d", axis_index_groups=CHIP_SETS, axis=0)
    edges = lax.dynamic_slice(own, (0, PLANE * 8 + 32 * (1 - core), 0), (2, 32, TILE)).reshape(64, TILE)
    away = jnp.concatenate([own[:, 0 : PLANE * 8].reshape(256, TILE), edges], axis=0)
    came = lax.ppermute(away, "d", APART)
    own = own.reshape(2 * OWN_ROWS, TILE)
    half = jax.ShapeDtypeStruct((8 * 176, TILE), BF16)
    sel, near_zero, wide, m_high, m_low = call(
        second_kernel,
        [SMEM, VMEM],
        [(64, 192), (24, TILE), (4, 8 * TILE, TILE), half, half],
        [(TILE, TILE), (3, 8 * TILE, TILE), (NTERM * 8, TILE)],
        1 << 28,
        12,
        "second",
    )(me, block)
    came, sel = lax.optimization_barrier((came, sel))
    sides = lax.all_gather(came, "d", axis_index_groups=CHIP_SETS, axis=0).reshape(2 * SIDE_ROWS, TILE)
    residual, send = call(
        third_kernel,
        [SMEM] + [VMEM] * 10,
        [(24, TILE), (12, TILE)],
        [(256, TILE), (48, TILE), (48, TILE), (24, TILE), (TILE, TILE), (3, 4 * TILE, TILE)],
        1 << 28,
        16,
        "third",
    )(me, block, own, sides, sel, near_zero, wide, m_high, m_low, t_high, t_low)
    got = lax.ppermute(send, "d", NEAR_SIDE)
    rows, keep, wide = call(
        window_kernel,
        [SMEM] + [VMEM] * 2,
        [(TILE, TILE), (12, 6 * TILE, TILE), (4, 6 * TILE, TILE)],
        [(TILE, TILE)],
        1 << 28,
        16,
        "window",
    )(me, block, sides)
    new, out = call(
        fourth_kernel,
        [SMEM] + [VMEM] * 5,
        [(3, 2 * TILE), (3, 2 * TILE)],
        [(3, 16, TILE), (TILE, TILE), (3, 6 * TILE, TILE)],
        1 << 28,
        16,
        "fourth",
    )(me, rows, keep, wide, residual, got)
    return new, out


def solution(mesh):
    flat = Mesh(mesh.devices.reshape(-1), ("d",))
    return jax.shard_map(
        on_device,
        mesh=flat,
        in_specs=(
            P(None, "d"), P(None, "d"), P(None, "d"), P("d"), P("d"), P("d", None), P("d", None), P("d"), P("d", None), P(),
        ),
        out_specs=(P(None, "d"), P(None, "d")),
        check_vma=False,
    )
```

```python
import jax
import jax.numpy as jnp
from jax import lax
from jax.experimental import pallas as pl
from jax.experimental.pallas import tpu as pltpu
from jax.sharding import Mesh
from jax.sharding import PartitionSpec as P

TILE = 128
ORDER = 8
NTERM = 165
REST = NTERM - TILE
ILIST = 189
CLASSES = 8
GROUPS = 8
OWNERS = 64
NX = 4
NY = 4
PLANE = NX * NY
CHUNK = 40
F32 = jnp.float32
BF16 = jnp.bfloat16

HALF = 5.4
ROOT_THOLE = 0.39**0.5
NT = (((1,), (1,)), ((), ()))
NN = (((1,), (0,)), ((), ()))


def term_table():
    listing = []
    for degree in range(ORDER + 1):
        for first in range(degree + 1):
            for second in range(degree + 1 - first):
                listing.append((first, second, degree - first - second))
    return listing


TERMS = term_table()


def dot(a, b, dims):
    return lax.dot_general(a, b, dims, preferred_element_type=F32)


def halves(x):
    high = x.astype(BF16)
    return high, (x - high.astype(F32)).astype(BF16)


def dot_three(a, b, dims):
    a_high, a_low = halves(a)
    b_high, b_low = halves(b)
    return dot(a_high, b_high, dims) + (dot(a_high, b_low, dims) + dot(a_low, b_high, dims))


def chebyshev(coord):
    series = [None, coord]
    doubled = 2.0 * coord
    series.append(doubled * coord - 1.0)
    for _ in range(3, ORDER + 1):
        series.append(doubled * series[-1] - series[-2])
    return series


def write_monomials(ref, px, py, pz):
    cx, cy, cz = chebyshev(px), chebyshev(py), chebyshev(pz)
    cross = {}
    for t, (i, j, k) in enumerate(TERMS):
        if (i, j) not in cross:
            if i and j:
                cross[i, j] = cx[i] * cy[j]
            else:
                cross[i, j] = cx[i] if i else cy[j]
        head = cross[i, j]
        if head is None:
            value = jnp.ones_like(px) if k == 0 else cz[k]
        else:
            value = head if k == 0 else head * cz[k]
        ref[t * 8 : t * 8 + 8, :] = value


def own_place():
    me = lax.axis_index("d")
    return (me // OWNERS) & 1, (me // NX) & (OWNERS // NX - 1), me & (NX - 1), (me // (2 * OWNERS)) * NX


def first_kernel(
    occ_hbm, count_hbm, dip_hbm, perm_hbm, pos_hbm, pol_hbm, boxes_hbm, class_hbm, scale_hbm, out_ref,
    mono, chunk, dip_ref, perm_ref, pos_ref, pol_ref, scale_ref, boxes_ref, class_ref, occ_ref, count_ref, sems,
):
    pairs = (
        (pos_hbm, pos_ref), (dip_hbm, dip_ref), (pol_hbm, pol_ref), (perm_hbm, perm_ref),
        (boxes_hbm, boxes_ref), (class_hbm, class_ref), (scale_hbm, scale_ref), (occ_hbm, occ_ref), (count_hbm, count_ref),
    )
    copies = [pltpu.make_async_copy(source, target, sems.at[n]) for n, (source, target) in enumerate(pairs)]
    for copy in copies:
        copy.start()
    chunk[...] = jnp.zeros_like(chunk)
    lane = lax.broadcasted_iota(jnp.int32, (1, TILE), 1)
    for copy in copies:
        copy.wait()
    for w in range(2):
        live = (lane < occ_ref[w]).astype(F32)
        lanes = slice(w * TILE, (w + 1) * TILE)
        base = 8 + w * 8
        chunk[base : base + 3, :] = pos_ref[:, lanes]
        chunk[base + 3 : base + 4, :] = pol_ref[:, lanes]
        chunk[base + 4 : base + 7, :] = dip_ref[:, lanes] * live
        chunk[base + 7 : base + 8, :] = live
        chunk[24 + w * 3 : 27 + w * 3, :] = perm_ref[:, lanes]
    plane = own_place()[1]
    box = boxes_ref[...]
    within = box & 1
    layer = (box >> 1) & (OWNERS - 1)
    group = box >> 7
    step = (layer >> 2) - plane
    stack = jnp.where(step == 0, 0, jnp.where(step < 0, 1, 2))
    place = within * 96 + stack * 32 + (group & 1) * PLANE + (group >> 1) * NX + (layer & 3)
    place = place.astype(F32)
    kind = class_ref[...].astype(F32)
    entry = lax.broadcasted_iota(jnp.int32, (1, ILIST), 1)
    for w in range(2):
        weight = scale_ref[w : w + 1, :] * (entry < count_ref[w]).astype(F32)
        for n, row in enumerate((place[w : w + 1, :], kind[w : w + 1, :], weight)):
            chunk[30 + w * 3 + n : 31 + w * 3 + n, :] = row[:, :TILE]
            chunk[36 + n : 37 + n, w * 64 : w * 64 + ILIST - TILE] = row[:, TILE:]
    def both(row):
        two = chunk[pl.ds(8 + row, 2, stride=8), :]
        return jnp.concatenate([two, two, two, two], axis=0)

    write_monomials(mono, both(0), both(1), both(2))
    for w in range(2):
        terms = mono[pl.ds(w, NTERM, stride=8), :]
        moment = dot_three(chunk[12 + w * 8 : 15 + w * 8, :], terms, NT)
        for c in range(3):
            chunk[c * 2 + w : c * 2 + w + 1, :] = moment[c : c + 1, :TILE]
            chunk[6 + w : 7 + w, c * REST : (c + 1) * REST] = moment[c : c + 1, TILE:]
    whole = chunk[...]
    for m in range(PLANE):
        out_ref[m, :, :] = whole


def write_fields(rows_ref, number, px, py, pz, root, first_layer):
    box = lax.broadcasted_iota(jnp.int32, (number, TILE), 0)
    rows_ref[pl.ds(0, number, stride=8), :] = HALF * (px + 2.0 * (box & 1).astype(F32))
    rows_ref[pl.ds(1, number, stride=8), :] = HALF * py
    rows_ref[pl.ds(2, number, stride=8), :] = HALF * (pz + 2.0 * ((box >> 1) + first_layer).astype(F32))
    rows_ref[pl.ds(3, number, stride=8), :] = root


def root_of(pol):
    return jnp.where(pol > 0.0, ROOT_THOLE * lax.rsqrt(jnp.where(pol > 0.0, pol, 1.0)), 0.0)


def scalars(delta, roots):
    dx, dy, dz = delta
    squared = dx * dx + dy * dy + (dz * dz + 1.0)
    inverse = lax.rsqrt(squared)
    inv_two = inverse * inverse
    inv_three = inverse * inv_two
    minus = (squared * (squared * inverse)) * roots
    damping = jnp.exp(minus)
    lambda_three = 1.0 - damping
    lambda_five = lambda_three + minus * damping
    return (3.0 * lambda_five) * (inv_three * inv_two), lambda_three * inv_three


def field_of(delta, radial, direct, moment):
    along = radial * (delta[0] * moment[0] + delta[1] * moment[1] + delta[2] * moment[2])
    return [delta[c] * along - direct * moment[c] for c in range(3)]


def added(parts):
    while len(parts) > 1:
        parts = [parts[i] + parts[i + 1] if i + 1 < len(parts) else parts[i] for i in range(0, len(parts), 2)]
    return parts[0]


def row(ref, at):
    return ref[pl.ds(at, 8, stride=0), :]


def tile_at(n, base=0):
    return pl.ds(pl.multiple_of(base + n * 8, 8), 8)


def trips_of(live):
    count = jnp.sum(live, axis=1, keepdims=True)
    return ((count + 7.0) * 0.125).astype(jnp.int32)


def spread(wide_ref, cols, boxes, fields):
    for slot, box in enumerate(boxes):
        for f in fields:
            at = box * 8 + f
            value = jnp.broadcast_to(cols[:, at : at + 1], (TILE, TILE))
            wide_ref[f, slot * TILE : (slot + 1) * TILE, :] = -value if f == 3 else value


def near_boxes(total_ref, slots, wide_ref, targets, trips, rows_ref, sources):
    def body(n, carry):
        mine = [[wide_ref[f, tile_at(n, target * TILE), :] for f in range(4)] for target in targets]
        parts = [[] for _ in targets]
        for box in sources:
            where = [row(rows_ref, box * 8 + f) for f in range(7)]
            for i, spot in enumerate(mine):
                delta = [spot[c] - where[c] for c in range(3)]
                radial, direct = scalars(delta, spot[3] * where[3])
                parts[i].append(field_of(delta, radial, direct, where[4:7]))
        for i, slot in enumerate(slots):
            for c in range(3):
                total_ref[c, tile_at(n, slot * TILE), :] = added([part[c] for part in parts[i]])
        return carry

    lax.fori_loop(0, trips, body, 0)


def lane_sums(total_ref, c, slot):
    return jnp.sum(jnp.transpose(total_ref[c, slot * TILE : (slot + 1) * TILE, :]), axis=0, keepdims=True)


def self_term(root):
    return 1.0 - jnp.exp(-(root * root))


def prepare_kernel(trans_ref, high_ref, low_ref):
    high_ref[...] = jnp.zeros_like(high_ref)
    low_ref[...] = jnp.zeros_like(low_ref)
    for o in range(CLASSES):
        high, low = halves(jnp.transpose(trans_ref[:, o, :]))
        high_ref[o * 256 : o * 256 + NTERM, :] = high
        low_ref[o * 256 : o * 256 + NTERM, :] = low


def second_kernel(block_ref, sel_ref, near_ref, wide, m_high_ref, m_low_ref, rows, total, mono):
    mine = own_place()[3]
    rows[...] = jnp.zeros_like(rows)
    for x in range(NX):
        rows[x * 16 : x * 16 + 16, :] = block_ref[mine + x, 8:24, :]

    def field(f):
        return rows[pl.ds(f, 8, stride=8), :]

    px, py, pz, root = field(0), field(1), field(2), root_of(field(3))
    trips = trips_of(field(7))
    write_monomials(mono, px, py, pz)
    write_fields(rows, 8, px, py, pz, root, 0)
    spread(wide, jnp.transpose(rows[...]), range(8), range(4))
    for k in range(8):
        high, low = halves(mono[pl.ds(k, NTERM, stride=8), :])
        m_high_ref[k * 176 : k * 176 + NTERM, :] = high
        m_low_ref[k * 176 : k * 176 + NTERM, :] = low
    for box in range(8):
        low, high = max(box // 2 - 1, 0), min(box // 2 + 1, NX - 1)
        near_boxes(total, [box], wide, [box], trips[box, 0], rows, range(low * 2, high * 2 + 2))
    spot = lax.broadcasted_iota(jnp.int32, (192, TILE), 0)
    kinds = lax.broadcasted_iota(jnp.int32, (CLASSES, TILE), 0)
    side = lax.broadcasted_iota(jnp.int32, (CLASSES, TILE), 1) >> 6
    for x in range(NX):
        got = jnp.zeros((32, 192), F32)
        first, second = [], []
        for w in range(2):
            at = 30 + w * 3
            place = block_ref[mine + x, at : at + 1, :].astype(jnp.int32)
            kind = block_ref[mine + x, at + 1 : at + 2, :].astype(jnp.int32)
            weight = jnp.where(kinds == kind, block_ref[mine + x, at + 2 : at + 3, :], 0.0)
            chosen = jnp.where(spot == place, 1.0, 0.0).astype(BF16)
            high = weight.astype(BF16).astype(F32)
            first.append(dot(jnp.concatenate([high, weight - high], axis=0).astype(BF16), chosen, NT))
        place = block_ref[mine + x, 36:37, :].astype(jnp.int32)
        kind = block_ref[mine + x, 37:38, :].astype(jnp.int32)
        weight = jnp.where(kinds == kind, block_ref[mine + x, 38:39, :], 0.0)
        high = weight.astype(BF16).astype(F32)
        low = weight - high
        both = [jnp.where(side == w, part, 0.0) for w in range(2) for part in (high, low)]
        chosen = jnp.where(spot == place, 1.0, 0.0).astype(BF16)
        second = dot(jnp.concatenate(both, axis=0).astype(BF16), chosen, NT)
        for w in range(2):
            k = x * 2 + w
            tail = second[w * 16 : w * 16 + 16]
            sel_ref[k * 8 : k * 8 + 8, :] = (first[w][0:8] + tail[0:8]) + (first[w][8:16] + tail[8:16])
    for c in range(3):
        for box in range(8):
            near_ref[c * 8 + box : c * 8 + box + 1, :] = lane_sums(total, c, box)


def third_kernel(
    block_ref, own_ref, sides_ref, sel_ref, near_ref, wide_ref, m_high_ref, m_low_ref, t_high_ref, t_low_ref,
    res_ref, send_ref, summed, head, rest, far, rows, total,
):
    core, _, x_me, mine = own_place()
    sel_high, sel_low = halves(sel_ref[...])
    both = jnp.concatenate([sel_high, sel_low], axis=0)
    for kind in range(4):
        pieces = []
        for w in range(2):
            pieces += [own_ref[pl.ds(at + kind * 2 + w, 16, stride=8), :] for at in (0, OWN_ROWS)]
            pieces += [sides_ref[pl.ds(at + kind * 2 + w, 32, stride=8), :] for at in (0, SIDE_ROWS)]
        high, low = halves(jnp.concatenate(pieces, axis=0))
        got = dot(both, high, NN)
        summed[kind * 64 : kind * 64 + 64, :] = got[0:64] + (got[64:128] + dot(sel_high, low, NN))
    parts = []
    for c in range(3):
        pieces = []
        for o in range(CLASSES):
            pieces.append(summed[pl.ds(c * 64 + o, 8, stride=8), :])
            tail = summed[pl.ds(192 + o, 8, stride=8), :][:, c * REST : (c + 1) * REST]
            pieces.append(jnp.concatenate([tail, jnp.zeros((8, TILE - REST), F32)], axis=1))
        parts.append(jnp.concatenate(pieces, axis=1))
    parts.append(jnp.zeros((8, CLASSES * 256), F32))
    high, low = halves(jnp.concatenate(parts, axis=0))
    got = dot(jnp.concatenate([high, low], axis=0), t_high_ref[...], NN)
    moved = got[0:24] + (got[32:56] + dot(high, t_low_ref[...], NN)[0:24])
    moved_high = moved.astype(BF16).astype(F32)
    for n, part in enumerate((moved_high, moved - moved_high)):
        head[n * 24 : n * 24 + 24, :] = part[:, 0:TILE]
        rest[n * 24 : n * 24 + 24, 0:REST] = part[:, TILE:]
    rows[...] = jnp.zeros_like(rows)
    rows[0:16, :] = sides_ref[pl.ds(pl.multiple_of(272 + 32 * core, 8), 16), :]
    for x in range(NX):
        rows[16 + x * 16 : 32 + x * 16, :] = block_ref[mine + x, 8:24, :]
    rows[80:96, :] = sides_ref[pl.ds(pl.multiple_of(SIDE_ROWS + 256 + 32 * core, 8), 16), :]

    def field(f):
        return rows[pl.ds(f, 12, stride=8), :]

    px, py, pz, pol = field(0), field(1), field(2), field(3)
    live = rows[pl.ds(16 + 7, 8, stride=8), :]
    source = [rows[pl.ds(16 + 4 + c, 8, stride=8), :] for c in range(3)]
    root = root_of(pol)
    trips = trips_of(live)
    write_fields(rows, 12, px, py, pz, root, -1)
    for slots, boxes, sources in (((0, 1), (0, 1), (0, 1)), ((2, 3), (6, 7), (10, 11))):
        most = jnp.maximum(trips[boxes[0], 0], trips[boxes[1], 0])
        near_boxes(total, slots, wide_ref, boxes, most, rows, sources)
    for k in range(8):
        left = jnp.concatenate([head[pl.ds(k, 6, stride=8), :], rest[pl.ds(k, 6, stride=8), :][:, 0:REST]], axis=1)
        left = left.astype(BF16)
        with_high = dot(left, m_high_ref[k * 176 : k * 176 + NTERM, :], NN)
        with_low = dot(left, m_low_ref[k * 176 : k * 176 + NTERM, :], NN)
        value = with_high[0:3] + (with_high[3:6] + with_low[0:3])
        for c in range(3):
            far[c * 8 + k : c * 8 + k + 1, :] = value[c : c + 1]
    alone = self_term(root[2:10])
    nothing = jnp.zeros((4, TILE), F32)
    for c in range(3):
        perm = jnp.concatenate(
            [block_ref[mine + x, 24 + w * 3 + c : 25 + w * 3 + c, :] for x in range(NX) for w in range(2)], axis=0
        )
        ends = [lane_sums(total, c, slot) for slot in range(4)]
        edge = jnp.concatenate(ends[0:2] + [nothing] + ends[2:4], axis=0)
        near_zero = near_ref[c * 8 : c * 8 + 8, :] + edge + alone * source[c]
        res_ref[c * 8 : c * 8 + 8, :] = jnp.where(
            live > 0.0, perm + far[c * 8 : c * 8 + 8, :] + near_zero - source[c] / pol[2:10], 0.0
        )
    first = jnp.where(x_me < 2, 4, 0)
    for c in range(3):
        for k in range(4):
            send_ref[c * 4 + k : c * 4 + k + 1, :] = res_ref[pl.ds(c * 8 + first + k, 1), :]


def window_kernel(block_ref, sides_ref, wide_ref, rows, keep, spots, every, edge):
    core, _, x_me, mine = own_place()
    first = x_me * 2
    every[0:32, :] = sides_ref[pl.ds(pl.multiple_of(256 + 32 * core, 8), 32), :]
    for x in range(NX):
        every[32 + x * 16 : 48 + x * 16, :] = block_ref[mine + x, 8:24, :]
    every[96:128, :] = sides_ref[pl.ds(pl.multiple_of(SIDE_ROWS + 256 + 32 * core, 8), 32), :]
    rows[...] = jnp.zeros_like(rows)
    for k in range(10):
        rows[k * 8 : k * 8 + 8, :] = every[pl.ds(pl.multiple_of((first + k) * 8, 8), 8), :]

    def field(f):
        return rows[pl.ds(f, 10, stride=8), :]

    px, py, pz, pol, live = field(0), field(1), field(2), field(3), field(7)
    root = root_of(pol)
    rows[80:90, :] = pol
    rows[96:106, :] = self_term(root)
    trips = trips_of(live)
    write_fields(rows, 10, px, py, pz, root, x_me - 2)
    high_side = x_me >= 2
    cols = jnp.transpose(rows[...])
    for w in range(2):
        for f in range(4):
            low, high = (2 + w) * 8 + f, (6 + w) * 8 + f
            column = jnp.where(high_side, cols[:, high : high + 1], cols[:, low : low + 1])
            value = jnp.broadcast_to(column, (TILE, TILE))
            edge[f, w * TILE : (w + 1) * TILE, :] = -value if f == 3 else value
    for box in range(2, 8):
        at_edge = {1: x_me == 0, 3: x_me == NX - 1}.get(box // 2)
        plane_box = first + box - 4
        if at_edge is not None:
            plane_box = jnp.where(at_edge, 0, plane_box)

        def body(n, carry):
            for u in range(2):
                at = tile_at(n * 2 + u, (box - 2) * TILE)
                spot = [wide_ref[f, tile_at(n * 2 + u, plane_box * TILE), :] for f in range(4)]
                if at_edge is not None:
                    beside = tile_at(n * 2 + u, (box % 2) * TILE)
                    spot = [jnp.where(at_edge, edge[f, beside, :], spot[f]) for f in range(4)]
                for c in range(3):
                    spots[c, at, :] = spot[c]
                for k in range(6):
                    source = (box // 2 - 1) * 2 + k
                    delta = [spot[c] - row(rows, source * 8 + c) for c in range(3)]
                    radial, direct = scalars(delta, spot[3] * row(rows, source * 8 + 3))
                    keep[k, at, :] = radial
                    keep[6 + k, at, :] = direct
            return carry

        lax.fori_loop(0, (trips[box, 0] + 1) // 2, body, 0)


def fourth_kernel(rows_ref, keep_ref, wide_ref, res_ref, got_ref, new_ref, out_ref, moved, rows, total):
    first = own_place()[2] * 2
    for c in range(3):
        got = got_ref[c * 4 : c * 4 + 4, :]
        moved[c, 0:4, :] = got
        moved[c, 4:12, :] = res_ref[c * 8 : c * 8 + 8, :]
        moved[c, 12:16, :] = got
    rows[...] = rows_ref[...]
    pol, alone = rows[80:90, :], rows[96:106, :]
    live = rows[pl.ds(7, 10, stride=8), :]
    trips = trips_of(live)
    source = [rows[pl.ds(32 + 4 + c, 2, stride=8), :] for c in range(3)]
    residual = [jnp.concatenate([moved[c, pl.ds(first + k, 1), :] for k in range(10)], axis=0) for c in range(3)]

    def sweep(boxes, moments):
        for c in range(3):
            rows[pl.ds(4 + c, 10, stride=8), :] = moments[c]
        for box in boxes:

            def body(n, carry):
                at = tile_at(n, (box - 2) * TILE)
                spot = [wide_ref[c, at, :] for c in range(3)]
                parts = []
                for k in range(6):
                    near = (box // 2 - 1) * 2 + k
                    delta = [spot[c] - row(rows, near * 8 + c) for c in range(3)]
                    moment = [row(rows, near * 8 + 4 + c) for c in range(3)]
                    parts.append(field_of(delta, keep_ref[k, at, :], keep_ref[6 + k, at, :], moment))
                for c in range(3):
                    total[c, at, :] = added([part[c] for part in parts])
                return carry

            lax.fori_loop(0, trips[box, 0], body, 0)
        return [jnp.concatenate([lane_sums(total, c, box - 2) for box in boxes], axis=0) for c in range(3)]

    one = [pol * residual[c] for c in range(3)]
    fields = sweep(range(2, 8), one)
    two = []
    edge = jnp.zeros((2, TILE), F32)
    for c in range(3):
        value = pol[2:8] * (residual[c][2:8] + fields[c] + alone[2:8] * one[c][2:8])
        two.append(jnp.concatenate([edge, jnp.where(live[2:8] > 0.0, value, 0.0), edge], axis=0))
    fields = sweep(range(4, 6), two)
    for c in range(3):
        value = pol[4:6] * (residual[c][4:6] + fields[c] + alone[4:6] * two[c][4:6])
        three = source[c] + jnp.where(live[4:6] > 0.0, value, 0.0)
        for w in range(2):
            new_ref[c : c + 1, w * TILE : (w + 1) * TILE] = three[w : w + 1]
            out_ref[c : c + 1, w * TILE : (w + 1) * TILE] = residual[c][4 + w : 5 + w]


VMEM = pl.BlockSpec(memory_space=pltpu.VMEM)
HBM = pl.BlockSpec(memory_space=pltpu.HBM)


def shape_of(shape):
    return shape if isinstance(shape, jax.ShapeDtypeStruct) else jax.ShapeDtypeStruct(shape, F32)


def call(body, ins, outs, scratch, cost, limit, name):
    return pl.pallas_call(
        body,
        in_specs=ins,
        out_specs=[VMEM] * len(outs),
        out_shape=[shape_of(shape) for shape in outs],
        scratch_shapes=[pltpu.VMEM(shape, F32) if isinstance(shape, tuple) else shape for shape in scratch],
        cost_estimate=pl.CostEstimate(flops=cost, bytes_accessed=1 << 20, transcendentals=0),
        compiler_params=pltpu.CompilerParams(vmem_limit_bytes=limit << 20),
        name=name,
    )


def device(group, box):
    return group * OWNERS + box


def rounds():
    plane = [
        [device(2 * y + core, z * NX + x) for y in range(NY) for x in range(NX)]
        for core in range(2)
        for z in range(OWNERS // NX)
    ]
    chip = [[device(2 * y, b), device(2 * y + 1, b)] for y in range(NY) for b in range(OWNERS)]
    up = [[(device(g, b), device(g, b + NX)) for b in range(OWNERS - NX)] for g in range(GROUPS)]
    down = [[(target, source) for source, target in pairs] for pairs in up]
    apart = [pair for g in range(GROUPS) for pair in (down[g] if g % 2 else up[g])]
    near_side = [(s, t) for pairs in up for s, t in pairs if s % NX < 2]
    near_side += [(s, t) for pairs in down for s, t in pairs if s % NX >= 2]
    return plane, chip, apart, near_side


PLANE_SETS, CHIP_SETS, APART, NEAR_SIDE = rounds()
OWN_ROWS = PLANE * 8 + 64
SIDE_ROWS = 256 + 64


def on_device(
    dipoles, perm_field, positions, polarizability, occupancy, far_boxes, far_class, far_count, far_scale, translations
):
    me = lax.axis_index("d").astype(jnp.int32)
    two = pltpu.SMEM((2,), jnp.int32)
    lists = pltpu.VMEM((2, ILIST), jnp.int32)
    [chunk] = call(
        first_kernel,
        [HBM] * 9,
        [(PLANE, CHUNK, TILE)],
        [(NTERM * 8, TILE), (CHUNK, TILE)]
        + [(3, 2 * TILE)] * 3
        + [(1, 2 * TILE), (2, ILIST), lists, lists, two, two, pltpu.SemaphoreType.DMA((9,))],
        1 << 20,
        60,
        "first",
    )(
        occupancy, far_count, dipoles, perm_field, positions, polarizability.reshape(1, 2 * TILE),
        far_boxes, far_class, far_scale,
    )
    block = lax.all_to_all(chunk, "d", 0, 0, axis_index_groups=PLANE_SETS, tiled=True)
    half = jax.ShapeDtypeStruct((CLASSES * 256, NTERM), BF16)
    t_high, t_low = call(prepare_kernel, [VMEM], [half, half], [], 1 << 28, 12, "prepare")(
        jnp.transpose(translations, (1, 0, 2))
    )
    mine = (me // (2 * OWNERS)) * NX
    core = (me // OWNERS) & 1
    near = lax.dynamic_slice(block, (mine, 8, 0), (NX, 16, TILE)).reshape(64, TILE)
    part = jnp.concatenate([block[:, 0:8, :].reshape(PLANE * 8, TILE), near], axis=0)
    part, t_high, t_low = lax.optimization_barrier((part, t_high, t_low))
    own = lax.all_gather(part, "d", axis_index_groups=CHIP_SETS, axis=0)
    edges = lax.dynamic_slice(own, (0, PLANE * 8 + 32 * (1 - core), 0), (2, 32, TILE)).reshape(64, TILE)
    away = jnp.concatenate([own[:, 0 : PLANE * 8].reshape(256, TILE), edges], axis=0)
    came = lax.ppermute(away, "d", APART)
    own = own.reshape(2 * OWN_ROWS, TILE)
    half = jax.ShapeDtypeStruct((8 * 176, TILE), BF16)
    sel, near_zero, wide, m_high, m_low = call(
        second_kernel,
        [VMEM],
        [(64, 192), (24, TILE), (4, 8 * TILE, TILE), half, half],
        [(TILE, TILE), (3, 8 * TILE, TILE), (NTERM * 8, TILE)],
        1 << 28,
        12,
        "second",
    )(block)
    came, sel = lax.optimization_barrier((came, sel))
    sides = lax.all_gather(came, "d", axis_index_groups=CHIP_SETS, axis=0).reshape(2 * SIDE_ROWS, TILE)
    residual, send = call(
        third_kernel,
        [VMEM] * 10,
        [(24, TILE), (12, TILE)],
        [(256, TILE), (48, TILE), (48, TILE), (24, TILE), (TILE, TILE), (3, 4 * TILE, TILE)],
        1 << 28,
        16,
        "third",
    )(block, own, sides, sel, near_zero, wide, m_high, m_low, t_high, t_low)
    got = lax.ppermute(send, "d", NEAR_SIDE)
    rows, keep, spots = call(
        window_kernel,
        [VMEM] * 3,
        [(TILE, TILE), (12, 6 * TILE, TILE), (3, 6 * TILE, TILE)],
        [(TILE, TILE), (4, 2 * TILE, TILE)],
        1 << 28,
        16,
        "window",
    )(block, sides, wide)
    new, out = call(
        fourth_kernel,
        [VMEM] * 5,
        [(3, 2 * TILE), (3, 2 * TILE)],
        [(3, 16, TILE), (TILE, TILE), (3, 6 * TILE, TILE)],
        1 << 28,
        16,
        "fourth",
    )(rows, keep, spots, residual, got)
    return new, out


def solution(mesh):
    flat = Mesh(mesh.devices.reshape(-1), ("d",))
    return jax.shard_map(
        on_device,
        mesh=flat,
        in_specs=(
            P(None, "d"), P(None, "d"), P(None, "d"), P("d"), P("d"), P("d", None), P("d", None), P("d"), P("d", None), P(),
        ),
        out_specs=(P(None, "d"), P(None, "d")),
        check_vma=False,
    )
```

```python
import jax
import jax.numpy as jnp
from jax import lax
from jax.experimental import pallas as pl
from jax.experimental.pallas import tpu as pltpu
from jax.sharding import Mesh
from jax.sharding import PartitionSpec as P

TILE = 128
ORDER = 8
NTERM = 165
REST = NTERM - TILE
ILIST = 189
CLASSES = 8
GROUPS = 8
OWNERS = 64
NX = 4
NY = 4
PLANE = NX * NY
CHUNK = 40
F32 = jnp.float32
BF16 = jnp.bfloat16

HALF = 5.4
ROOT_THOLE = 0.39**0.5
NT = (((1,), (1,)), ((), ()))
NN = (((1,), (0,)), ((), ()))


def term_table():
    listing = []
    for degree in range(ORDER + 1):
        for first in range(degree + 1):
            for second in range(degree + 1 - first):
                listing.append((first, second, degree - first - second))
    return listing


TERMS = term_table()


def dot(a, b, dims):
    return lax.dot_general(a, b, dims, preferred_element_type=F32)


def halves(x):
    high = x.astype(BF16)
    return high, (x - high.astype(F32)).astype(BF16)


def dot_three(a, b, dims):
    a_high, a_low = halves(a)
    b_high, b_low = halves(b)
    return dot(a_high, b_high, dims) + (dot(a_high, b_low, dims) + dot(a_low, b_high, dims))


def chebyshev(coord):
    series = [None, coord]
    doubled = 2.0 * coord
    series.append(doubled * coord - 1.0)
    for _ in range(3, ORDER + 1):
        series.append(doubled * series[-1] - series[-2])
    return series


def write_monomials(ref, px, py, pz):
    cx, cy, cz = chebyshev(px), chebyshev(py), chebyshev(pz)
    cross = {}
    for t, (i, j, k) in enumerate(TERMS):
        if (i, j) not in cross:
            if i and j:
                cross[i, j] = cx[i] * cy[j]
            else:
                cross[i, j] = cx[i] if i else cy[j]
        head = cross[i, j]
        if head is None:
            value = jnp.ones_like(px) if k == 0 else cz[k]
        else:
            value = head if k == 0 else head * cz[k]
        ref[t * 8 : t * 8 + 8, :] = value


def own_place():
    me = lax.axis_index("d")
    return (me // OWNERS) & 1, (me // NX) & (OWNERS // NX - 1), me & (NX - 1), (me // (2 * OWNERS)) * NX


def first_kernel(
    occ_hbm, count_hbm, dip_hbm, perm_hbm, pos_hbm, pol_hbm, boxes_hbm, class_hbm, scale_hbm, out_ref,
    mono, chunk, dip_ref, perm_ref, pos_ref, pol_ref, scale_ref, boxes_ref, class_ref, occ_ref, count_ref, sems,
):
    pairs = (
        (pos_hbm, pos_ref), (dip_hbm, dip_ref), (pol_hbm, pol_ref), (perm_hbm, perm_ref),
        (boxes_hbm, boxes_ref), (class_hbm, class_ref), (scale_hbm, scale_ref), (occ_hbm, occ_ref), (count_hbm, count_ref),
    )
    copies = [pltpu.make_async_copy(source, target, sems.at[n]) for n, (source, target) in enumerate(pairs)]
    for copy in copies:
        copy.start()
    chunk[...] = jnp.zeros_like(chunk)
    lane = lax.broadcasted_iota(jnp.int32, (1, TILE), 1)
    for copy in copies:
        copy.wait()
    for w in range(2):
        live = (lane < occ_ref[w]).astype(F32)
        lanes = slice(w * TILE, (w + 1) * TILE)
        base = 8 + w * 8
        chunk[base : base + 3, :] = pos_ref[:, lanes]
        chunk[base + 3 : base + 4, :] = pol_ref[:, lanes]
        chunk[base + 4 : base + 7, :] = dip_ref[:, lanes] * live
        chunk[base + 7 : base + 8, :] = live
        chunk[24 + w * 3 : 27 + w * 3, :] = perm_ref[:, lanes]
    plane = own_place()[1]
    box = boxes_ref[...]
    within = box & 1
    layer = (box >> 1) & (OWNERS - 1)
    group = box >> 7
    step = (layer >> 2) - plane
    stack = jnp.where(step == 0, 0, jnp.where(step < 0, 1, 2))
    place = within * 96 + stack * 32 + (group & 1) * PLANE + (group >> 1) * NX + (layer & 3)
    place = place.astype(F32)
    kind = class_ref[...].astype(F32)
    entry = lax.broadcasted_iota(jnp.int32, (1, ILIST), 1)
    for w in range(2):
        weight = scale_ref[w : w + 1, :] * (entry < count_ref[w]).astype(F32)
        for n, row in enumerate((place[w : w + 1, :], kind[w : w + 1, :], weight)):
            chunk[30 + w * 3 + n : 31 + w * 3 + n, :] = row[:, :TILE]
            chunk[36 + n : 37 + n, w * 64 : w * 64 + ILIST - TILE] = row[:, TILE:]
    def both(row):
        two = chunk[pl.ds(8 + row, 2, stride=8), :]
        return jnp.concatenate([two, two, two, two], axis=0)

    write_monomials(mono, both(0), both(1), both(2))
    for w in range(2):
        terms = mono[pl.ds(w, NTERM, stride=8), :]
        moment = dot_three(chunk[12 + w * 8 : 15 + w * 8, :], terms, NT)
        for c in range(3):
            chunk[c * 2 + w : c * 2 + w + 1, :] = moment[c : c + 1, :TILE]
            chunk[6 + w : 7 + w, c * REST : (c + 1) * REST] = moment[c : c + 1, TILE:]
    whole = chunk[...]
    for m in range(PLANE):
        out_ref[m, :, :] = whole


def write_fields(rows_ref, number, px, py, pz, root, first_layer):
    box = lax.broadcasted_iota(jnp.int32, (number, TILE), 0)
    rows_ref[pl.ds(0, number, stride=8), :] = HALF * (px + 2.0 * (box & 1).astype(F32))
    rows_ref[pl.ds(1, number, stride=8), :] = HALF * py
    rows_ref[pl.ds(2, number, stride=8), :] = HALF * (pz + 2.0 * ((box >> 1) + first_layer).astype(F32))
    rows_ref[pl.ds(3, number, stride=8), :] = root


def root_of(pol):
    return jnp.where(pol > 0.0, ROOT_THOLE * lax.rsqrt(jnp.where(pol > 0.0, pol, 1.0)), 0.0)


def scalars(delta, roots):
    dx, dy, dz = delta
    squared = dx * dx + dy * dy + (dz * dz + 1.0)
    inverse = lax.rsqrt(squared)
    inv_two = inverse * inverse
    inv_three = inverse * inv_two
    minus = (squared * (squared * inverse)) * roots
    damping = jnp.exp(minus)
    lambda_three = 1.0 - damping
    lambda_five = lambda_three + minus * damping
    return (3.0 * lambda_five) * (inv_three * inv_two), lambda_three * inv_three


def field_of(delta, radial, direct, moment):
    along = radial * (delta[0] * moment[0] + delta[1] * moment[1] + delta[2] * moment[2])
    return [delta[c] * along - direct * moment[c] for c in range(3)]


def added(parts):
    while len(parts) > 1:
        parts = [parts[i] + parts[i + 1] if i + 1 < len(parts) else parts[i] for i in range(0, len(parts), 2)]
    return parts[0]


def row(ref, at):
    return ref[pl.ds(at, 8, stride=0), :]


def tile_at(n, base=0):
    return pl.ds(pl.multiple_of(base + n * 8, 8), 8)


def trips_of(live):
    count = jnp.sum(live, axis=1, keepdims=True)
    return ((count + 7.0) * 0.125).astype(jnp.int32)


def spread(wide_ref, cols, boxes, fields):
    for slot, box in enumerate(boxes):
        for f in fields:
            at = box * 8 + f
            value = jnp.broadcast_to(cols[:, at : at + 1], (TILE, TILE))
            wide_ref[f, slot * TILE : (slot + 1) * TILE, :] = -value if f == 3 else value


def near_boxes(total_ref, slots, wide_ref, targets, trips, rows_ref, sources, keep_ref, first_kept):
    half = keep_ref.shape[0] // 2

    def body(n, carry):
        mine = [[wide_ref[f, tile_at(n, target * TILE), :] for f in range(4)] for target in targets]
        parts = [[] for _ in targets]
        for k, box in enumerate(sources):
            where = [row(rows_ref, box * 8 + f) for f in range(7)]
            for i, spot in enumerate(mine):
                delta = [spot[c] - where[c] for c in range(3)]
                radial, direct = scalars(delta, spot[3] * where[3])
                kept = tile_at(n, slots[i] * TILE)
                keep_ref[first_kept + k, kept, :] = radial
                keep_ref[half + first_kept + k, kept, :] = direct
                parts[i].append(field_of(delta, radial, direct, where[4:7]))
        for i, slot in enumerate(slots):
            for c in range(3):
                total_ref[c, tile_at(n, slot * TILE), :] = added([part[c] for part in parts[i]])
        return carry

    lax.fori_loop(0, trips, body, 0)


def lane_sums(total_ref, c, slot):
    return jnp.sum(jnp.transpose(total_ref[c, slot * TILE : (slot + 1) * TILE, :]), axis=0, keepdims=True)


def self_term(root):
    return 1.0 - jnp.exp(-(root * root))


def prepare_kernel(trans_ref, high_ref, low_ref):
    high_ref[...] = jnp.zeros_like(high_ref)
    low_ref[...] = jnp.zeros_like(low_ref)
    for o in range(CLASSES):
        high, low = halves(jnp.transpose(trans_ref[:, o, :]))
        high_ref[o * 256 : o * 256 + NTERM, :] = high
        low_ref[o * 256 : o * 256 + NTERM, :] = low


def second_kernel(block_ref, sel_ref, near_ref, wide, m_high_ref, m_low_ref, keep, rows, total, mono):
    mine = own_place()[3]
    rows[...] = jnp.zeros_like(rows)
    for x in range(NX):
        rows[x * 16 : x * 16 + 16, :] = block_ref[mine + x, 8:24, :]

    def field(f):
        return rows[pl.ds(f, 8, stride=8), :]

    px, py, pz, root = field(0), field(1), field(2), root_of(field(3))
    trips = trips_of(field(7))
    write_monomials(mono, px, py, pz)
    write_fields(rows, 8, px, py, pz, root, 0)
    spread(wide, jnp.transpose(rows[...]), range(8), range(4))
    for k in range(8):
        high, low = halves(mono[pl.ds(k, NTERM, stride=8), :])
        m_high_ref[k * 176 : k * 176 + NTERM, :] = high
        m_low_ref[k * 176 : k * 176 + NTERM, :] = low
    for box in range(8):
        low, high = max(box // 2 - 1, 0), min(box // 2 + 1, NX - 1)
        sources = range(low * 2, high * 2 + 2)
        near_boxes(total, [box], wide, [box], trips[box, 0], rows, sources, keep, low * 2 - (box // 2 - 1) * 2)
    spot = lax.broadcasted_iota(jnp.int32, (192, TILE), 0)
    kinds = lax.broadcasted_iota(jnp.int32, (CLASSES, TILE), 0)
    side = lax.broadcasted_iota(jnp.int32, (CLASSES, TILE), 1) >> 6
    for x in range(NX):
        got = jnp.zeros((32, 192), F32)
        first, second = [], []
        for w in range(2):
            at = 30 + w * 3
            place = block_ref[mine + x, at : at + 1, :].astype(jnp.int32)
            kind = block_ref[mine + x, at + 1 : at + 2, :].astype(jnp.int32)
            weight = jnp.where(kinds == kind, block_ref[mine + x, at + 2 : at + 3, :], 0.0)
            chosen = jnp.where(spot == place, 1.0, 0.0).astype(BF16)
            high = weight.astype(BF16).astype(F32)
            first.append(dot(jnp.concatenate([high, weight - high], axis=0).astype(BF16), chosen, NT))
        place = block_ref[mine + x, 36:37, :].astype(jnp.int32)
        kind = block_ref[mine + x, 37:38, :].astype(jnp.int32)
        weight = jnp.where(kinds == kind, block_ref[mine + x, 38:39, :], 0.0)
        high = weight.astype(BF16).astype(F32)
        low = weight - high
        both = [jnp.where(side == w, part, 0.0) for w in range(2) for part in (high, low)]
        chosen = jnp.where(spot == place, 1.0, 0.0).astype(BF16)
        second = dot(jnp.concatenate(both, axis=0).astype(BF16), chosen, NT)
        for w in range(2):
            k = x * 2 + w
            tail = second[w * 16 : w * 16 + 16]
            sel_ref[k * 8 : k * 8 + 8, :] = (first[w][0:8] + tail[0:8]) + (first[w][8:16] + tail[8:16])
    for c in range(3):
        for box in range(8):
            near_ref[c * 8 + box : c * 8 + box + 1, :] = lane_sums(total, c, box)


def third_kernel(
    block_ref, own_ref, sides_ref, sel_ref, near_ref, wide_ref, m_high_ref, m_low_ref, t_high_ref, t_low_ref,
    res_ref, send_ref, keep, summed, head, rest, far, rows, total,
):
    core, _, x_me, mine = own_place()
    sel_high, sel_low = halves(sel_ref[...])
    both = jnp.concatenate([sel_high, sel_low], axis=0)
    for kind in range(4):
        pieces = []
        for w in range(2):
            pieces += [own_ref[pl.ds(at + kind * 2 + w, 16, stride=8), :] for at in (0, OWN_ROWS)]
            pieces += [sides_ref[pl.ds(at + kind * 2 + w, 32, stride=8), :] for at in (0, SIDE_ROWS)]
        high, low = halves(jnp.concatenate(pieces, axis=0))
        got = dot(both, high, NN)
        summed[kind * 64 : kind * 64 + 64, :] = got[0:64] + (got[64:128] + dot(sel_high, low, NN))
    parts = []
    for c in range(3):
        pieces = []
        for o in range(CLASSES):
            pieces.append(summed[pl.ds(c * 64 + o, 8, stride=8), :])
            tail = summed[pl.ds(192 + o, 8, stride=8), :][:, c * REST : (c + 1) * REST]
            pieces.append(jnp.concatenate([tail, jnp.zeros((8, TILE - REST), F32)], axis=1))
        parts.append(jnp.concatenate(pieces, axis=1))
    parts.append(jnp.zeros((8, CLASSES * 256), F32))
    high, low = halves(jnp.concatenate(parts, axis=0))
    got = dot(jnp.concatenate([high, low], axis=0), t_high_ref[...], NN)
    moved = got[0:24] + (got[32:56] + dot(high, t_low_ref[...], NN)[0:24])
    moved_high = moved.astype(BF16).astype(F32)
    for n, part in enumerate((moved_high, moved - moved_high)):
        head[n * 24 : n * 24 + 24, :] = part[:, 0:TILE]
        rest[n * 24 : n * 24 + 24, 0:REST] = part[:, TILE:]
    rows[...] = jnp.zeros_like(rows)
    rows[0:16, :] = sides_ref[pl.ds(pl.multiple_of(272 + 32 * core, 8), 16), :]
    for x in range(NX):
        rows[16 + x * 16 : 32 + x * 16, :] = block_ref[mine + x, 8:24, :]
    rows[80:96, :] = sides_ref[pl.ds(pl.multiple_of(SIDE_ROWS + 256 + 32 * core, 8), 16), :]

    def field(f):
        return rows[pl.ds(f, 12, stride=8), :]

    px, py, pz, pol = field(0), field(1), field(2), field(3)
    live = rows[pl.ds(16 + 7, 8, stride=8), :]
    source = [rows[pl.ds(16 + 4 + c, 8, stride=8), :] for c in range(3)]
    root = root_of(pol)
    trips = trips_of(live)
    write_fields(rows, 12, px, py, pz, root, -1)
    for slots, boxes, sources in (((0, 1), (0, 1), (0, 1)), ((2, 3), (6, 7), (10, 11))):
        most = jnp.maximum(trips[boxes[0], 0], trips[boxes[1], 0])
        near_boxes(total, slots, wide_ref, boxes, most, rows, sources, keep, 0)
    for k in range(8):
        left = jnp.concatenate([head[pl.ds(k, 6, stride=8), :], rest[pl.ds(k, 6, stride=8), :][:, 0:REST]], axis=1)
        left = left.astype(BF16)
        with_high = dot(left, m_high_ref[k * 176 : k * 176 + NTERM, :], NN)
        with_low = dot(left, m_low_ref[k * 176 : k * 176 + NTERM, :], NN)
        value = with_high[0:3] + (with_high[3:6] + with_low[0:3])
        for c in range(3):
            far[c * 8 + k : c * 8 + k + 1, :] = value[c : c + 1]
    alone = self_term(root[2:10])
    nothing = jnp.zeros((4, TILE), F32)
    for c in range(3):
        perm = jnp.concatenate(
            [block_ref[mine + x, 24 + w * 3 + c : 25 + w * 3 + c, :] for x in range(NX) for w in range(2)], axis=0
        )
        ends = [lane_sums(total, c, slot) for slot in range(4)]
        edge = jnp.concatenate(ends[0:2] + [nothing] + ends[2:4], axis=0)
        near_zero = near_ref[c * 8 : c * 8 + 8, :] + edge + alone * source[c]
        res_ref[c * 8 : c * 8 + 8, :] = jnp.where(
            live > 0.0, perm + far[c * 8 : c * 8 + 8, :] + near_zero - source[c] / pol[2:10], 0.0
        )
    first = jnp.where(x_me < 2, 4, 0)
    for c in range(3):
        for k in range(4):
            send_ref[c * 4 + k : c * 4 + k + 1, :] = res_ref[pl.ds(c * 8 + first + k, 1), :]


def window_kernel(block_ref, sides_ref, rows, keep, edge, every):
    core, _, x_me, mine = own_place()
    first = x_me * 2
    every[0:32, :] = sides_ref[pl.ds(pl.multiple_of(256 + 32 * core, 8), 32), :]
    for x in range(NX):
        every[32 + x * 16 : 48 + x * 16, :] = block_ref[mine + x, 8:24, :]
    every[96:128, :] = sides_ref[pl.ds(pl.multiple_of(SIDE_ROWS + 256 + 32 * core, 8), 32), :]
    rows[...] = jnp.zeros_like(rows)
    for k in range(10):
        rows[k * 8 : k * 8 + 8, :] = every[pl.ds(pl.multiple_of((first + k) * 8, 8), 8), :]

    def field(f):
        return rows[pl.ds(f, 10, stride=8), :]

    px, py, pz, pol, live = field(0), field(1), field(2), field(3), field(7)
    root = root_of(pol)
    rows[80:90, :] = pol
    rows[96:106, :] = self_term(root)
    trips = trips_of(live)
    write_fields(rows, 10, px, py, pz, root, x_me - 2)
    for outside, layer in ((x_me == 0, 1), (x_me == NX - 1, 3)):

        @pl.when(outside)
        def _():
            cols = jnp.transpose(rows[...])
            spread(edge, cols, (layer * 2, layer * 2 + 1), range(4))
            for w in range(2):

                def body(n, carry):
                    for u in range(2):
                        at = tile_at(n * 2 + u, w * TILE)
                        spot = [edge[f, at, :] for f in range(4)]
                        for k in range(6):
                            source = (layer - 1) * 2 + k
                            delta = [spot[c] - row(rows, source * 8 + c) for c in range(3)]
                            radial, direct = scalars(delta, spot[3] * row(rows, source * 8 + 3))
                            keep[k, at, :] = radial
                            keep[6 + k, at, :] = direct
                    return carry

                lax.fori_loop(0, (trips[layer * 2 + w, 0] + 1) // 2, body, 0)


def fourth_kernel(
    rows_ref, plane_keep, edge_keep, out_keep, plane_wide, out_wide, res_ref, got_ref, new_ref, out_ref,
    moved, rows, total, two_ref,
):
    x_me = own_place()[2]
    first = x_me * 2
    for c in range(3):
        got = got_ref[c * 4 : c * 4 + 4, :]
        moved[c, 0:4, :] = got
        moved[c, 4:12, :] = res_ref[c * 8 : c * 8 + 8, :]
        moved[c, 12:16, :] = got
    rows[...] = rows_ref[...]
    pol, alone = rows[80:90, :], rows[96:106, :]
    live = rows[pl.ds(7, 10, stride=8), :]
    trips = trips_of(live)
    source = [rows[pl.ds(32 + 4 + c, 2, stride=8), :] for c in range(3)]
    residual = [jnp.concatenate([moved[c, pl.ds(first + k, 1), :] for k in range(10)], axis=0) for c in range(3)]

    def tiles(box, x):
        layer, w = x + box // 2 - 2, box % 2
        inside = 0 <= layer < NX
        spot_ref = plane_wide if inside else out_wide
        base = (layer * 2 + w if inside else w) * TILE

        def scalar(k, part, n):
            if not inside:
                return out_keep[part * 6 + k, tile_at(n, base), :]
            if layer == 0 and k < 2:
                return edge_keep[part * 2 + k, tile_at(n, w * TILE), :]
            if layer == NX - 1 and k >= 4:
                return edge_keep[part * 2 + k - 4, tile_at(n, (2 + w) * TILE), :]
            return plane_keep[part * 6 + k, tile_at(n, base), :]

        def body(n, carry):
            for u in range(2):
                tile = n * 2 + u
                spot = [spot_ref[c, tile_at(tile, base), :] for c in range(3)]
                parts = []
                for k in range(6):
                    near = (box // 2 - 1) * 2 + k
                    delta = [spot[c] - row(rows, near * 8 + c) for c in range(3)]
                    moment = [row(rows, near * 8 + 4 + c) for c in range(3)]
                    parts.append(field_of(delta, scalar(k, 0, tile), scalar(k, 1, tile), moment))
                for c in range(3):
                    total[c, tile_at(tile, (box - 2) * TILE), :] = added([part[c] for part in parts])
            return carry

        lax.fori_loop(0, (trips[box, 0] + 1) // 2, body, 0)

    def sweep(boxes, moments):
        for c in range(3):
            rows[pl.ds(4 + c, 10, stride=8), :] = moments[c]
        for x in range(NX):

            @pl.when(x_me == x)
            def _():
                for box in boxes:
                    tiles(box, x)

        return [jnp.concatenate([lane_sums(total, c, box - 2) for box in boxes], axis=0) for c in range(3)]

    one = [pol * residual[c] for c in range(3)]
    fields = sweep(range(2, 8), one)
    two = []
    edge = jnp.zeros((2, TILE), F32)
    for c in range(3):
        value = pol[2:8] * (residual[c][2:8] + fields[c] + alone[2:8] * one[c][2:8])
        two.append(jnp.concatenate([edge, jnp.where(live[2:8] > 0.0, value, 0.0), edge], axis=0))
        two_ref[c, 0:10, :] = two[c]
    fields = sweep(range(4, 6), two)
    for c in range(3):
        value = pol[4:6] * (residual[c][4:6] + fields[c] + alone[4:6] * two_ref[c, 4:6, :])
        three = source[c] + jnp.where(live[4:6] > 0.0, value, 0.0)
        for w in range(2):
            new_ref[c : c + 1, w * TILE : (w + 1) * TILE] = three[w : w + 1]
            out_ref[c : c + 1, w * TILE : (w + 1) * TILE] = residual[c][4 + w : 5 + w]


VMEM = pl.BlockSpec(memory_space=pltpu.VMEM)
HBM = pl.BlockSpec(memory_space=pltpu.HBM)


def shape_of(shape):
    return shape if isinstance(shape, jax.ShapeDtypeStruct) else jax.ShapeDtypeStruct(shape, F32)


def call(body, ins, outs, scratch, cost, limit, name):
    return pl.pallas_call(
        body,
        in_specs=ins,
        out_specs=[VMEM] * len(outs),
        out_shape=[shape_of(shape) for shape in outs],
        scratch_shapes=[pltpu.VMEM(shape, F32) if isinstance(shape, tuple) else shape for shape in scratch],
        cost_estimate=pl.CostEstimate(flops=cost, bytes_accessed=1 << 20, transcendentals=0),
        compiler_params=pltpu.CompilerParams(vmem_limit_bytes=limit << 20),
        name=name,
    )


def device(group, box):
    return group * OWNERS + box


def rounds():
    plane = [
        [device(2 * y + core, z * NX + x) for y in range(NY) for x in range(NX)]
        for core in range(2)
        for z in range(OWNERS // NX)
    ]
    chip = [[device(2 * y, b), device(2 * y + 1, b)] for y in range(NY) for b in range(OWNERS)]
    up = [[(device(g, b), device(g, b + NX)) for b in range(OWNERS - NX)] for g in range(GROUPS)]
    down = [[(target, source) for source, target in pairs] for pairs in up]
    apart = [pair for g in range(GROUPS) for pair in (down[g] if g % 2 else up[g])]
    near_side = [(s, t) for pairs in up for s, t in pairs if s % NX < 2]
    near_side += [(s, t) for pairs in down for s, t in pairs if s % NX >= 2]
    return plane, chip, apart, near_side


PLANE_SETS, CHIP_SETS, APART, NEAR_SIDE = rounds()
OWN_ROWS = PLANE * 8 + 64
SIDE_ROWS = 256 + 64


def on_device(
    dipoles, perm_field, positions, polarizability, occupancy, far_boxes, far_class, far_count, far_scale, translations
):
    me = lax.axis_index("d").astype(jnp.int32)
    two = pltpu.SMEM((2,), jnp.int32)
    lists = pltpu.VMEM((2, ILIST), jnp.int32)
    [chunk] = call(
        first_kernel,
        [HBM] * 9,
        [(PLANE, CHUNK, TILE)],
        [(NTERM * 8, TILE), (CHUNK, TILE)]
        + [(3, 2 * TILE)] * 3
        + [(1, 2 * TILE), (2, ILIST), lists, lists, two, two, pltpu.SemaphoreType.DMA((9,))],
        1 << 20,
        60,
        "first",
    )(
        occupancy, far_count, dipoles, perm_field, positions, polarizability.reshape(1, 2 * TILE),
        far_boxes, far_class, far_scale,
    )
    block = lax.all_to_all(chunk, "d", 0, 0, axis_index_groups=PLANE_SETS, tiled=True)
    half = jax.ShapeDtypeStruct((CLASSES * 256, NTERM), BF16)
    t_high, t_low = call(prepare_kernel, [VMEM], [half, half], [], 1 << 28, 12, "prepare")(
        jnp.transpose(translations, (1, 0, 2))
    )
    mine = (me // (2 * OWNERS)) * NX
    core = (me // OWNERS) & 1
    near = lax.dynamic_slice(block, (mine, 8, 0), (NX, 16, TILE)).reshape(64, TILE)
    part = jnp.concatenate([block[:, 0:8, :].reshape(PLANE * 8, TILE), near], axis=0)
    part, t_high, t_low = lax.optimization_barrier((part, t_high, t_low))
    own = lax.all_gather(part, "d", axis_index_groups=CHIP_SETS, axis=0)
    edges = lax.dynamic_slice(own, (0, PLANE * 8 + 32 * (1 - core), 0), (2, 32, TILE)).reshape(64, TILE)
    away = jnp.concatenate([own[:, 0 : PLANE * 8].reshape(256, TILE), edges], axis=0)
    came = lax.ppermute(away, "d", APART)
    own = own.reshape(2 * OWN_ROWS, TILE)
    half = jax.ShapeDtypeStruct((8 * 176, TILE), BF16)
    sel, near_zero, wide, m_high, m_low, plane_keep = call(
        second_kernel,
        [VMEM],
        [(64, 192), (24, TILE), (4, 8 * TILE, TILE), half, half, (12, 8 * TILE, TILE)],
        [(TILE, TILE), (3, 8 * TILE, TILE), (NTERM * 8, TILE)],
        1 << 28,
        20,
        "second",
    )(block)
    came, sel = lax.optimization_barrier((came, sel))
    sides = lax.all_gather(came, "d", axis_index_groups=CHIP_SETS, axis=0).reshape(2 * SIDE_ROWS, TILE)
    residual, send, edge_keep = call(
        third_kernel,
        [VMEM] * 10,
        [(24, TILE), (12, TILE), (4, 4 * TILE, TILE)],
        [(256, TILE), (48, TILE), (48, TILE), (24, TILE), (TILE, TILE), (3, 4 * TILE, TILE)],
        1 << 28,
        16,
        "third",
    )(block, own, sides, sel, near_zero, wide, m_high, m_low, t_high, t_low)
    got = lax.ppermute(send, "d", NEAR_SIDE)
    rows, out_keep, out_wide = call(
        window_kernel,
        [VMEM] * 2,
        [(TILE, TILE), (12, 2 * TILE, TILE), (4, 2 * TILE, TILE)],
        [(TILE, TILE)],
        1 << 28,
        12,
        "window",
    )(block, sides)
    new, out = call(
        fourth_kernel,
        [VMEM] * 8,
        [(3, 2 * TILE), (3, 2 * TILE)],
        [(3, 16, TILE), (TILE, TILE), (3, 6 * TILE, TILE), (3, 16, TILE)],
        1 << 28,
        20,
        "fourth",
    )(rows, plane_keep, edge_keep, out_keep, wide, out_wide, residual, got)
    return new, out


def solution(mesh):
    flat = Mesh(mesh.devices.reshape(-1), ("d",))
    return jax.shard_map(
        on_device,
        mesh=flat,
        in_specs=(
            P(None, "d"), P(None, "d"), P(None, "d"), P("d"), P("d"), P("d", None), P("d", None), P("d"), P("d", None), P(),
        ),
        out_specs=(P(None, "d"), P(None, "d")),
        check_vma=False,
    )
```

```python
import jax
import jax.numpy as jnp
from jax import lax
from jax.experimental import pallas as pl
from jax.experimental.pallas import tpu as pltpu
from jax.sharding import Mesh
from jax.sharding import PartitionSpec as P

TILE = 128
ORDER = 8
NTERM = 165
REST = NTERM - TILE
ILIST = 189
CLASSES = 8
GROUPS = 8
OWNERS = 64
NX = 4
NY = 4
PLANE = NX * NY
CHUNK = 40
F32 = jnp.float32
BF16 = jnp.bfloat16

HALF = 5.4
ROOT_THOLE = 0.39**0.5
NT = (((1,), (1,)), ((), ()))
NN = (((1,), (0,)), ((), ()))


def term_table():
    listing = []
    for degree in range(ORDER + 1):
        for first in range(degree + 1):
            for second in range(degree + 1 - first):
                listing.append((first, second, degree - first - second))
    return listing


TERMS = term_table()


def dot(a, b, dims):
    return lax.dot_general(a, b, dims, preferred_element_type=F32)


def halves(x):
    high = x.astype(BF16)
    return high, (x - high.astype(F32)).astype(BF16)


def dot_three(a, b, dims):
    a_high, a_low = halves(a)
    b_high, b_low = halves(b)
    return dot(a_high, b_high, dims) + (dot(a_high, b_low, dims) + dot(a_low, b_high, dims))


def chebyshev(coord):
    series = [None, coord]
    doubled = 2.0 * coord
    series.append(doubled * coord - 1.0)
    for _ in range(3, ORDER + 1):
        series.append(doubled * series[-1] - series[-2])
    return series


def write_monomials(ref, px, py, pz):
    cx, cy, cz = chebyshev(px), chebyshev(py), chebyshev(pz)
    cross = {}
    for t, (i, j, k) in enumerate(TERMS):
        if (i, j) not in cross:
            if i and j:
                cross[i, j] = cx[i] * cy[j]
            else:
                cross[i, j] = cx[i] if i else cy[j]
        head = cross[i, j]
        if head is None:
            value = jnp.ones_like(px) if k == 0 else cz[k]
        else:
            value = head if k == 0 else head * cz[k]
        ref[t * 8 : t * 8 + 8, :] = value


def own_place():
    me = lax.axis_index("d")
    return (me // OWNERS) & 1, (me // NX) & (OWNERS // NX - 1), me & (NX - 1), (me // (2 * OWNERS)) * NX


def first_kernel(
    occ_hbm, count_hbm, dip_hbm, perm_hbm, pos_hbm, pol_hbm, boxes_hbm, class_hbm, scale_hbm, out_ref,
    mono, chunk, dip_ref, perm_ref, pos_ref, pol_ref, scale_ref, boxes_ref, class_ref, occ_ref, count_ref, sems,
):
    pairs = (
        (pos_hbm, pos_ref), (dip_hbm, dip_ref), (pol_hbm, pol_ref), (perm_hbm, perm_ref),
        (boxes_hbm, boxes_ref), (class_hbm, class_ref), (scale_hbm, scale_ref), (occ_hbm, occ_ref), (count_hbm, count_ref),
    )
    copies = [pltpu.make_async_copy(source, target, sems.at[n]) for n, (source, target) in enumerate(pairs)]
    for copy in copies:
        copy.start()
    chunk[...] = jnp.zeros_like(chunk)
    lane = lax.broadcasted_iota(jnp.int32, (1, TILE), 1)
    for copy in copies:
        copy.wait()
    for w in range(2):
        live = (lane < occ_ref[w]).astype(F32)
        lanes = slice(w * TILE, (w + 1) * TILE)
        base = 8 + w * 8
        chunk[base : base + 3, :] = pos_ref[:, lanes]
        chunk[base + 3 : base + 4, :] = pol_ref[:, lanes]
        chunk[base + 4 : base + 7, :] = dip_ref[:, lanes] * live
        chunk[base + 7 : base + 8, :] = live
        chunk[24 + w * 3 : 27 + w * 3, :] = perm_ref[:, lanes]
    plane = own_place()[1]
    box = boxes_ref[...]
    within = box & 1
    layer = (box >> 1) & (OWNERS - 1)
    group = box >> 7
    step = (layer >> 2) - plane
    stack = jnp.where(step == 0, 0, jnp.where(step < 0, 1, 2))
    place = within * 96 + stack * 32 + (group & 1) * PLANE + (group >> 1) * NX + (layer & 3)
    place = place.astype(F32)
    kind = class_ref[...].astype(F32)
    entry = lax.broadcasted_iota(jnp.int32, (1, ILIST), 1)
    for w in range(2):
        weight = scale_ref[w : w + 1, :] * (entry < count_ref[w]).astype(F32)
        for n, row in enumerate((place[w : w + 1, :], kind[w : w + 1, :], weight)):
            chunk[30 + w * 3 + n : 31 + w * 3 + n, :] = row[:, :TILE]
            chunk[36 + n : 37 + n, w * 64 : w * 64 + ILIST - TILE] = row[:, TILE:]
    def both(row):
        two = chunk[pl.ds(8 + row, 2, stride=8), :]
        return jnp.concatenate([two, two, two, two], axis=0)

    write_monomials(mono, both(0), both(1), both(2))
    for w in range(2):
        terms = mono[pl.ds(w, NTERM, stride=8), :]
        moment = dot_three(chunk[12 + w * 8 : 15 + w * 8, :], terms, NT)
        for c in range(3):
            chunk[c * 2 + w : c * 2 + w + 1, :] = moment[c : c + 1, :TILE]
            chunk[6 + w : 7 + w, c * REST : (c + 1) * REST] = moment[c : c + 1, TILE:]
    whole = chunk[...]
    for m in range(PLANE):
        out_ref[m, :, :] = whole


def write_fields(rows_ref, number, px, py, pz, root, first_layer):
    box = lax.broadcasted_iota(jnp.int32, (number, TILE), 0)
    rows_ref[pl.ds(0, number, stride=8), :] = HALF * (px + 2.0 * (box & 1).astype(F32))
    rows_ref[pl.ds(1, number, stride=8), :] = HALF * py
    rows_ref[pl.ds(2, number, stride=8), :] = HALF * (pz + 2.0 * ((box >> 1) + first_layer).astype(F32))
    rows_ref[pl.ds(3, number, stride=8), :] = root


def root_of(pol):
    return jnp.where(pol > 0.0, ROOT_THOLE * lax.rsqrt(jnp.where(pol > 0.0, pol, 1.0)), 0.0)


def scalars(delta, roots):
    dx, dy, dz = delta
    squared = dx * dx + dy * dy + (dz * dz + 1.0)
    inverse = lax.rsqrt(squared)
    inv_two = inverse * inverse
    inv_three = inverse * inv_two
    minus = (squared * (squared * inverse)) * roots
    damping = jnp.exp(minus)
    lambda_three = 1.0 - damping
    lambda_five = lambda_three + minus * damping
    return (3.0 * lambda_five) * (inv_three * inv_two), lambda_three * inv_three


def field_of(delta, radial, direct, moment):
    along = radial * (delta[0] * moment[0] + delta[1] * moment[1] + delta[2] * moment[2])
    return [delta[c] * along - direct * moment[c] for c in range(3)]


def added(parts):
    while len(parts) > 1:
        parts = [parts[i] + parts[i + 1] if i + 1 < len(parts) else parts[i] for i in range(0, len(parts), 2)]
    return parts[0]


def row(ref, at):
    return ref[pl.ds(at, 8, stride=0), :]


def tile_at(n, base=0):
    return pl.ds(pl.multiple_of(base + n * 8, 8), 8)


def trips_of(live):
    count = jnp.sum(live, axis=1, keepdims=True)
    return ((count + 7.0) * 0.125).astype(jnp.int32)


def spread(wide_ref, cols, boxes, fields):
    for slot, box in enumerate(boxes):
        for f in fields:
            at = box * 8 + f
            value = jnp.broadcast_to(cols[:, at : at + 1], (TILE, TILE))
            wide_ref[f, slot * TILE : (slot + 1) * TILE, :] = -value if f == 3 else value


def near_boxes(total_ref, slots, wide_ref, targets, trips, rows_ref, sources, keep_ref):
    def body(n, carry):
        mine = [[wide_ref[f, tile_at(n, target * TILE), :] for f in range(4)] for target in targets]
        parts = [[] for _ in targets]
        for k, box in enumerate(sources):
            where = [row(rows_ref, box * 8 + f) for f in range(7)]
            for i, spot in enumerate(mine):
                delta = [spot[c] - where[c] for c in range(3)]
                radial, direct = scalars(delta, spot[3] * where[3])
                if keep_ref is not None:
                    kept = tile_at(n, slots[i] * TILE)
                    keep_ref[k, kept, :] = radial
                    keep_ref[6 + k, kept, :] = direct
                parts[i].append(field_of(delta, radial, direct, where[4:7]))
        for i, slot in enumerate(slots):
            for c in range(3):
                total_ref[c, tile_at(n, slot * TILE), :] = added([part[c] for part in parts[i]])
        return carry

    lax.fori_loop(0, trips, body, 0)


def lane_sums(total_ref, c, slot):
    return jnp.sum(jnp.transpose(total_ref[c, slot * TILE : (slot + 1) * TILE, :]), axis=0, keepdims=True)


def self_term(root):
    return 1.0 - jnp.exp(-(root * root))


def prepare_kernel(trans_ref, high_ref, low_ref):
    high_ref[...] = jnp.zeros_like(high_ref)
    low_ref[...] = jnp.zeros_like(low_ref)
    for o in range(CLASSES):
        high, low = halves(jnp.transpose(trans_ref[:, o, :]))
        high_ref[o * 256 : o * 256 + NTERM, :] = high
        low_ref[o * 256 : o * 256 + NTERM, :] = low


def second_kernel(block_ref, sel_ref, near_ref, wide, m_high_ref, m_low_ref, keep, rows, total, mono):
    mine = own_place()[3]
    rows[...] = jnp.zeros_like(rows)
    for x in range(NX):
        rows[x * 16 : x * 16 + 16, :] = block_ref[mine + x, 8:24, :]

    def field(f):
        return rows[pl.ds(f, 8, stride=8), :]

    px, py, pz, root = field(0), field(1), field(2), root_of(field(3))
    trips = trips_of(field(7))
    write_monomials(mono, px, py, pz)
    write_fields(rows, 8, px, py, pz, root, 0)
    spread(wide, jnp.transpose(rows[...]), range(8), range(4))
    for k in range(8):
        high, low = halves(mono[pl.ds(k, NTERM, stride=8), :])
        m_high_ref[k * 176 : k * 176 + NTERM, :] = high
        m_low_ref[k * 176 : k * 176 + NTERM, :] = low
    x_me = own_place()[2]
    near_ref[...] = jnp.zeros_like(near_ref)
    for box in range(2, 6):
        first = (box // 2 - 1) * 2
        near_boxes(total, [box - 2], wide, [box], trips[box, 0], rows, range(first, first + 6), keep)
    for sent, boxes, sources in ((x_me < 2, (6, 7), range(4, 8)), (x_me >= 2, (0, 1), range(4))):

        @pl.when(sent)
        def _():
            for w, box in enumerate(boxes):
                near_boxes(total, [4 + w], wide, [box], trips[box, 0], rows, sources, None)
            for c in range(3):
                for w, box in enumerate(boxes):
                    near_ref[c * 8 + box : c * 8 + box + 1, :] = lane_sums(total, c, 4 + w)

    spot = lax.broadcasted_iota(jnp.int32, (192, TILE), 0)
    kinds = lax.broadcasted_iota(jnp.int32, (CLASSES, TILE), 0)
    side = lax.broadcasted_iota(jnp.int32, (CLASSES, TILE), 1) >> 6
    for x in range(NX):
        got = jnp.zeros((32, 192), F32)
        first, second = [], []
        for w in range(2):
            at = 30 + w * 3
            place = block_ref[mine + x, at : at + 1, :].astype(jnp.int32)
            kind = block_ref[mine + x, at + 1 : at + 2, :].astype(jnp.int32)
            weight = jnp.where(kinds == kind, block_ref[mine + x, at + 2 : at + 3, :], 0.0)
            chosen = jnp.where(spot == place, 1.0, 0.0).astype(BF16)
            high = weight.astype(BF16).astype(F32)
            first.append(dot(jnp.concatenate([high, weight - high], axis=0).astype(BF16), chosen, NT))
        place = block_ref[mine + x, 36:37, :].astype(jnp.int32)
        kind = block_ref[mine + x, 37:38, :].astype(jnp.int32)
        weight = jnp.where(kinds == kind, block_ref[mine + x, 38:39, :], 0.0)
        high = weight.astype(BF16).astype(F32)
        low = weight - high
        both = [jnp.where(side == w, part, 0.0) for w in range(2) for part in (high, low)]
        chosen = jnp.where(spot == place, 1.0, 0.0).astype(BF16)
        second = dot(jnp.concatenate(both, axis=0).astype(BF16), chosen, NT)
        for w in range(2):
            k = x * 2 + w
            tail = second[w * 16 : w * 16 + 16]
            sel_ref[k * 8 : k * 8 + 8, :] = (first[w][0:8] + tail[0:8]) + (first[w][8:16] + tail[8:16])
    for c in range(3):
        for box in range(2, 6):
            near_ref[c * 8 + box : c * 8 + box + 1, :] = lane_sums(total, c, box - 2)


def third_kernel(
    block_ref, own_ref, sides_ref, sel_ref, near_ref, wide_ref, m_high_ref, m_low_ref, t_high_ref, t_low_ref,
    res_ref, send_ref, summed, head, rest, far, rows, total,
):
    core, _, x_me, mine = own_place()
    sel_high, sel_low = halves(sel_ref[...])
    both = jnp.concatenate([sel_high, sel_low], axis=0)
    for kind in range(4):
        pieces = []
        for w in range(2):
            pieces += [own_ref[pl.ds(at + kind * 2 + w, 16, stride=8), :] for at in (0, OWN_ROWS)]
            pieces += [sides_ref[pl.ds(at + kind * 2 + w, 32, stride=8), :] for at in (0, SIDE_ROWS)]
        high, low = halves(jnp.concatenate(pieces, axis=0))
        got = dot(both, high, NN)
        summed[kind * 64 : kind * 64 + 64, :] = got[0:64] + (got[64:128] + dot(sel_high, low, NN))
    parts = []
    for c in range(3):
        pieces = []
        for o in range(CLASSES):
            pieces.append(summed[pl.ds(c * 64 + o, 8, stride=8), :])
            tail = summed[pl.ds(192 + o, 8, stride=8), :][:, c * REST : (c + 1) * REST]
            pieces.append(jnp.concatenate([tail, jnp.zeros((8, TILE - REST), F32)], axis=1))
        parts.append(jnp.concatenate(pieces, axis=1))
    parts.append(jnp.zeros((8, CLASSES * 256), F32))
    high, low = halves(jnp.concatenate(parts, axis=0))
    got = dot(jnp.concatenate([high, low], axis=0), t_high_ref[...], NN)
    moved = got[0:24] + (got[32:56] + dot(high, t_low_ref[...], NN)[0:24])
    moved_high = moved.astype(BF16).astype(F32)
    for n, part in enumerate((moved_high, moved - moved_high)):
        head[n * 24 : n * 24 + 24, :] = part[:, 0:TILE]
        rest[n * 24 : n * 24 + 24, 0:REST] = part[:, TILE:]
    rows[...] = jnp.zeros_like(rows)
    rows[0:16, :] = sides_ref[pl.ds(pl.multiple_of(272 + 32 * core, 8), 16), :]
    for x in range(NX):
        rows[16 + x * 16 : 32 + x * 16, :] = block_ref[mine + x, 8:24, :]
    rows[80:96, :] = sides_ref[pl.ds(pl.multiple_of(SIDE_ROWS + 256 + 32 * core, 8), 16), :]

    def field(f):
        return rows[pl.ds(f, 12, stride=8), :]

    px, py, pz, pol = field(0), field(1), field(2), field(3)
    live = rows[pl.ds(16 + 7, 8, stride=8), :]
    source = [rows[pl.ds(16 + 4 + c, 8, stride=8), :] for c in range(3)]
    root = root_of(pol)
    trips = trips_of(live)
    write_fields(rows, 12, px, py, pz, root, -1)
    for sent, boxes, sources in ((x_me < 2, (6, 7), (10, 11)), (x_me >= 2, (0, 1), (0, 1))):

        @pl.when(sent)
        def _():
            most = jnp.maximum(trips[boxes[0], 0], trips[boxes[1], 0])
            near_boxes(total, (0, 1), wide_ref, boxes, most, rows, sources, None)

    for k in range(8):
        left = jnp.concatenate([head[pl.ds(k, 6, stride=8), :], rest[pl.ds(k, 6, stride=8), :][:, 0:REST]], axis=1)
        left = left.astype(BF16)
        with_high = dot(left, m_high_ref[k * 176 : k * 176 + NTERM, :], NN)
        with_low = dot(left, m_low_ref[k * 176 : k * 176 + NTERM, :], NN)
        value = with_high[0:3] + (with_high[3:6] + with_low[0:3])
        for c in range(3):
            far[c * 8 + k : c * 8 + k + 1, :] = value[c : c + 1]
    alone = self_term(root[2:10])
    nothing = jnp.zeros((6, TILE), F32)
    for c in range(3):
        perm = jnp.concatenate(
            [block_ref[mine + x, 24 + w * 3 + c : 25 + w * 3 + c, :] for x in range(NX) for w in range(2)], axis=0
        )
        ends = [lane_sums(total, c, slot) for slot in range(2)]
        edge = jnp.where(x_me < 2, jnp.concatenate([nothing] + ends, axis=0), jnp.concatenate(ends + [nothing], axis=0))
        near_zero = near_ref[c * 8 : c * 8 + 8, :] + edge + alone * source[c]
        res_ref[c * 8 : c * 8 + 8, :] = jnp.where(
            live > 0.0, perm + far[c * 8 : c * 8 + 8, :] + near_zero - source[c] / pol[2:10], 0.0
        )
    first = jnp.where(x_me < 2, 4, 0)
    for c in range(3):
        for k in range(4):
            send_ref[c * 4 + k : c * 4 + k + 1, :] = res_ref[pl.ds(c * 8 + first + k, 1), :]


def window_kernel(block_ref, sides_ref, wide_ref, rows, keep, edge, late_keep, late_ref, every, total):
    core, _, x_me, mine = own_place()
    first = x_me * 2
    every[0:32, :] = sides_ref[pl.ds(pl.multiple_of(256 + 32 * core, 8), 32), :]
    for x in range(NX):
        every[32 + x * 16 : 48 + x * 16, :] = block_ref[mine + x, 8:24, :]
    every[96:128, :] = sides_ref[pl.ds(pl.multiple_of(SIDE_ROWS + 256 + 32 * core, 8), 32), :]
    rows[...] = jnp.zeros_like(rows)
    for k in range(10):
        rows[k * 8 : k * 8 + 8, :] = every[pl.ds(pl.multiple_of((first + k) * 8, 8), 8), :]

    def field(f):
        return rows[pl.ds(f, 10, stride=8), :]

    px, py, pz, pol, live = field(0), field(1), field(2), field(3), field(7)
    root = root_of(pol)
    rows[80:90, :] = pol
    rows[96:106, :] = self_term(root)
    trips = trips_of(live)
    write_fields(rows, 10, px, py, pz, root, x_me - 2)
    for x, layer in enumerate((2, 1, 3, 2)):

        @pl.when(x_me == x)
        def _():
            plane_box = 0 if x < 2 else 6
            first_source = (layer - 1) * 2
            for w in range(2):
                sources = range(first_source, first_source + 6)
                many = trips[layer * 2 + w, 0]
                near_boxes(total, [w], wide_ref, [plane_box + w], many, rows, sources, late_keep)
            for w in range(2):
                alive = live[layer * 2 + w : layer * 2 + w + 1] > 0.0
                for c in range(3):
                    late_ref[c * 2 + w : c * 2 + w + 1, :] = jnp.where(alive, lane_sums(total, c, w), 0.0)

    for outside, layer in ((x_me == 0, 1), (x_me == NX - 1, 3)):

        @pl.when(outside)
        def _():
            cols = jnp.transpose(rows[...])
            spread(edge, cols, (layer * 2, layer * 2 + 1), range(4))
            for w in range(2):

                def body(n, carry):
                    for u in range(2):
                        at = tile_at(n * 2 + u, w * TILE)
                        spot = [edge[f, at, :] for f in range(4)]
                        for k in range(6):
                            source = (layer - 1) * 2 + k
                            delta = [spot[c] - row(rows, source * 8 + c) for c in range(3)]
                            radial, direct = scalars(delta, spot[3] * row(rows, source * 8 + 3))
                            keep[k, at, :] = radial
                            keep[6 + k, at, :] = direct
                    return carry

                lax.fori_loop(0, (trips[layer * 2 + w, 0] + 1) // 2, body, 0)


def fourth_kernel(
    rows_ref, plane_keep, late_keep, late_ref, out_keep, plane_wide, out_wide, res_ref, got_ref, new_ref, out_ref,
    moved, rows, total, two_ref,
):
    x_me = own_place()[2]
    first = x_me * 2
    for c in range(3):
        got = got_ref[c * 4 : c * 4 + 4, :]
        moved[c, 0:4, :] = got
        moved[c, 4:12, :] = res_ref[c * 8 : c * 8 + 8, :]
        moved[c, 12:16, :] = got
        for w in range(2):
            at = pl.ds(jnp.where(x_me < 2, 4, 10) + w, 1)
            moved[c, at, :] = moved[c, at, :] + late_ref[c * 2 + w : c * 2 + w + 1, :]
    rows[...] = rows_ref[...]
    pol, alone = rows[80:90, :], rows[96:106, :]
    live = rows[pl.ds(7, 10, stride=8), :]
    trips = trips_of(live)
    source = [rows[pl.ds(32 + 4 + c, 2, stride=8), :] for c in range(3)]
    residual = [jnp.concatenate([moved[c, pl.ds(first + k, 1), :] for k in range(10)], axis=0) for c in range(3)]

    def tiles(box, x):
        layer, w = x + box // 2 - 2, box % 2
        inside = 0 <= layer < NX
        spot_ref = plane_wide if inside else out_wide
        base = (layer * 2 + w if inside else w) * TILE

        def scalar(k, part, n):
            if not inside:
                return out_keep[part * 6 + k, tile_at(n, base), :]
            if layer == (0 if x < 2 else NX - 1):
                return late_keep[part * 6 + k, tile_at(n, w * TILE), :]
            return plane_keep[part * 6 + k, tile_at(n, base - 2 * TILE), :]

        def body(n, carry):
            for u in range(2):
                tile = n * 2 + u
                spot = [spot_ref[c, tile_at(tile, base), :] for c in range(3)]
                parts = []
                for k in range(6):
                    near = (box // 2 - 1) * 2 + k
                    delta = [spot[c] - row(rows, near * 8 + c) for c in range(3)]
                    moment = [row(rows, near * 8 + 4 + c) for c in range(3)]
                    parts.append(field_of(delta, scalar(k, 0, tile), scalar(k, 1, tile), moment))
                for c in range(3):
                    total[c, tile_at(tile, (box - 2) * TILE), :] = added([part[c] for part in parts])
            return carry

        lax.fori_loop(0, (trips[box, 0] + 1) // 2, body, 0)

    def sweep(boxes, moments):
        for c in range(3):
            rows[pl.ds(4 + c, 10, stride=8), :] = moments[c]
        for x in range(NX):

            @pl.when(x_me == x)
            def _():
                for box in boxes:
                    tiles(box, x)

        return [jnp.concatenate([lane_sums(total, c, box - 2) for box in boxes], axis=0) for c in range(3)]

    one = [pol * residual[c] for c in range(3)]
    fields = sweep(range(2, 8), one)
    two = []
    edge = jnp.zeros((2, TILE), F32)
    for c in range(3):
        value = pol[2:8] * (residual[c][2:8] + fields[c] + alone[2:8] * one[c][2:8])
        two.append(jnp.concatenate([edge, jnp.where(live[2:8] > 0.0, value, 0.0), edge], axis=0))
        two_ref[c, 0:10, :] = two[c]
    fields = sweep(range(4, 6), two)
    for c in range(3):
        value = pol[4:6] * (residual[c][4:6] + fields[c] + alone[4:6] * two_ref[c, 4:6, :])
        three = source[c] + jnp.where(live[4:6] > 0.0, value, 0.0)
        for w in range(2):
            new_ref[c : c + 1, w * TILE : (w + 1) * TILE] = three[w : w + 1]
            out_ref[c : c + 1, w * TILE : (w + 1) * TILE] = residual[c][4 + w : 5 + w]


VMEM = pl.BlockSpec(memory_space=pltpu.VMEM)
HBM = pl.BlockSpec(memory_space=pltpu.HBM)


def shape_of(shape):
    return shape if isinstance(shape, jax.ShapeDtypeStruct) else jax.ShapeDtypeStruct(shape, F32)


def call(body, ins, outs, scratch, cost, limit, name):
    return pl.pallas_call(
        body,
        in_specs=ins,
        out_specs=[VMEM] * len(outs),
        out_shape=[shape_of(shape) for shape in outs],
        scratch_shapes=[pltpu.VMEM(shape, F32) if isinstance(shape, tuple) else shape for shape in scratch],
        cost_estimate=pl.CostEstimate(flops=cost, bytes_accessed=1 << 20, transcendentals=0),
        compiler_params=pltpu.CompilerParams(vmem_limit_bytes=limit << 20),
        name=name,
    )


def device(group, box):
    return group * OWNERS + box


def rounds():
    plane = [
        [device(2 * y + core, z * NX + x) for y in range(NY) for x in range(NX)]
        for core in range(2)
        for z in range(OWNERS // NX)
    ]
    chip = [[device(2 * y, b), device(2 * y + 1, b)] for y in range(NY) for b in range(OWNERS)]
    up = [[(device(g, b), device(g, b + NX)) for b in range(OWNERS - NX)] for g in range(GROUPS)]
    down = [[(target, source) for source, target in pairs] for pairs in up]
    apart = [pair for g in range(GROUPS) for pair in (down[g] if g % 2 else up[g])]
    near_side = [(s, t) for pairs in up for s, t in pairs if s % NX < 2]
    near_side += [(s, t) for pairs in down for s, t in pairs if s % NX >= 2]
    return plane, chip, apart, near_side


PLANE_SETS, CHIP_SETS, APART, NEAR_SIDE = rounds()
OWN_ROWS = PLANE * 8 + 64
SIDE_ROWS = 256 + 64


def on_device(
    dipoles, perm_field, positions, polarizability, occupancy, far_boxes, far_class, far_count, far_scale, translations
):
    me = lax.axis_index("d").astype(jnp.int32)
    two = pltpu.SMEM((2,), jnp.int32)
    lists = pltpu.VMEM((2, ILIST), jnp.int32)
    [chunk] = call(
        first_kernel,
        [HBM] * 9,
        [(PLANE, CHUNK, TILE)],
        [(NTERM * 8, TILE), (CHUNK, TILE)]
        + [(3, 2 * TILE)] * 3
        + [(1, 2 * TILE), (2, ILIST), lists, lists, two, two, pltpu.SemaphoreType.DMA((9,))],
        1 << 20,
        60,
        "first",
    )(
        occupancy, far_count, dipoles, perm_field, positions, polarizability.reshape(1, 2 * TILE),
        far_boxes, far_class, far_scale,
    )
    block = lax.all_to_all(chunk, "d", 0, 0, axis_index_groups=PLANE_SETS, tiled=True)
    half = jax.ShapeDtypeStruct((CLASSES * 256, NTERM), BF16)
    t_high, t_low = call(prepare_kernel, [VMEM], [half, half], [], 1 << 28, 12, "prepare")(
        jnp.transpose(translations, (1, 0, 2))
    )
    mine = (me // (2 * OWNERS)) * NX
    core = (me // OWNERS) & 1
    near = lax.dynamic_slice(block, (mine, 8, 0), (NX, 16, TILE)).reshape(64, TILE)
    part = jnp.concatenate([block[:, 0:8, :].reshape(PLANE * 8, TILE), near], axis=0)
    part, t_high, t_low = lax.optimization_barrier((part, t_high, t_low))
    own = lax.all_gather(part, "d", axis_index_groups=CHIP_SETS, axis=0)
    edges = lax.dynamic_slice(own, (0, PLANE * 8 + 32 * (1 - core), 0), (2, 32, TILE)).reshape(64, TILE)
    away = jnp.concatenate([own[:, 0 : PLANE * 8].reshape(256, TILE), edges], axis=0)
    came = lax.ppermute(away, "d", APART)
    own = own.reshape(2 * OWN_ROWS, TILE)
    half = jax.ShapeDtypeStruct((8 * 176, TILE), BF16)
    sel, near_zero, wide, m_high, m_low, plane_keep = call(
        second_kernel,
        [VMEM],
        [(64, 192), (24, TILE), (4, 8 * TILE, TILE), half, half, (12, 4 * TILE, TILE)],
        [(TILE, TILE), (3, 6 * TILE, TILE), (NTERM * 8, TILE)],
        1 << 28,
        20,
        "second",
    )(block)
    came, sel = lax.optimization_barrier((came, sel))
    sides = lax.all_gather(came, "d", axis_index_groups=CHIP_SETS, axis=0).reshape(2 * SIDE_ROWS, TILE)
    residual, send = call(
        third_kernel,
        [VMEM] * 10,
        [(24, TILE), (12, TILE)],
        [(256, TILE), (48, TILE), (48, TILE), (24, TILE), (TILE, TILE), (3, 2 * TILE, TILE)],
        1 << 28,
        16,
        "third",
    )(block, own, sides, sel, near_zero, wide, m_high, m_low, t_high, t_low)
    got = lax.ppermute(send, "d", NEAR_SIDE)
    rows, out_keep, out_wide, late_keep, late = call(
        window_kernel,
        [VMEM] * 3,
        [(TILE, TILE), (12, 2 * TILE, TILE), (4, 2 * TILE, TILE), (12, 2 * TILE, TILE), (8, TILE)],
        [(TILE, TILE), (3, 2 * TILE, TILE)],
        1 << 28,
        16,
        "window",
    )(block, sides, wide)
    new, out = call(
        fourth_kernel,
        [VMEM] * 9,
        [(3, 2 * TILE), (3, 2 * TILE)],
        [(3, 16, TILE), (TILE, TILE), (3, 6 * TILE, TILE), (3, 16, TILE)],
        1 << 28,
        20,
        "fourth",
    )(rows, plane_keep, late_keep, late, out_keep, wide, out_wide, residual, got)
    return new, out


def solution(mesh):
    flat = Mesh(mesh.devices.reshape(-1), ("d",))
    return jax.shard_map(
        on_device,
        mesh=flat,
        in_specs=(
            P(None, "d"), P(None, "d"), P(None, "d"), P("d"), P("d"), P("d", None), P("d", None), P("d"), P("d", None), P(),
        ),
        out_specs=(P(None, "d"), P(None, "d")),
        check_vma=False,
    )
```

```python
import jax
import jax.numpy as jnp
from jax import lax
from jax.experimental import pallas as pl
from jax.experimental.pallas import tpu as pltpu
from jax.sharding import Mesh
from jax.sharding import PartitionSpec as P

TILE = 128
ORDER = 8
NTERM = 165
REST = NTERM - TILE
ILIST = 189
CLASSES = 8
GROUPS = 8
OWNERS = 64
NX = 4
NY = 4
PLANE = NX * NY
CHUNK = 40
F32 = jnp.float32
BF16 = jnp.bfloat16

HALF = 5.4
ROOT_THOLE = 0.39**0.5
NT = (((1,), (1,)), ((), ()))
NN = (((1,), (0,)), ((), ()))


def term_table():
    listing = []
    for degree in range(ORDER + 1):
        for first in range(degree + 1):
            for second in range(degree + 1 - first):
                listing.append((first, second, degree - first - second))
    return listing


TERMS = term_table()


def dot(a, b, dims):
    return lax.dot_general(a, b, dims, preferred_element_type=F32)


def halves(x):
    high = x.astype(BF16)
    return high, (x - high.astype(F32)).astype(BF16)


def dot_three(a, b, dims):
    a_high, a_low = halves(a)
    b_high, b_low = halves(b)
    return dot(a_high, b_high, dims) + (dot(a_high, b_low, dims) + dot(a_low, b_high, dims))


def chebyshev(coord):
    series = [None, coord]
    doubled = 2.0 * coord
    series.append(doubled * coord - 1.0)
    for _ in range(3, ORDER + 1):
        series.append(doubled * series[-1] - series[-2])
    return series


def write_monomials(ref, px, py, pz):
    cx, cy, cz = chebyshev(px), chebyshev(py), chebyshev(pz)
    cross = {}
    for t, (i, j, k) in enumerate(TERMS):
        if (i, j) not in cross:
            if i and j:
                cross[i, j] = cx[i] * cy[j]
            else:
                cross[i, j] = cx[i] if i else cy[j]
        head = cross[i, j]
        if head is None:
            value = jnp.ones_like(px) if k == 0 else cz[k]
        else:
            value = head if k == 0 else head * cz[k]
        ref[t * 8 : t * 8 + 8, :] = value


def own_place():
    me = lax.axis_index("d")
    return (me // OWNERS) & 1, (me // NX) & (OWNERS // NX - 1), me & (NX - 1), (me // (2 * OWNERS)) * NX


def first_kernel(
    occ_hbm, count_hbm, dip_hbm, perm_hbm, pos_hbm, pol_hbm, boxes_hbm, class_hbm, scale_hbm, out_ref,
    mono, chunk, dip_ref, perm_ref, pos_ref, pol_ref, scale_ref, boxes_ref, class_ref, occ_ref, count_ref, sems,
):
    pairs = (
        (pos_hbm, pos_ref), (dip_hbm, dip_ref), (pol_hbm, pol_ref), (perm_hbm, perm_ref),
        (boxes_hbm, boxes_ref), (class_hbm, class_ref), (scale_hbm, scale_ref), (occ_hbm, occ_ref), (count_hbm, count_ref),
    )
    copies = [pltpu.make_async_copy(source, target, sems.at[n]) for n, (source, target) in enumerate(pairs)]
    for copy in copies:
        copy.start()
    chunk[...] = jnp.zeros_like(chunk)
    lane = lax.broadcasted_iota(jnp.int32, (1, TILE), 1)
    for copy in copies:
        copy.wait()
    for w in range(2):
        live = (lane < occ_ref[w]).astype(F32)
        lanes = slice(w * TILE, (w + 1) * TILE)
        base = 8 + w * 8
        chunk[base : base + 3, :] = pos_ref[:, lanes]
        chunk[base + 3 : base + 4, :] = pol_ref[:, lanes]
        chunk[base + 4 : base + 7, :] = dip_ref[:, lanes] * live
        chunk[base + 7 : base + 8, :] = live
        chunk[24 + w * 3 : 27 + w * 3, :] = perm_ref[:, lanes]
    plane = own_place()[1]
    box = boxes_ref[...]
    within = box & 1
    layer = (box >> 1) & (OWNERS - 1)
    group = box >> 7
    step = (layer >> 2) - plane
    stack = jnp.where(step == 0, 0, jnp.where(step < 0, 1, 2))
    place = within * 96 + stack * 32 + (group & 1) * PLANE + (group >> 1) * NX + (layer & 3)
    place = place.astype(F32)
    kind = class_ref[...].astype(F32)
    entry = lax.broadcasted_iota(jnp.int32, (1, ILIST), 1)
    for w in range(2):
        weight = scale_ref[w : w + 1, :] * (entry < count_ref[w]).astype(F32)
        for n, row in enumerate((place[w : w + 1, :], kind[w : w + 1, :], weight)):
            chunk[30 + w * 3 + n : 31 + w * 3 + n, :] = row[:, :TILE]
            chunk[36 + n : 37 + n, w * 64 : w * 64 + ILIST - TILE] = row[:, TILE:]
    def both(row):
        two = chunk[pl.ds(8 + row, 2, stride=8), :]
        return jnp.concatenate([two, two, two, two], axis=0)

    write_monomials(mono, both(0), both(1), both(2))
    for w in range(2):
        terms = mono[pl.ds(w, NTERM, stride=8), :]
        moment = dot_three(chunk[12 + w * 8 : 15 + w * 8, :], terms, NT)
        for c in range(3):
            chunk[c * 2 + w : c * 2 + w + 1, :] = moment[c : c + 1, :TILE]
            chunk[6 + w : 7 + w, c * REST : (c + 1) * REST] = moment[c : c + 1, TILE:]
    whole = chunk[...]
    for m in range(PLANE):
        out_ref[m, :, :] = whole


def write_fields(rows_ref, number, px, py, pz, root, first_layer):
    box = lax.broadcasted_iota(jnp.int32, (number, TILE), 0)
    rows_ref[pl.ds(0, number, stride=8), :] = HALF * (px + 2.0 * (box & 1).astype(F32))
    rows_ref[pl.ds(1, number, stride=8), :] = HALF * py
    rows_ref[pl.ds(2, number, stride=8), :] = HALF * (pz + 2.0 * ((box >> 1) + first_layer).astype(F32))
    rows_ref[pl.ds(3, number, stride=8), :] = root


def root_of(pol):
    return jnp.where(pol > 0.0, ROOT_THOLE * lax.rsqrt(jnp.where(pol > 0.0, pol, 1.0)), 0.0)


def scalars(delta, roots):
    dx, dy, dz = delta
    squared = dx * dx + dy * dy + (dz * dz + 1.0)
    inverse = lax.rsqrt(squared)
    inv_two = inverse * inverse
    inv_three = inverse * inv_two
    minus = (squared * (squared * inverse)) * roots
    damping = jnp.exp(minus)
    lambda_three = 1.0 - damping
    lambda_five = lambda_three + minus * damping
    return (3.0 * lambda_five) * (inv_three * inv_two), lambda_three * inv_three


def field_of(delta, radial, direct, moment):
    along = radial * (delta[0] * moment[0] + delta[1] * moment[1] + delta[2] * moment[2])
    return [delta[c] * along - direct * moment[c] for c in range(3)]


def added(parts):
    while len(parts) > 1:
        parts = [parts[i] + parts[i + 1] if i + 1 < len(parts) else parts[i] for i in range(0, len(parts), 2)]
    return parts[0]


def row(ref, at):
    return ref[pl.ds(at, 8, stride=0), :]


def tile_at(n, base=0):
    return pl.ds(pl.multiple_of(base + n * 8, 8), 8)


def trips_of(live):
    count = jnp.sum(live, axis=1, keepdims=True)
    tiles = ((count + 7.0) * 0.125).astype(jnp.int32)
    return [tiles[k, 0] for k in range(live.shape[0])]


def spread(wide_ref, cols, boxes, fields):
    for slot, box in enumerate(boxes):
        for f in fields:
            at = box * 8 + f
            value = jnp.broadcast_to(cols[:, at : at + 1], (TILE, TILE))
            wide_ref[f, slot * TILE : (slot + 1) * TILE, :] = -value if f == 3 else value


def near_boxes(total_ref, slots, wide_ref, targets, trips, rows_ref, sources, keep_ref):
    def body(n, carry):
        mine = [[wide_ref[f, tile_at(n, target * TILE), :] for f in range(4)] for target in targets]
        parts = [[] for _ in targets]
        for k, box in enumerate(sources):
            where = [row(rows_ref, box * 8 + f) for f in range(7)]
            for i, spot in enumerate(mine):
                delta = [spot[c] - where[c] for c in range(3)]
                radial, direct = scalars(delta, spot[3] * where[3])
                if keep_ref is not None:
                    kept = tile_at(n, slots[i] * TILE)
                    keep_ref[k, kept, :] = radial
                    keep_ref[6 + k, kept, :] = direct
                parts[i].append(field_of(delta, radial, direct, where[4:7]))
        for i, slot in enumerate(slots):
            for c in range(3):
                total_ref[c, tile_at(n, slot * TILE), :] = added([part[c] for part in parts[i]])
        return carry

    lax.fori_loop(0, trips, body, 0)


def lane_sums(total_ref, c, slot):
    return jnp.sum(jnp.transpose(total_ref[c, slot * TILE : (slot + 1) * TILE, :]), axis=0, keepdims=True)


def self_term(root):
    return 1.0 - jnp.exp(-(root * root))


def prepare_kernel(trans_ref, high_ref, low_ref):
    high_ref[...] = jnp.zeros_like(high_ref)
    low_ref[...] = jnp.zeros_like(low_ref)
    for o in range(CLASSES):
        high, low = halves(jnp.transpose(trans_ref[:, o, :]))
        high_ref[o * 256 : o * 256 + NTERM, :] = high
        low_ref[o * 256 : o * 256 + NTERM, :] = low


def second_kernel(block_ref, sel_ref, near_ref, wide, m_high_ref, m_low_ref, keep, rows, total, mono):
    mine = own_place()[3]
    rows[...] = jnp.zeros_like(rows)
    for x in range(NX):
        rows[x * 16 : x * 16 + 16, :] = block_ref[mine + x, 8:24, :]

    def field(f):
        return rows[pl.ds(f, 8, stride=8), :]

    px, py, pz, root = field(0), field(1), field(2), root_of(field(3))
    trips = trips_of(field(7))
    write_monomials(mono, px, py, pz)
    write_fields(rows, 8, px, py, pz, root, 0)
    spread(wide, jnp.transpose(rows[...]), range(8), range(4))
    for k in range(8):
        high, low = halves(mono[pl.ds(k, NTERM, stride=8), :])
        m_high_ref[k * 176 : k * 176 + NTERM, :] = high
        m_low_ref[k * 176 : k * 176 + NTERM, :] = low
    x_me = own_place()[2]
    near_ref[...] = jnp.zeros_like(near_ref)
    for box in range(2, 6):
        first = (box // 2 - 1) * 2
        near_boxes(total, [box - 2], wide, [box], trips[box], rows, range(first, first + 6), keep)
    for sent, boxes, sources in ((x_me < 2, (6, 7), range(4, 8)), (x_me >= 2, (0, 1), range(4))):

        @pl.when(sent)
        def _():
            for w, box in enumerate(boxes):
                near_boxes(total, [4 + w], wide, [box], trips[box], rows, sources, None)
            for c in range(3):
                for w, box in enumerate(boxes):
                    near_ref[c * 8 + box : c * 8 + box + 1, :] = lane_sums(total, c, 4 + w)

    spot = lax.broadcasted_iota(jnp.int32, (192, TILE), 0)
    kinds = lax.broadcasted_iota(jnp.int32, (CLASSES, TILE), 0)
    side = lax.broadcasted_iota(jnp.int32, (CLASSES, TILE), 1) >> 6
    for x in range(NX):
        got = jnp.zeros((32, 192), F32)
        first, second = [], []
        for w in range(2):
            at = 30 + w * 3
            place = block_ref[mine + x, at : at + 1, :].astype(jnp.int32)
            kind = block_ref[mine + x, at + 1 : at + 2, :].astype(jnp.int32)
            weight = jnp.where(kinds == kind, block_ref[mine + x, at + 2 : at + 3, :], 0.0)
            chosen = jnp.where(spot == place, 1.0, 0.0).astype(BF16)
            high = weight.astype(BF16).astype(F32)
            first.append(dot(jnp.concatenate([high, weight - high], axis=0).astype(BF16), chosen, NT))
        place = block_ref[mine + x, 36:37, :].astype(jnp.int32)
        kind = block_ref[mine + x, 37:38, :].astype(jnp.int32)
        weight = jnp.where(kinds == kind, block_ref[mine + x, 38:39, :], 0.0)
        high = weight.astype(BF16).astype(F32)
        low = weight - high
        both = [jnp.where(side == w, part, 0.0) for w in range(2) for part in (high, low)]
        chosen = jnp.where(spot == place, 1.0, 0.0).astype(BF16)
        second = dot(jnp.concatenate(both, axis=0).astype(BF16), chosen, NT)
        for w in range(2):
            k = x * 2 + w
            tail = second[w * 16 : w * 16 + 16]
            sel_ref[k * 8 : k * 8 + 8, :] = (first[w][0:8] + tail[0:8]) + (first[w][8:16] + tail[8:16])
    for c in range(3):
        for box in range(2, 6):
            near_ref[c * 8 + box : c * 8 + box + 1, :] = lane_sums(total, c, box - 2)


def third_kernel(
    block_ref, own_ref, sides_ref, sel_ref, near_ref, wide_ref, m_high_ref, m_low_ref, t_high_ref, t_low_ref,
    res_ref, send_ref, summed, head, rest, far, rows, total,
):
    core, _, x_me, mine = own_place()
    sel_high, sel_low = halves(sel_ref[...])
    both = jnp.concatenate([sel_high, sel_low], axis=0)
    for kind in range(4):
        pieces = []
        for w in range(2):
            pieces += [own_ref[pl.ds(at + kind * 2 + w, 16, stride=8), :] for at in (0, OWN_ROWS)]
            pieces += [sides_ref[pl.ds(at + kind * 2 + w, 32, stride=8), :] for at in (0, SIDE_ROWS)]
        high, low = halves(jnp.concatenate(pieces, axis=0))
        got = dot(both, high, NN)
        summed[kind * 64 : kind * 64 + 64, :] = got[0:64] + (got[64:128] + dot(sel_high, low, NN))
    parts = []
    for c in range(3):
        pieces = []
        for o in range(CLASSES):
            pieces.append(summed[pl.ds(c * 64 + o, 8, stride=8), :])
            tail = summed[pl.ds(192 + o, 8, stride=8), :][:, c * REST : (c + 1) * REST]
            pieces.append(jnp.concatenate([tail, jnp.zeros((8, TILE - REST), F32)], axis=1))
        parts.append(jnp.concatenate(pieces, axis=1))
    parts.append(jnp.zeros((8, CLASSES * 256), F32))
    high, low = halves(jnp.concatenate(parts, axis=0))
    got = dot(jnp.concatenate([high, low], axis=0), t_high_ref[...], NN)
    moved = got[0:24] + (got[32:56] + dot(high, t_low_ref[...], NN)[0:24])
    moved_high = moved.astype(BF16).astype(F32)
    for n, part in enumerate((moved_high, moved - moved_high)):
        head[n * 24 : n * 24 + 24, :] = part[:, 0:TILE]
        rest[n * 24 : n * 24 + 24, 0:REST] = part[:, TILE:]
    rows[...] = jnp.zeros_like(rows)
    rows[0:16, :] = sides_ref[pl.ds(pl.multiple_of(272 + 32 * core, 8), 16), :]
    for x in range(NX):
        rows[16 + x * 16 : 32 + x * 16, :] = block_ref[mine + x, 8:24, :]
    rows[80:96, :] = sides_ref[pl.ds(pl.multiple_of(SIDE_ROWS + 256 + 32 * core, 8), 16), :]

    def field(f):
        return rows[pl.ds(f, 12, stride=8), :]

    px, py, pz, pol = field(0), field(1), field(2), field(3)
    live = rows[pl.ds(16 + 7, 8, stride=8), :]
    source = [rows[pl.ds(16 + 4 + c, 8, stride=8), :] for c in range(3)]
    root = root_of(pol)
    trips = trips_of(live)
    write_fields(rows, 12, px, py, pz, root, -1)
    for sent, boxes, sources in ((x_me < 2, (6, 7), (10, 11)), (x_me >= 2, (0, 1), (0, 1))):

        @pl.when(sent)
        def _():
            most = jnp.maximum(trips[boxes[0]], trips[boxes[1]])
            near_boxes(total, (0, 1), wide_ref, boxes, most, rows, sources, None)

    for k in range(8):
        left = jnp.concatenate([head[pl.ds(k, 6, stride=8), :], rest[pl.ds(k, 6, stride=8), :][:, 0:REST]], axis=1)
        left = left.astype(BF16)
        with_high = dot(left, m_high_ref[k * 176 : k * 176 + NTERM, :], NN)
        with_low = dot(left, m_low_ref[k * 176 : k * 176 + NTERM, :], NN)
        value = with_high[0:3] + (with_high[3:6] + with_low[0:3])
        for c in range(3):
            far[c * 8 + k : c * 8 + k + 1, :] = value[c : c + 1]
    alone = self_term(root[2:10])
    nothing = jnp.zeros((6, TILE), F32)
    for c in range(3):
        perm = jnp.concatenate(
            [block_ref[mine + x, 24 + w * 3 + c : 25 + w * 3 + c, :] for x in range(NX) for w in range(2)], axis=0
        )
        ends = [lane_sums(total, c, slot) for slot in range(2)]
        edge = jnp.where(x_me < 2, jnp.concatenate([nothing] + ends, axis=0), jnp.concatenate(ends + [nothing], axis=0))
        near_zero = near_ref[c * 8 : c * 8 + 8, :] + edge + alone * source[c]
        res_ref[c * 8 : c * 8 + 8, :] = jnp.where(
            live > 0.0, perm + far[c * 8 : c * 8 + 8, :] + near_zero - source[c] / pol[2:10], 0.0
        )
    first = jnp.where(x_me < 2, 4, 0)
    for c in range(3):
        for k in range(4):
            send_ref[c * 4 + k : c * 4 + k + 1, :] = res_ref[pl.ds(c * 8 + first + k, 1), :]


def window_kernel(block_ref, sides_ref, wide_ref, rows, keep, edge, late_keep, late_ref, every, total):
    core, _, x_me, mine = own_place()
    first = x_me * 2
    every[0:32, :] = sides_ref[pl.ds(pl.multiple_of(256 + 32 * core, 8), 32), :]
    for x in range(NX):
        every[32 + x * 16 : 48 + x * 16, :] = block_ref[mine + x, 8:24, :]
    every[96:128, :] = sides_ref[pl.ds(pl.multiple_of(SIDE_ROWS + 256 + 32 * core, 8), 32), :]
    rows[...] = jnp.zeros_like(rows)
    for k in range(10):
        rows[k * 8 : k * 8 + 8, :] = every[pl.ds(pl.multiple_of((first + k) * 8, 8), 8), :]

    def field(f):
        return rows[pl.ds(f, 10, stride=8), :]

    px, py, pz, pol, live = field(0), field(1), field(2), field(3), field(7)
    root = root_of(pol)
    rows[80:90, :] = pol
    rows[96:106, :] = self_term(root)
    trips = trips_of(live)
    write_fields(rows, 10, px, py, pz, root, x_me - 2)
    for x, layer in enumerate((2, 1, 3, 2)):

        @pl.when(x_me == x)
        def _():
            plane_box = 0 if x < 2 else 6
            first_source = (layer - 1) * 2
            for w in range(2):
                sources = range(first_source, first_source + 6)
                many = trips[layer * 2 + w]
                near_boxes(total, [w], wide_ref, [plane_box + w], many, rows, sources, late_keep)
            for w in range(2):
                alive = live[layer * 2 + w : layer * 2 + w + 1] > 0.0
                for c in range(3):
                    late_ref[c * 2 + w : c * 2 + w + 1, :] = jnp.where(alive, lane_sums(total, c, w), 0.0)

    for outside, layer in ((x_me == 0, 1), (x_me == NX - 1, 3)):

        @pl.when(outside)
        def _():
            cols = jnp.transpose(rows[...])
            spread(edge, cols, (layer * 2, layer * 2 + 1), range(4))
            for w in range(2):

                def body(n, carry):
                    for u in range(2):
                        at = tile_at(n * 2 + u, w * TILE)
                        spot = [edge[f, at, :] for f in range(4)]
                        for k in range(6):
                            source = (layer - 1) * 2 + k
                            delta = [spot[c] - row(rows, source * 8 + c) for c in range(3)]
                            radial, direct = scalars(delta, spot[3] * row(rows, source * 8 + 3))
                            keep[k, at, :] = radial
                            keep[6 + k, at, :] = direct
                    return carry

                lax.fori_loop(0, (trips[layer * 2 + w] + 1) // 2, body, 0)


def fourth_kernel(
    rows_ref, plane_keep, late_keep, late_ref, out_keep, plane_wide, out_wide, res_ref, got_ref, new_ref, out_ref,
    moved, rows, total, two_ref,
):
    x_me = own_place()[2]
    first = x_me * 2
    for c in range(3):
        got = got_ref[c * 4 : c * 4 + 4, :]
        moved[c, 0:4, :] = got
        moved[c, 4:12, :] = res_ref[c * 8 : c * 8 + 8, :]
        moved[c, 12:16, :] = got
        for w in range(2):
            at = pl.ds(jnp.where(x_me < 2, 4, 10) + w, 1)
            moved[c, at, :] = moved[c, at, :] + late_ref[c * 2 + w : c * 2 + w + 1, :]
    rows[...] = rows_ref[...]
    pol, alone = rows[80:90, :], rows[96:106, :]
    live = rows[pl.ds(7, 10, stride=8), :]
    trips = trips_of(live)
    source = [rows[pl.ds(32 + 4 + c, 2, stride=8), :] for c in range(3)]
    residual = [jnp.concatenate([moved[c, pl.ds(first + k, 1), :] for k in range(10)], axis=0) for c in range(3)]

    def tiles(box, x):
        layer, w = x + box // 2 - 2, box % 2
        inside = 0 <= layer < NX
        spot_ref = plane_wide if inside else out_wide
        base = (layer * 2 + w if inside else w) * TILE

        def scalar(k, part, n):
            if not inside:
                return out_keep[part * 6 + k, tile_at(n, base), :]
            if layer == (0 if x < 2 else NX - 1):
                return late_keep[part * 6 + k, tile_at(n, w * TILE), :]
            return plane_keep[part * 6 + k, tile_at(n, base - 2 * TILE), :]

        def body(n, carry):
            for u in range(2):
                tile = n * 2 + u
                spot = [spot_ref[c, tile_at(tile, base), :] for c in range(3)]
                parts = []
                for k in range(6):
                    near = (box // 2 - 1) * 2 + k
                    delta = [spot[c] - row(rows, near * 8 + c) for c in range(3)]
                    moment = [row(rows, near * 8 + 4 + c) for c in range(3)]
                    parts.append(field_of(delta, scalar(k, 0, tile), scalar(k, 1, tile), moment))
                for c in range(3):
                    total[c, tile_at(tile, (box - 2) * TILE), :] = added([part[c] for part in parts])
            return carry

        lax.fori_loop(0, (trips[box] + 1) // 2, body, 0)

    def sweep(boxes, moments):
        for c in range(3):
            rows[pl.ds(4 + c, 10, stride=8), :] = moments[c]
        for x in range(NX):

            @pl.when(x_me == x)
            def _():
                for box in boxes:
                    tiles(box, x)

        return [jnp.concatenate([lane_sums(total, c, box - 2) for box in boxes], axis=0) for c in range(3)]

    one = [pol * residual[c] for c in range(3)]
    fields = sweep(range(2, 8), one)
    two = []
    edge = jnp.zeros((2, TILE), F32)
    for c in range(3):
        value = pol[2:8] * (residual[c][2:8] + fields[c] + alone[2:8] * one[c][2:8])
        two.append(jnp.concatenate([edge, jnp.where(live[2:8] > 0.0, value, 0.0), edge], axis=0))
        two_ref[c, 0:10, :] = two[c]
    fields = sweep(range(4, 6), two)
    for c in range(3):
        value = pol[4:6] * (residual[c][4:6] + fields[c] + alone[4:6] * two_ref[c, 4:6, :])
        three = source[c] + jnp.where(live[4:6] > 0.0, value, 0.0)
        for w in range(2):
            new_ref[c : c + 1, w * TILE : (w + 1) * TILE] = three[w : w + 1]
            out_ref[c : c + 1, w * TILE : (w + 1) * TILE] = residual[c][4 + w : 5 + w]


VMEM = pl.BlockSpec(memory_space=pltpu.VMEM)
HBM = pl.BlockSpec(memory_space=pltpu.HBM)


def shape_of(shape):
    return shape if isinstance(shape, jax.ShapeDtypeStruct) else jax.ShapeDtypeStruct(shape, F32)


def call(body, ins, outs, scratch, cost, limit, name):
    return pl.pallas_call(
        body,
        in_specs=ins,
        out_specs=[VMEM] * len(outs),
        out_shape=[shape_of(shape) for shape in outs],
        scratch_shapes=[pltpu.VMEM(shape, F32) if isinstance(shape, tuple) else shape for shape in scratch],
        cost_estimate=pl.CostEstimate(flops=cost, bytes_accessed=1 << 20, transcendentals=0),
        compiler_params=pltpu.CompilerParams(vmem_limit_bytes=limit << 20),
        name=name,
    )


def device(group, box):
    return group * OWNERS + box


def rounds():
    plane = [
        [device(2 * y + core, z * NX + x) for y in range(NY) for x in range(NX)]
        for core in range(2)
        for z in range(OWNERS // NX)
    ]
    chip = [[device(2 * y, b), device(2 * y + 1, b)] for y in range(NY) for b in range(OWNERS)]
    up = [[(device(g, b), device(g, b + NX)) for b in range(OWNERS - NX)] for g in range(GROUPS)]
    down = [[(target, source) for source, target in pairs] for pairs in up]
    apart = [pair for g in range(GROUPS) for pair in (down[g] if g % 2 else up[g])]
    near_side = [(s, t) for pairs in up for s, t in pairs if s % NX < 2]
    near_side += [(s, t) for pairs in down for s, t in pairs if s % NX >= 2]
    return plane, chip, apart, near_side


PLANE_SETS, CHIP_SETS, APART, NEAR_SIDE = rounds()
OWN_ROWS = PLANE * 8 + 64
SIDE_ROWS = 256 + 64


def on_device(
    dipoles, perm_field, positions, polarizability, occupancy, far_boxes, far_class, far_count, far_scale, translations
):
    me = lax.axis_index("d").astype(jnp.int32)
    two = pltpu.SMEM((2,), jnp.int32)
    lists = pltpu.VMEM((2, ILIST), jnp.int32)
    [chunk] = call(
        first_kernel,
        [HBM] * 9,
        [(PLANE, CHUNK, TILE)],
        [(NTERM * 8, TILE), (CHUNK, TILE)]
        + [(3, 2 * TILE)] * 3
        + [(1, 2 * TILE), (2, ILIST), lists, lists, two, two, pltpu.SemaphoreType.DMA((9,))],
        1 << 20,
        60,
        "first",
    )(
        occupancy, far_count, dipoles, perm_field, positions, polarizability.reshape(1, 2 * TILE),
        far_boxes, far_class, far_scale,
    )
    block = lax.all_to_all(chunk, "d", 0, 0, axis_index_groups=PLANE_SETS, tiled=True)
    half = jax.ShapeDtypeStruct((CLASSES * 256, NTERM), BF16)
    t_high, t_low = call(prepare_kernel, [VMEM], [half, half], [], 1 << 28, 12, "prepare")(
        jnp.transpose(translations, (1, 0, 2))
    )
    mine = (me // (2 * OWNERS)) * NX
    core = (me // OWNERS) & 1
    near = lax.dynamic_slice(block, (mine, 8, 0), (NX, 16, TILE)).reshape(64, TILE)
    part = jnp.concatenate([block[:, 0:8, :].reshape(PLANE * 8, TILE), near], axis=0)
    part, t_high, t_low = lax.optimization_barrier((part, t_high, t_low))
    own = lax.all_gather(part, "d", axis_index_groups=CHIP_SETS, axis=0)
    edges = lax.dynamic_slice(own, (0, PLANE * 8 + 32 * (1 - core), 0), (2, 32, TILE)).reshape(64, TILE)
    away = jnp.concatenate([own[:, 0 : PLANE * 8].reshape(256, TILE), edges], axis=0)
    came = lax.ppermute(away, "d", APART)
    own = own.reshape(2 * OWN_ROWS, TILE)
    half = jax.ShapeDtypeStruct((8 * 176, TILE), BF16)
    sel, near_zero, wide, m_high, m_low, plane_keep = call(
        second_kernel,
        [VMEM],
        [(64, 192), (24, TILE), (4, 8 * TILE, TILE), half, half, (12, 4 * TILE, TILE)],
        [(TILE, TILE), (3, 6 * TILE, TILE), (NTERM * 8, TILE)],
        1 << 28,
        20,
        "second",
    )(block)
    came, sel = lax.optimization_barrier((came, sel))
    sides = lax.all_gather(came, "d", axis_index_groups=CHIP_SETS, axis=0).reshape(2 * SIDE_ROWS, TILE)
    residual, send = call(
        third_kernel,
        [VMEM] * 10,
        [(24, TILE), (12, TILE)],
        [(256, TILE), (48, TILE), (48, TILE), (24, TILE), (TILE, TILE), (3, 2 * TILE, TILE)],
        1 << 28,
        16,
        "third",
    )(block, own, sides, sel, near_zero, wide, m_high, m_low, t_high, t_low)
    got = lax.ppermute(send, "d", NEAR_SIDE)
    rows, out_keep, out_wide, late_keep, late = call(
        window_kernel,
        [VMEM] * 3,
        [(TILE, TILE), (12, 2 * TILE, TILE), (4, 2 * TILE, TILE), (12, 2 * TILE, TILE), (8, TILE)],
        [(TILE, TILE), (3, 2 * TILE, TILE)],
        1 << 28,
        16,
        "window",
    )(block, sides, wide)
    new, out = call(
        fourth_kernel,
        [VMEM] * 9,
        [(3, 2 * TILE), (3, 2 * TILE)],
        [(3, 16, TILE), (TILE, TILE), (3, 6 * TILE, TILE), (3, 16, TILE)],
        1 << 28,
        20,
        "fourth",
    )(rows, plane_keep, late_keep, late, out_keep, wide, out_wide, residual, got)
    return new, out


def solution(mesh):
    flat = Mesh(mesh.devices.reshape(-1), ("d",))
    return jax.shard_map(
        on_device,
        mesh=flat,
        in_specs=(
            P(None, "d"), P(None, "d"), P(None, "d"), P("d"), P("d"), P("d", None), P("d", None), P("d"), P("d", None), P(),
        ),
        out_specs=(P(None, "d"), P(None, "d")),
        check_vma=False,
    )
```

```python
import jax
import jax.numpy as jnp
from jax import lax
from jax.experimental import pallas as pl
from jax.experimental.pallas import tpu as pltpu
from jax.sharding import Mesh
from jax.sharding import PartitionSpec as P

TILE = 128
ORDER = 8
NTERM = 165
REST = NTERM - TILE
ILIST = 189
CLASSES = 8
GROUPS = 8
OWNERS = 64
NX = 4
NY = 4
PLANE = NX * NY
CHUNK = 40
F32 = jnp.float32
BF16 = jnp.bfloat16

HALF = 5.4
ROOT_THOLE = 0.39**0.5
NT = (((1,), (1,)), ((), ()))
NN = (((1,), (0,)), ((), ()))


def term_table():
    listing = []
    for degree in range(ORDER + 1):
        for first in range(degree + 1):
            for second in range(degree + 1 - first):
                listing.append((first, second, degree - first - second))
    return listing


TERMS = term_table()


def dot(a, b, dims):
    return lax.dot_general(a, b, dims, preferred_element_type=F32)


def halves(x):
    high = x.astype(BF16)
    return high, (x - high.astype(F32)).astype(BF16)


def dot_three(a, b, dims):
    a_high, a_low = halves(a)
    b_high, b_low = halves(b)
    return dot(a_high, b_high, dims) + (dot(a_high, b_low, dims) + dot(a_low, b_high, dims))


def chebyshev(coord):
    series = [None, coord]
    doubled = 2.0 * coord
    series.append(doubled * coord - 1.0)
    for _ in range(3, ORDER + 1):
        series.append(doubled * series[-1] - series[-2])
    return series


def write_monomials(ref, px, py, pz):
    cx, cy, cz = chebyshev(px), chebyshev(py), chebyshev(pz)
    cross = {}
    for t, (i, j, k) in enumerate(TERMS):
        if (i, j) not in cross:
            if i and j:
                cross[i, j] = cx[i] * cy[j]
            else:
                cross[i, j] = cx[i] if i else cy[j]
        head = cross[i, j]
        if head is None:
            value = jnp.ones_like(px) if k == 0 else cz[k]
        else:
            value = head if k == 0 else head * cz[k]
        ref[t * 8 : t * 8 + 8, :] = value


def own_place():
    me = lax.axis_index("d")
    return (me // OWNERS) & 1, (me // NX) & (OWNERS // NX - 1), me & (NX - 1), (me // (2 * OWNERS)) * NX


def first_kernel(
    occ_hbm, count_hbm, dip_hbm, perm_hbm, pos_hbm, pol_hbm, boxes_hbm, class_hbm, scale_hbm, out_ref,
    mono, chunk, dip_ref, perm_ref, pos_ref, pol_ref, scale_ref, boxes_ref, class_ref, occ_ref, count_ref, sems,
):
    pairs = (
        (pos_hbm, pos_ref), (dip_hbm, dip_ref), (pol_hbm, pol_ref), (perm_hbm, perm_ref),
        (boxes_hbm, boxes_ref), (class_hbm, class_ref), (scale_hbm, scale_ref), (occ_hbm, occ_ref), (count_hbm, count_ref),
    )
    copies = [pltpu.make_async_copy(source, target, sems.at[n]) for n, (source, target) in enumerate(pairs)]
    for copy in copies:
        copy.start()
    chunk[...] = jnp.zeros_like(chunk)
    lane = lax.broadcasted_iota(jnp.int32, (1, TILE), 1)
    for copy in copies:
        copy.wait()
    for w in range(2):
        live = (lane < occ_ref[w]).astype(F32)
        lanes = slice(w * TILE, (w + 1) * TILE)
        base = 8 + w * 8
        chunk[base : base + 3, :] = pos_ref[:, lanes]
        chunk[base + 3 : base + 4, :] = pol_ref[:, lanes]
        chunk[base + 4 : base + 7, :] = dip_ref[:, lanes] * live
        chunk[base + 7 : base + 8, :] = live
        chunk[24 + w * 3 : 27 + w * 3, :] = perm_ref[:, lanes]
    plane = own_place()[1]
    box = boxes_ref[...]
    within = box & 1
    layer = (box >> 1) & (OWNERS - 1)
    group = box >> 7
    step = (layer >> 2) - plane
    stack = jnp.where(step == 0, 0, jnp.where(step < 0, 1, 2))
    place = within * 96 + stack * 32 + (group & 1) * PLANE + (group >> 1) * NX + (layer & 3)
    place = place.astype(F32)
    kind = class_ref[...].astype(F32)
    entry = lax.broadcasted_iota(jnp.int32, (1, ILIST), 1)
    for w in range(2):
        weight = scale_ref[w : w + 1, :] * (entry < count_ref[w]).astype(F32)
        for n, row in enumerate((place[w : w + 1, :], kind[w : w + 1, :], weight)):
            chunk[30 + w * 3 + n : 31 + w * 3 + n, :] = row[:, :TILE]
            chunk[36 + n : 37 + n, w * 64 : w * 64 + ILIST - TILE] = row[:, TILE:]
    def both(row):
        two = chunk[pl.ds(8 + row, 2, stride=8), :]
        return jnp.concatenate([two, two, two, two], axis=0)

    write_monomials(mono, both(0), both(1), both(2))
    for w in range(2):
        terms = mono[pl.ds(w, NTERM, stride=8), :]
        moment = dot_three(chunk[12 + w * 8 : 15 + w * 8, :], terms, NT)
        for c in range(3):
            chunk[c * 2 + w : c * 2 + w + 1, :] = moment[c : c + 1, :TILE]
            chunk[6 + w : 7 + w, c * REST : (c + 1) * REST] = moment[c : c + 1, TILE:]
    whole = chunk[0:CHUNK, :]
    for m in range(PLANE):
        out_ref[m, :, :] = whole


def write_fields(rows_ref, number, px, py, pz, root, first_layer):
    box = lax.broadcasted_iota(jnp.int32, (number, TILE), 0)
    rows_ref[pl.ds(0, number, stride=8), :] = HALF * (px + 2.0 * (box & 1).astype(F32))
    rows_ref[pl.ds(1, number, stride=8), :] = HALF * py
    rows_ref[pl.ds(2, number, stride=8), :] = HALF * (pz + 2.0 * ((box >> 1) + first_layer).astype(F32))
    rows_ref[pl.ds(3, number, stride=8), :] = root


def root_of(pol):
    return jnp.where(pol > 0.0, ROOT_THOLE * lax.rsqrt(jnp.where(pol > 0.0, pol, 1.0)), 0.0)


def scalars(delta, roots):
    dx, dy, dz = delta
    squared = dx * dx + dy * dy + (dz * dz + 1.0)
    inverse = lax.rsqrt(squared)
    inv_two = inverse * inverse
    inv_three = inverse * inv_two
    minus = (squared * (squared * inverse)) * roots
    damping = jnp.exp(minus)
    lambda_three = 1.0 - damping
    lambda_five = lambda_three + minus * damping
    return (3.0 * lambda_five) * (inv_three * inv_two), lambda_three * inv_three


def field_of(delta, radial, direct, moment):
    along = radial * (delta[0] * moment[0] + delta[1] * moment[1] + delta[2] * moment[2])
    return [delta[c] * along - direct * moment[c] for c in range(3)]


def added(parts):
    while len(parts) > 1:
        parts = [parts[i] + parts[i + 1] if i + 1 < len(parts) else parts[i] for i in range(0, len(parts), 2)]
    return parts[0]


def row(ref, at):
    return ref[pl.ds(at, 8, stride=0), :]


def tile_at(n, base=0):
    return pl.ds(pl.multiple_of(base + n * 8, 8), 8)


def trips_of(live):
    count = jnp.sum(live, axis=1, keepdims=True)
    tiles = ((count + 7.0) * 0.125).astype(jnp.int32)
    return [tiles[k, 0] for k in range(live.shape[0])]


def spread(wide_ref, cols, boxes, fields):
    for slot, box in enumerate(boxes):
        for f in fields:
            at = box * 8 + f
            value = jnp.broadcast_to(cols[:, at : at + 1], (TILE, TILE))
            wide_ref[f, slot * TILE : (slot + 1) * TILE, :] = -value if f == 3 else value


def near_boxes(total_ref, slots, wide_ref, targets, trips, rows_ref, sources, keep_ref):
    def body(n, carry):
        mine = [[wide_ref[f, tile_at(n, target * TILE), :] for f in range(4)] for target in targets]
        parts = [[] for _ in targets]
        for k, box in enumerate(sources):
            where = [row(rows_ref, box * 8 + f) for f in range(7)]
            for i, spot in enumerate(mine):
                delta = [spot[c] - where[c] for c in range(3)]
                radial, direct = scalars(delta, spot[3] * where[3])
                if keep_ref is not None:
                    kept = tile_at(n, slots[i] * TILE)
                    keep_ref[k, kept, :] = radial
                    keep_ref[6 + k, kept, :] = direct
                parts[i].append(field_of(delta, radial, direct, where[4:7]))
        for i, slot in enumerate(slots):
            for c in range(3):
                total_ref[c, tile_at(n, slot * TILE), :] = added([part[c] for part in parts[i]])
        return carry

    lax.fori_loop(0, trips, body, 0)


def lane_sums(total_ref, c, slot):
    return jnp.sum(jnp.transpose(total_ref[c, slot * TILE : (slot + 1) * TILE, :]), axis=0, keepdims=True)


def self_term(root):
    return 1.0 - jnp.exp(-(root * root))


def prepare_kernel(trans_ref, high_ref, low_ref):
    high_ref[...] = jnp.zeros_like(high_ref)
    low_ref[...] = jnp.zeros_like(low_ref)
    for o in range(CLASSES):
        high, low = halves(jnp.transpose(trans_ref[:, o, :]))
        high_ref[o * 256 : o * 256 + NTERM, :] = high
        low_ref[o * 256 : o * 256 + NTERM, :] = low


def second_kernel(block_ref, sel_ref, near_ref, wide, m_high_ref, m_low_ref, keep, rows, total, mono):
    mine = own_place()[3]
    rows[...] = jnp.zeros_like(rows)
    for x in range(NX):
        rows[x * 16 : x * 16 + 16, :] = block_ref[mine + x, 8:24, :]

    def field(f):
        return rows[pl.ds(f, 8, stride=8), :]

    px, py, pz, root = field(0), field(1), field(2), root_of(field(3))
    trips = trips_of(field(7))
    write_monomials(mono, px, py, pz)
    write_fields(rows, 8, px, py, pz, root, 0)
    spread(wide, jnp.transpose(rows[...]), range(8), range(4))
    for k in range(8):
        high, low = halves(mono[pl.ds(k, NTERM, stride=8), :])
        m_high_ref[k * 176 : k * 176 + NTERM, :] = high
        m_low_ref[k * 176 : k * 176 + NTERM, :] = low
    x_me = own_place()[2]
    near_ref[...] = jnp.zeros_like(near_ref)
    for box in range(2, 6):
        first = (box // 2 - 1) * 2
        near_boxes(total, [box - 2], wide, [box], trips[box], rows, range(first, first + 6), keep)
    for sent, boxes, sources in ((x_me < 2, (6, 7), range(4, 8)), (x_me >= 2, (0, 1), range(4))):

        @pl.when(sent)
        def _():
            for w, box in enumerate(boxes):
                near_boxes(total, [4 + w], wide, [box], trips[box], rows, sources, None)
            for c in range(3):
                for w, box in enumerate(boxes):
                    near_ref[c * 8 + box : c * 8 + box + 1, :] = lane_sums(total, c, 4 + w)

    spot = lax.broadcasted_iota(jnp.int32, (192, TILE), 0)
    kinds = lax.broadcasted_iota(jnp.int32, (CLASSES, TILE), 0)
    side = lax.broadcasted_iota(jnp.int32, (CLASSES, TILE), 1) >> 6
    for x in range(NX):
        got = jnp.zeros((32, 192), F32)
        first, second = [], []
        for w in range(2):
            at = 30 + w * 3
            place = block_ref[mine + x, at : at + 1, :].astype(jnp.int32)
            kind = block_ref[mine + x, at + 1 : at + 2, :].astype(jnp.int32)
            weight = jnp.where(kinds == kind, block_ref[mine + x, at + 2 : at + 3, :], 0.0)
            chosen = jnp.where(spot == place, 1.0, 0.0).astype(BF16)
            high = weight.astype(BF16).astype(F32)
            first.append(dot(jnp.concatenate([high, weight - high], axis=0).astype(BF16), chosen, NT))
        place = block_ref[mine + x, 36:37, :].astype(jnp.int32)
        kind = block_ref[mine + x, 37:38, :].astype(jnp.int32)
        weight = jnp.where(kinds == kind, block_ref[mine + x, 38:39, :], 0.0)
        high = weight.astype(BF16).astype(F32)
        low = weight - high
        both = [jnp.where(side == w, part, 0.0) for w in range(2) for part in (high, low)]
        chosen = jnp.where(spot == place, 1.0, 0.0).astype(BF16)
        second = dot(jnp.concatenate(both, axis=0).astype(BF16), chosen, NT)
        for w in range(2):
            k = x * 2 + w
            tail = second[w * 16 : w * 16 + 16]
            sel_ref[k * 8 : k * 8 + 8, :] = (first[w][0:8] + tail[0:8]) + (first[w][8:16] + tail[8:16])
    for c in range(3):
        for box in range(2, 6):
            near_ref[c * 8 + box : c * 8 + box + 1, :] = lane_sums(total, c, box - 2)


def third_kernel(
    block_ref, own_ref, sides_ref, sel_ref, near_ref, wide_ref, m_high_ref, m_low_ref, t_high_ref, t_low_ref,
    res_ref, send_ref, summed, head, rest, far, rows, total,
):
    core, _, x_me, mine = own_place()
    sel_high, sel_low = halves(sel_ref[...])
    both = jnp.concatenate([sel_high, sel_low], axis=0)
    for kind in range(4):
        pieces = []
        for w in range(2):
            pieces += [own_ref[pl.ds(at + kind * 2 + w, 16, stride=8), :] for at in (0, OWN_ROWS)]
            pieces += [sides_ref[pl.ds(at + kind * 2 + w, 32, stride=8), :] for at in (0, SIDE_ROWS)]
        high, low = halves(jnp.concatenate(pieces, axis=0))
        got = dot(both, high, NN)
        summed[kind * 64 : kind * 64 + 64, :] = got[0:64] + (got[64:128] + dot(sel_high, low, NN))
    parts = []
    for c in range(3):
        pieces = []
        for o in range(CLASSES):
            pieces.append(summed[pl.ds(c * 64 + o, 8, stride=8), :])
            tail = summed[pl.ds(192 + o, 8, stride=8), :][:, c * REST : (c + 1) * REST]
            pieces.append(jnp.concatenate([tail, jnp.zeros((8, TILE - REST), F32)], axis=1))
        parts.append(jnp.concatenate(pieces, axis=1))
    parts.append(jnp.zeros((8, CLASSES * 256), F32))
    high, low = halves(jnp.concatenate(parts, axis=0))
    got = dot(jnp.concatenate([high, low], axis=0), t_high_ref[...], NN)
    moved = got[0:24] + (got[32:56] + dot(high, t_low_ref[...], NN)[0:24])
    moved_high = moved.astype(BF16).astype(F32)
    for n, part in enumerate((moved_high, moved - moved_high)):
        head[n * 24 : n * 24 + 24, :] = part[:, 0:TILE]
        rest[n * 24 : n * 24 + 24, 0:REST] = part[:, TILE:]
    rows[...] = jnp.zeros_like(rows)
    rows[0:16, :] = sides_ref[pl.ds(pl.multiple_of(272 + 32 * core, 8), 16), :]
    for x in range(NX):
        rows[16 + x * 16 : 32 + x * 16, :] = block_ref[mine + x, 8:24, :]
    rows[80:96, :] = sides_ref[pl.ds(pl.multiple_of(SIDE_ROWS + 256 + 32 * core, 8), 16), :]

    def field(f):
        return rows[pl.ds(f, 12, stride=8), :]

    px, py, pz, pol = field(0), field(1), field(2), field(3)
    live = rows[pl.ds(16 + 7, 8, stride=8), :]
    source = [rows[pl.ds(16 + 4 + c, 8, stride=8), :] for c in range(3)]
    root = root_of(pol)
    trips = trips_of(live)
    write_fields(rows, 12, px, py, pz, root, -1)
    for sent, boxes, sources in ((x_me < 2, (6, 7), (10, 11)), (x_me >= 2, (0, 1), (0, 1))):

        @pl.when(sent)
        def _():
            most = jnp.maximum(trips[boxes[0]], trips[boxes[1]])
            near_boxes(total, (0, 1), wide_ref, boxes, most, rows, sources, None)

    for k in range(8):
        left = jnp.concatenate([head[pl.ds(k, 6, stride=8), :], rest[pl.ds(k, 6, stride=8), :][:, 0:REST]], axis=1)
        left = left.astype(BF16)
        with_high = dot(left, m_high_ref[k * 176 : k * 176 + NTERM, :], NN)
        with_low = dot(left, m_low_ref[k * 176 : k * 176 + NTERM, :], NN)
        value = with_high[0:3] + (with_high[3:6] + with_low[0:3])
        for c in range(3):
            far[c * 8 + k : c * 8 + k + 1, :] = value[c : c + 1]
    alone = self_term(root[2:10])
    nothing = jnp.zeros((6, TILE), F32)
    for c in range(3):
        perm = jnp.concatenate(
            [block_ref[mine + x, 24 + w * 3 + c : 25 + w * 3 + c, :] for x in range(NX) for w in range(2)], axis=0
        )
        ends = [lane_sums(total, c, slot) for slot in range(2)]
        edge = jnp.where(x_me < 2, jnp.concatenate([nothing] + ends, axis=0), jnp.concatenate(ends + [nothing], axis=0))
        near_zero = near_ref[c * 8 : c * 8 + 8, :] + edge + alone * source[c]
        res_ref[c * 8 : c * 8 + 8, :] = jnp.where(
            live > 0.0, perm + far[c * 8 : c * 8 + 8, :] + near_zero - source[c] / pol[2:10], 0.0
        )
    first = jnp.where(x_me < 2, 4, 0)
    for c in range(3):
        for k in range(4):
            send_ref[c * 4 + k : c * 4 + k + 1, :] = res_ref[pl.ds(c * 8 + first + k, 1), :]


def window_kernel(block_ref, sides_ref, wide_ref, rows, keep, edge, late_keep, late_ref, every, total):
    core, _, x_me, mine = own_place()
    first = x_me * 2
    every[0:32, :] = sides_ref[pl.ds(pl.multiple_of(256 + 32 * core, 8), 32), :]
    for x in range(NX):
        every[32 + x * 16 : 48 + x * 16, :] = block_ref[mine + x, 8:24, :]
    every[96:128, :] = sides_ref[pl.ds(pl.multiple_of(SIDE_ROWS + 256 + 32 * core, 8), 32), :]
    rows[...] = jnp.zeros_like(rows)
    for k in range(10):
        rows[k * 8 : k * 8 + 8, :] = every[pl.ds(pl.multiple_of((first + k) * 8, 8), 8), :]

    def field(f):
        return rows[pl.ds(f, 10, stride=8), :]

    px, py, pz, pol, live = field(0), field(1), field(2), field(3), field(7)
    root = root_of(pol)
    rows[80:90, :] = pol
    rows[96:106, :] = self_term(root)
    trips = trips_of(live)
    write_fields(rows, 10, px, py, pz, root, x_me - 2)
    for x, layer in enumerate((2, 1, 3, 2)):

        @pl.when(x_me == x)
        def _():
            plane_box = 0 if x < 2 else 6
            first_source = (layer - 1) * 2
            for w in range(2):
                sources = range(first_source, first_source + 6)
                many = trips[layer * 2 + w]
                near_boxes(total, [w], wide_ref, [plane_box + w], many, rows, sources, late_keep)
            for w in range(2):
                alive = live[layer * 2 + w : layer * 2 + w + 1] > 0.0
                for c in range(3):
                    late_ref[c * 2 + w : c * 2 + w + 1, :] = jnp.where(alive, lane_sums(total, c, w), 0.0)

    for outside, layer in ((x_me == 0, 1), (x_me == NX - 1, 3)):

        @pl.when(outside)
        def _():
            cols = jnp.transpose(rows[...])
            spread(edge, cols, (layer * 2, layer * 2 + 1), range(4))
            for w in range(2):

                def body(n, carry):
                    for u in range(2):
                        at = tile_at(n * 2 + u, w * TILE)
                        spot = [edge[f, at, :] for f in range(4)]
                        for k in range(6):
                            source = (layer - 1) * 2 + k
                            delta = [spot[c] - row(rows, source * 8 + c) for c in range(3)]
                            radial, direct = scalars(delta, spot[3] * row(rows, source * 8 + 3))
                            keep[k, at, :] = radial
                            keep[6 + k, at, :] = direct
                    return carry

                lax.fori_loop(0, (trips[layer * 2 + w] + 1) // 2, body, 0)


def fourth_kernel(
    rows_ref, plane_keep, late_keep, late_ref, out_keep, plane_wide, out_wide, res_ref, got_ref, new_ref, out_ref,
    moved, rows, total, two_ref,
):
    x_me = own_place()[2]
    first = x_me * 2
    for c in range(3):
        got = got_ref[c * 4 : c * 4 + 4, :]
        moved[c, 0:4, :] = got
        moved[c, 4:12, :] = res_ref[c * 8 : c * 8 + 8, :]
        moved[c, 12:16, :] = got
        for w in range(2):
            at = pl.ds(jnp.where(x_me < 2, 4, 10) + w, 1)
            moved[c, at, :] = moved[c, at, :] + late_ref[c * 2 + w : c * 2 + w + 1, :]
    rows[...] = rows_ref[...]
    pol, alone = rows[80:90, :], rows[96:106, :]
    live = rows[pl.ds(7, 10, stride=8), :]
    trips = trips_of(live)
    source = [rows[pl.ds(32 + 4 + c, 2, stride=8), :] for c in range(3)]
    residual = [jnp.concatenate([moved[c, pl.ds(first + k, 1), :] for k in range(10)], axis=0) for c in range(3)]

    def tiles(box, x):
        layer, w = x + box // 2 - 2, box % 2
        inside = 0 <= layer < NX
        spot_ref = plane_wide if inside else out_wide
        base = (layer * 2 + w if inside else w) * TILE

        def scalar(k, part, n):
            if not inside:
                return out_keep[part * 6 + k, tile_at(n, base), :]
            if layer == (0 if x < 2 else NX - 1):
                return late_keep[part * 6 + k, tile_at(n, w * TILE), :]
            return plane_keep[part * 6 + k, tile_at(n, base - 2 * TILE), :]

        def body(n, carry):
            for u in range(2):
                tile = n * 2 + u
                spot = [spot_ref[c, tile_at(tile, base), :] for c in range(3)]
                parts = []
                for k in range(6):
                    near = (box // 2 - 1) * 2 + k
                    delta = [spot[c] - row(rows, near * 8 + c) for c in range(3)]
                    moment = [row(rows, near * 8 + 4 + c) for c in range(3)]
                    parts.append(field_of(delta, scalar(k, 0, tile), scalar(k, 1, tile), moment))
                for c in range(3):
                    total[c, tile_at(tile, (box - 2) * TILE), :] = added([part[c] for part in parts])
            return carry

        lax.fori_loop(0, (trips[box] + 1) // 2, body, 0)

    def sweep(boxes, moments):
        for c in range(3):
            rows[pl.ds(4 + c, 10, stride=8), :] = moments[c]
        for x in range(NX):

            @pl.when(x_me == x)
            def _():
                for box in boxes:
                    tiles(box, x)

        return [jnp.concatenate([lane_sums(total, c, box - 2) for box in boxes], axis=0) for c in range(3)]

    one = [pol * residual[c] for c in range(3)]
    fields = sweep(range(2, 8), one)
    two = []
    edge = jnp.zeros((2, TILE), F32)
    for c in range(3):
        value = pol[2:8] * (residual[c][2:8] + fields[c] + alone[2:8] * one[c][2:8])
        two.append(jnp.concatenate([edge, jnp.where(live[2:8] > 0.0, value, 0.0), edge], axis=0))
        two_ref[c, 0:10, :] = two[c]
    fields = sweep(range(4, 6), two)
    for c in range(3):
        value = pol[4:6] * (residual[c][4:6] + fields[c] + alone[4:6] * two_ref[c, 4:6, :])
        three = source[c] + jnp.where(live[4:6] > 0.0, value, 0.0)
        for w in range(2):
            new_ref[c : c + 1, w * TILE : (w + 1) * TILE] = three[w : w + 1]
            out_ref[c : c + 1, w * TILE : (w + 1) * TILE] = residual[c][4 + w : 5 + w]


VMEM = pl.BlockSpec(memory_space=pltpu.VMEM)
HBM = pl.BlockSpec(memory_space=pltpu.HBM)


def shape_of(shape):
    return shape if isinstance(shape, jax.ShapeDtypeStruct) else jax.ShapeDtypeStruct(shape, F32)


def call(body, ins, outs, scratch, cost, limit, name):
    return pl.pallas_call(
        body,
        in_specs=ins,
        out_specs=[VMEM] * len(outs),
        out_shape=[shape_of(shape) for shape in outs],
        scratch_shapes=[pltpu.VMEM(shape, F32) if isinstance(shape, tuple) else shape for shape in scratch],
        cost_estimate=pl.CostEstimate(flops=cost, bytes_accessed=1 << 20, transcendentals=0),
        compiler_params=pltpu.CompilerParams(vmem_limit_bytes=limit << 20),
        name=name,
    )


def device(group, box):
    return group * OWNERS + box


def rounds():
    plane = [
        [device(2 * y + core, z * NX + x) for y in range(NY) for x in range(NX)]
        for core in range(2)
        for z in range(OWNERS // NX)
    ]
    chip = [[device(2 * y, b), device(2 * y + 1, b)] for y in range(NY) for b in range(OWNERS)]
    up = [[(device(g, b), device(g, b + NX)) for b in range(OWNERS - NX)] for g in range(GROUPS)]
    down = [[(target, source) for source, target in pairs] for pairs in up]
    apart = [pair for g in range(GROUPS) for pair in (down[g] if g % 2 else up[g])]
    near_side = [(s, t) for pairs in up for s, t in pairs if s % NX < 2]
    near_side += [(s, t) for pairs in down for s, t in pairs if s % NX >= 2]
    return plane, chip, apart, near_side


PLANE_SETS, CHIP_SETS, APART, NEAR_SIDE = rounds()
OWN_ROWS = PLANE * 8 + 64
MONO_ROWS = (NTERM + 3) * 8
SIDE_ROWS = 256 + 64


def on_device(
    dipoles, perm_field, positions, polarizability, occupancy, far_boxes, far_class, far_count, far_scale, translations
):
    me = lax.axis_index("d").astype(jnp.int32)
    two = pltpu.SMEM((2,), jnp.int32)
    lists = pltpu.VMEM((2, ILIST), jnp.int32)
    [chunk] = call(
        first_kernel,
        [HBM] * 9,
        [(PLANE, CHUNK, TILE)],
        [(MONO_ROWS, TILE), (2 * CHUNK, TILE)]
        + [(3, 2 * TILE)] * 3
        + [(1, 2 * TILE), (2, ILIST), lists, lists, two, two, pltpu.SemaphoreType.DMA((9,))],
        1 << 20,
        60,
        "first",
    )(
        occupancy, far_count, dipoles, perm_field, positions, polarizability.reshape(1, 2 * TILE),
        far_boxes, far_class, far_scale,
    )
    block = lax.all_to_all(chunk, "d", 0, 0, axis_index_groups=PLANE_SETS, tiled=True)
    half = jax.ShapeDtypeStruct((CLASSES * 256, NTERM), BF16)
    t_high, t_low = call(prepare_kernel, [VMEM], [half, half], [], 1 << 28, 12, "prepare")(
        jnp.transpose(translations, (1, 0, 2))
    )
    mine = (me // (2 * OWNERS)) * NX
    core = (me // OWNERS) & 1
    near = lax.dynamic_slice(block, (mine, 8, 0), (NX, 16, TILE)).reshape(64, TILE)
    part = jnp.concatenate([block[:, 0:8, :].reshape(PLANE * 8, TILE), near], axis=0)
    part, t_high, t_low = lax.optimization_barrier((part, t_high, t_low))
    own = lax.all_gather(part, "d", axis_index_groups=CHIP_SETS, axis=0)
    edges = lax.dynamic_slice(own, (0, PLANE * 8 + 32 * (1 - core), 0), (2, 32, TILE)).reshape(64, TILE)
    away = jnp.concatenate([own[:, 0 : PLANE * 8].reshape(256, TILE), edges], axis=0)
    came = lax.ppermute(away, "d", APART)
    own = own.reshape(2 * OWN_ROWS, TILE)
    half = jax.ShapeDtypeStruct((8 * 176, TILE), BF16)
    sel, near_zero, wide, m_high, m_low, plane_keep = call(
        second_kernel,
        [VMEM],
        [(64, 192), (24, TILE), (4, 8 * TILE, TILE), half, half, (12, 4 * TILE, TILE)],
        [(TILE, TILE), (3, 6 * TILE, TILE), (MONO_ROWS, TILE)],
        1 << 28,
        20,
        "second",
    )(block)
    came, sel = lax.optimization_barrier((came, sel))
    sides = lax.all_gather(came, "d", axis_index_groups=CHIP_SETS, axis=0).reshape(2 * SIDE_ROWS, TILE)
    residual, send = call(
        third_kernel,
        [VMEM] * 10,
        [(24, TILE), (12, TILE)],
        [(256, TILE), (64, TILE), (64, TILE), (24, TILE), (TILE, TILE), (3, 2 * TILE, TILE)],
        1 << 28,
        16,
        "third",
    )(block, own, sides, sel, near_zero, wide, m_high, m_low, t_high, t_low)
    got = lax.ppermute(send, "d", NEAR_SIDE)
    rows, out_keep, out_wide, late_keep, late = call(
        window_kernel,
        [VMEM] * 3,
        [(TILE, TILE), (12, 2 * TILE, TILE), (4, 2 * TILE, TILE), (12, 2 * TILE, TILE), (8, TILE)],
        [(TILE, TILE), (3, 2 * TILE, TILE)],
        1 << 28,
        16,
        "window",
    )(block, sides, wide)
    new, out = call(
        fourth_kernel,
        [VMEM] * 9,
        [(3, 2 * TILE), (3, 2 * TILE)],
        [(3, 16, TILE), (TILE, TILE), (3, 6 * TILE, TILE), (3, 16, TILE)],
        1 << 28,
        20,
        "fourth",
    )(rows, plane_keep, late_keep, late, out_keep, wide, out_wide, residual, got)
    return new, out


def solution(mesh):
    flat = Mesh(mesh.devices.reshape(-1), ("d",))
    return jax.shard_map(
        on_device,
        mesh=flat,
        in_specs=(
            P(None, "d"), P(None, "d"), P(None, "d"), P("d"), P("d"), P("d", None), P("d", None), P("d"), P("d", None), P(),
        ),
        out_specs=(P(None, "d"), P(None, "d")),
        check_vma=False,
    )
```
